128 devices in a mesh: dp: 32 (over x, y, core), seq: 4 (over z).
Axes of the slice: x: 4, y: 4, z: 4, core: 2. Of those that a mesh axis runs over, the one named last changes fastest.
Arguments:
- audio: float32 [32, 655360], P(None, ('dp', 'seq')), may hold values from -0.4 to 0.4
- starts: int32 [32], replicated, may hold values from 0 to 327679, as said below
- lengths: int32 [32], replicated, may hold values from 163840 to 655360, as said below
- slots: int32 [32], replicated, may hold values from 0 to 31, each once
- conv1_weight: bfloat16 [9, 256], replicated, may hold values from -2 to 2
- conv2_weight: bfloat16 [2304, 256], replicated, may hold values from -0.125 to 0.125
- proj_weight: bfloat16 [5120, 1024], P('dp'), may hold values from -0.078125 to 0.078125
- qkv_weight: bfloat16 [1024, 3072], P('dp'), may hold values from -8 to 8
- out_weight: bfloat16 [1024, 1024], P(None, 'dp'), may hold values from -0.1875 to 0.1875
Outputs:
- regrouped: bfloat16 [32, 32, 4, 8, 1024], P('dp', None, 'seq')
- attended: bfloat16 [32, 32, 4, 8, 1024], P('dp', None, 'seq')
The draws below stay inside these ranges and needn't reach their ends.
Inputs may be any that keep to these rules, and one draw needn't show every extreme that they name: starts plus lengths is at most 655360 for every stream; some stream's utterance covers the whole stream, and some other stream's utterance starts at 327679. `lengths`: some stream's utterance has exactly 163840 samples. `slots`: every row number appears once.
All inputs are finite; a program needn't handle non-finite values.
Results may differ from the reference program's by a relative error of at most 0.013.
Values may be sent and summed in bfloat16 or wider, within the bound.
A program may use at most 128 MiB of HBM per device.

```python
import functools
import math
import jax
import jax.numpy as jnp
import numpy as np
from jax import lax

D = 1024
HEADS = 8
HEAD_DIM = 128
MELS = 80
CH = 256
N_FFT = 512
HOP = 160
W = 8
ROWS = 32
BLOCKS = 32
FRAMES = 1024
STREAM = 655360
FEAT = 5120
N_SEQ = 4


def utterance_bounds(key):
    base = jax.random.fold_in(key, 37)
    first_key, second_key, third_key, fourth_key = jax.random.split(base, 4)
    begins = jax.random.randint(first_key, (ROWS,), 0, STREAM // 2)
    spare = STREAM - STREAM // 4 - begins
    extra = jax.random.randint(second_key, (ROWS,), 0, 1 << 30) % (spare + 1)
    spans = STREAM // 4 + extra
    whole = jax.random.randint(third_key, (), 0, ROWS)
    latest = (whole + 1 + jax.random.randint(fourth_key, (), 0, ROWS - 1)) % ROWS
    index = jnp.arange(ROWS)
    begins = jnp.where(index == whole, 0, begins)
    spans = jnp.where(index == whole, STREAM, spans)
    begins = jnp.where(index == latest, STREAM // 2 - 1, begins)
    spans = jnp.where(index == latest, STREAM // 4, spans)
    return (begins.astype(jnp.int32), spans.astype(jnp.int32))


def draw_starts(key, part):
    return utterance_bounds(key)[0]


def draw_lengths(key, part):
    return utterance_bounds(key)[1]


def draw_qkv_weight(key, part):
    base = jax.random.fold_in(key, 101)
    first_key = jax.random.fold_in(base, 0)
    sigma = D ** (-0.5)
    values = jax.random.normal(first_key, (D, 3 * D), jnp.float32) * sigma
    column = jnp.arange(3 * D)
    values = values * jnp.where(column < D, 3.0, 1.0)[None, :]
    return jnp.clip(values, -8.0, 8.0).astype(jnp.bfloat16)


def steps_of(own_key, extent, cuts, least, high):
    loudness, own = 1.0, jax.random.fold_in(own_key, 6)
    for dim, shards_of in cuts:
        draws = jnp.exp(jax.random.uniform(jax.random.fold_in(own, dim), (shards_of,), jnp.float32, least / len(cuts), high / len(cuts)))
        loudness = loudness * jnp.repeat(draws, extent[dim] // shards_of).reshape([-1 if axis == dim else 1 for axis in range(len(extent))])
    return loudness


def bell_draw(rng, dims, scale, most, shards=(), kind=jnp.bfloat16):
    gain = steps_of(rng, dims, shards, -0.22, 0.18) if shards else 1.0
    values = jax.random.normal(rng, dims, jnp.float32) * scale * gain
    return jnp.minimum(jnp.maximum(values, -most), most).astype(kind)


def setup_inputs(seed: int = 0) -> dict:
    arg_keys = jax.random.split(jax.random.key(seed), 10)
    audio = bell_draw(arg_keys[0], (ROWS, STREAM), 0.05, 0.4, ((1, 128),), jnp.float32)
    starts = draw_starts(jax.random.fold_in(arg_keys[9], 71), 0)
    lengths = draw_lengths(jax.random.fold_in(arg_keys[9], 71), 0)
    slots = jax.random.permutation(arg_keys[3], ROWS).astype(jnp.int32)
    conv1_weight = bell_draw(arg_keys[4], (9, CH), 9 ** -0.5, 2.0)
    conv2_weight = bell_draw(arg_keys[5], (9 * CH, CH), (9 * CH) ** -0.5, 0.125)
    proj_weight = bell_draw(arg_keys[6], (FEAT, D), FEAT ** -0.5, 0.078125, ((0, 32),))
    qkv_weight = draw_qkv_weight(jax.random.fold_in(arg_keys[9], 71), 0)
    out_weight = bell_draw(arg_keys[8], (D, D), D ** -0.5, 0.1875, ((1, 32),))
    return dict(audio=audio, starts=starts, lengths=lengths, slots=slots, conv1_weight=conv1_weight, conv2_weight=conv2_weight, proj_weight=proj_weight, qkv_weight=qkv_weight, out_weight=out_weight)


SAMPLE_RATE = 16000.0
EPS_LOG = 1e-06
EPS_NORM = 1e-05
MASKED = -1e+30

def mel_table(size, bands):
    count = size // 2 + 1
    highest = 2595.0 * math.log10(1.0 + SAMPLE_RATE / 1400.0)
    points = np.linspace(0.0, highest, bands + 2)
    edges = 700.0 * (10.0 ** (points / 2595.0) - 1.0)
    edges[0] = 0.0
    edges[-1] = SAMPLE_RATE / 2.0
    frequency = np.arange(count) * (SAMPLE_RATE / size)
    lower = edges[:-2][None, :]
    middle = edges[1:-1][None, :]
    upper = edges[2:][None, :]
    rising = (frequency[:, None] - lower) / (middle - lower)
    falling = (upper - frequency[:, None]) / (upper - middle)
    return np.maximum(0.0, np.minimum(rising, falling)).astype(np.float32)

def first_conv(log_mel, weight):
    padded = jnp.pad(log_mel, ((0, 0), (0, 0), (1, 1)))
    outputs = (log_mel.shape[1] - 1) // 2
    width = log_mel.shape[2]
    tap_list = [padded[:, row_tap:row_tap + 2 * outputs - 1:2, col_tap:col_tap + width - 1:2] for row_tap in range(3) for col_tap in range(3)]
    patches = jnp.stack(tap_list, axis=-1)
    result = jnp.dot(patches.reshape(-1, 9), weight, preferred_element_type=jnp.float32)
    result = jax.nn.relu(result).astype(jnp.bfloat16)
    return result.reshape(log_mel.shape[0], outputs, width // 2, weight.shape[1])

def second_conv(first, weight):
    padded = jnp.pad(first, ((0, 0), (0, 0), (1, 1), (0, 0)))
    outputs = (first.shape[1] - 1) // 2
    width = first.shape[2]
    tap_list = [padded[:, row_tap:row_tap + 2 * outputs - 1:2, col_tap:col_tap + width - 1:2, :] for row_tap in range(3) for col_tap in range(3)]
    patches = jnp.concatenate(tap_list, axis=-1)
    result = jnp.dot(patches.reshape(-1, patches.shape[-1]), weight, preferred_element_type=jnp.float32)
    result = jax.nn.relu(result).astype(jnp.bfloat16)
    return result.reshape(first.shape[0] * outputs, width // 2 * weight.shape[1])

def front_stream(audio_row, conv1_weight, conv2_weight, proj_weight):
    rim_width = N_FFT + 2 * HOP
    frame_count = 4 * FRAMES + 3
    needed = (frame_count + 3) * HOP
    extended = jnp.concatenate([jnp.zeros((rim_width,), jnp.float32), audio_row, jnp.zeros((needed - rim_width - STREAM,), jnp.float32)])
    hop_rows = extended.reshape(frame_count + 3, HOP)
    frames = jnp.concatenate([hop_rows[offset:offset + frame_count] for offset in range(4)], axis=1)[:, :N_FFT]
    position = jnp.arange(N_FFT).astype(jnp.float32)
    window = 0.5 - 0.5 * jnp.cos(position * (2.0 * math.pi / N_FFT))
    spectrum = jnp.fft.rfft(frames * window[None, :], axis=1)
    power = (jnp.real(spectrum) ** 2 + jnp.imag(spectrum) ** 2).astype(jnp.float32)
    mel_power = jnp.dot(power, jnp.asarray(mel_table(N_FFT, MELS)), precision=lax.Precision.HIGHEST)
    log_mel = jnp.log(mel_power + EPS_LOG).astype(jnp.bfloat16)
    first = first_conv(log_mel[None], conv1_weight)
    features = second_conv(first, conv2_weight)
    return jnp.dot(features, proj_weight, preferred_element_type=jnp.float32).astype(jnp.bfloat16)

def attend_row(frames_x, valid, qkv_weight, out_weight):
    values = frames_x.astype(jnp.float32)
    mean = lax.optimization_barrier(jnp.mean(values, axis=1, keepdims=True))
    centered = values - mean
    variance = lax.optimization_barrier(jnp.mean(centered * centered, axis=1, keepdims=True))
    normed = (centered * lax.rsqrt(variance + EPS_NORM)).astype(jnp.bfloat16)
    mixed = jnp.dot(normed, qkv_weight, preferred_element_type=jnp.float32).astype(jnp.bfloat16)
    queries = mixed[:, :D].reshape(FRAMES, HEADS, HEAD_DIM).transpose(1, 0, 2)
    keys = mixed[:, D:2 * D].reshape(FRAMES, HEADS, HEAD_DIM).transpose(1, 0, 2)
    value_heads = mixed[:, 2 * D:].reshape(FRAMES, HEADS, HEAD_DIM).transpose(1, 0, 2)
    scale = HEAD_DIM ** (-0.5)

    def one_head(triple):
        query, key, value = triple
        scores = jnp.dot(query, key.T, preferred_element_type=jnp.float32) * scale
        masked = jnp.where(valid[None, :], scores, MASKED)
        peak = lax.optimization_barrier(jnp.max(masked, axis=1, keepdims=True))
        weights = jnp.where(valid[None, :], jnp.exp(masked - peak), 0.0)
        total = lax.optimization_barrier(jnp.sum(weights, axis=1, keepdims=True))
        summed = jnp.dot(weights.astype(jnp.bfloat16), value, preferred_element_type=jnp.float32)
        return (summed / total).astype(jnp.bfloat16)
    context = lax.map(one_head, (queries, keys, value_heads))
    context = context.transpose(1, 0, 2).reshape(FRAMES, D)
    output = jnp.dot(context, out_weight, preferred_element_type=jnp.float32)
    attended = jnp.where(valid[:, None], output, 0.0).astype(jnp.bfloat16)
    regrouped = jnp.where(valid[:, None], frames_x, jnp.zeros_like(frames_x))
    return (regrouped, attended)

def reference(audio, starts, lengths, slots, conv1_weight, conv2_weight, proj_weight, qkv_weight, out_weight):
    encode = functools.partial(front_stream, conv1_weight=conv1_weight, conv2_weight=conv2_weight, proj_weight=proj_weight)
    encoded = lax.map(encode, audio)
    row_index = jnp.arange(ROWS, dtype=jnp.int32)
    table = slots[None, :] == row_index[:, None]
    source = lax.optimization_barrier(jnp.sum(jnp.where(table, row_index[None, :], 0), axis=1)).astype(jnp.int32)
    ordered = jnp.take(encoded, source, axis=0)
    begins = jnp.take(starts, source)
    spans = jnp.take(lengths, source)
    position = jnp.arange(FRAMES, dtype=jnp.int32) * (4 * HOP)
    valid = (position[None, :] >= begins[:, None]) & (position[None, :] < (begins + spans)[:, None])

    def one_row(pair):
        return attend_row(pair[0], pair[1], qkv_weight, out_weight)
    regrouped, attended = lax.map(one_row, (ordered, valid))
    regrouped = regrouped.reshape(ROWS, BLOCKS, N_SEQ, W, D)
    attended = attended.reshape(ROWS, BLOCKS, N_SEQ, W, D)
    return (regrouped, attended)
```

```python
import functools
import math

import jax
import jax.numpy as jnp
import numpy as np
from jax import lax
from jax.experimental import pallas as pl
from jax.experimental.pallas import tpu as pltpu
from jax.sharding import PartitionSpec as P

D = 1024
HEADS = 8
HEAD_DIM = 128
MELS = 80
N_FFT = 512
HOP = 160
W = 8
CH = 256
ROWS = 32
RIM = 896
SPAN = 5120
EXT = 6272
BF = jnp.bfloat16
F32 = jnp.float32

SAMPLE_RATE = 16000.0
EPS_LOG = 1e-06
EPS_NORM = 1e-05
MASKED = -1e30
VMEM_LIMIT = 62 * 1024 * 1024


def mel_table(size, bands):
    count = size // 2 + 1
    highest = 2595.0 * math.log10(1.0 + SAMPLE_RATE / 1400.0)
    points = np.linspace(0.0, highest, bands + 2)
    edges = 700.0 * (10.0 ** (points / 2595.0) - 1.0)
    edges[0] = 0.0
    edges[-1] = SAMPLE_RATE / 2.0
    frequency = np.arange(count) * (SAMPLE_RATE / size)
    lower = edges[:-2][None, :]
    middle = edges[1:-1][None, :]
    upper = edges[2:][None, :]
    rising = (frequency[:, None] - lower) / (middle - lower)
    falling = (upper - frequency[:, None]) / (upper - middle)
    return np.maximum(0.0, np.minimum(rising, falling)).astype(np.float32)


def split_high_low(table):
    high = np.asarray(table, np.float64).astype(BF)
    low = (np.asarray(table, np.float64) - high.astype(np.float64)).astype(BF)
    return high, low


def spectrum_tables():
    sample = np.arange(N_FFT)
    angle = (sample[:, None] * np.arange(N_FFT // 2)[None, :] % N_FFT) * (2.0 * math.pi / N_FFT)
    window = 0.5 - 0.5 * np.cos(sample * (2.0 * math.pi / N_FFT))
    return split_high_low(np.concatenate([np.cos(angle), np.sin(angle)], axis=1) * window[:, None])


def filter_tables():
    padded = np.zeros((N_FFT // 2, 128), np.float64)
    padded[:, :MELS] = mel_table(N_FFT, MELS)[: N_FFT // 2]
    return split_high_low(padded)


def patch_table():
    table = np.zeros((3 * 128, 40 * 16), np.float32)
    for g in range(40):
        for a in range(3):
            for b in range(3):
                band = 2 * g - 1 + b
                if 0 <= band < MELS:
                    table[a * 128 + band, g * 16 + 3 * a + b] = 1.0
    return table.astype(BF)


def mm(a, b):
    return jnp.dot(a, b, preferred_element_type=F32)


def halves(value):
    high = value.astype(BF)
    return high, (value - high.astype(F32)).astype(BF)


def frame_step(p, ext, frames_high, frames_low):
    window = ext[:, pl.ds(pl.multiple_of(p * 640, 128), 1152)]
    rows = pl.ds(pl.multiple_of(p * 32, 32), 32)
    for q in range(4):
        start = 64 + HOP * q
        base, offset = start // 128 * 128, start % 128
        if offset:
            piece = pltpu.roll(window[:, base : base + 640], 640 - offset, 1)[:, :N_FFT]
        else:
            piece = window[:, base : base + N_FFT]
        high, low = halves(piece)
        frames_high[q, rows, :] = high
        frames_low[q, rows, :] = low


def mel_step(q, frames_high, frames_low, dft_high, dft_low, mel_high, mel_low, log_mel):
    high, low = frames_high[q], frames_low[q]
    spectrum = mm(high, dft_high[...]) + mm(high, dft_low[...]) + mm(low, dft_high[...])
    half = N_FFT // 2
    power = spectrum[:, :half] * spectrum[:, :half] + spectrum[:, half:] * spectrum[:, half:]
    high, low = halves(power)
    mel = mm(high, mel_high[...]) + mm(high, mel_low[...]) + mm(low, mel_high[...])
    log_mel[q] = jnp.log(mel + EPS_LOG).astype(BF)


def make_patches(log_mel, patch_map, patches):
    even = jnp.concatenate([log_mel[0], log_mel[1], log_mel[2]], axis=1)
    patches[:288, :] = mm(even, patch_map[...]).astype(BF)
    odd = jnp.concatenate([log_mel[2, :256], log_mel[3, :256], log_mel[0, 32:]], axis=1)
    patches[288:, :] = mm(odd, patch_map[...]).astype(BF)


def spread_taps(conv1, taps):
    taps[...] = jnp.zeros_like(taps)
    for j in range(8):
        taps[j, 16 * j : 16 * j + 16, :] = conv1[...]


def conv1_step(g, patches, taps, first):
    block, j = g // 8, g % 8
    lanes = pl.ds(pl.multiple_of(block * 128, 128), 128)
    result = mm(patches[:, lanes], taps[j])
    first[:, pl.ds(pl.multiple_of(g * CH + CH, CH), CH)] = jnp.maximum(result, 0.0).astype(BF)


def conv2_step(h, first, conv2, features):
    lanes = pl.ds(pl.multiple_of(h * 512, 512), 768)
    total = mm(first[0:256, lanes], conv2[0:768, :])
    total += mm(first[288:544, lanes], conv2[768:1536, :])
    total += mm(first[32:288, lanes], conv2[1536:2304, :])
    features[:, pl.ds(pl.multiple_of(h * CH, CH), CH)] = jnp.maximum(total, 0.0).astype(BF)


def to_rows(projected, slots_wide):
    out_index = lax.broadcasted_iota(jnp.int32, (256, 256), 0)
    in_index = lax.broadcasted_iota(jnp.int32, (256, 256), 1)
    same_row = slots_wide == out_index // 8
    same_frame = in_index // 32 == out_index % 8
    routing = jnp.where(same_row & same_frame, 1.0, 0.0).astype(BF)
    return mm(routing, projected).astype(BF)


def front_kernel(
    audio, rim, slots_wide, dft_high, dft_low, mel_high, mel_low, patch_map, conv1, conv2, proj,
    out, ext, frames_high, frames_low, log_mel, patches, taps, first, features,
):
    ext[:, :RIM] = rim[...]
    ext[:, RIM : RIM + SPAN] = audio[...]
    ext[:, RIM + SPAN :] = jnp.zeros((ROWS, EXT - RIM - SPAN), F32)
    spread_taps(conv1, taps)
    first[:, :CH] = jnp.zeros((544, CH), BF)

    @pl.loop(0, 9)
    def _(p):
        frame_step(p, ext, frames_high, frames_low)

    @pl.loop(0, 4)
    def _(q):
        mel_step(q, frames_high, frames_low, dft_high, dft_low, mel_high, mel_low, log_mel)

    make_patches(log_mel, patch_map, patches)

    @pl.loop(0, 40)
    def _(g):
        conv1_step(g, patches, taps, first)

    @pl.loop(0, 20)
    def _(h):
        conv2_step(h, first, conv2, features)

    projected = mm(features[...], proj[...]).astype(BF)
    out[...] = to_rows(projected, slots_wide[...])


def front(audio, rim, slots, conv1_weight, conv2_weight, proj):
    dft_high, dft_low = spectrum_tables()
    mel_high, mel_low = filter_tables()
    args = (
        audio, rim, jnp.tile(slots, 8).reshape(1, 256), dft_high, dft_low, mel_high, mel_low,
        patch_table(), jnp.pad(conv1_weight, ((0, 7), (0, 0))), conv2_weight, proj,
    )
    return pl.pallas_call(
        front_kernel,
        out_shape=jax.ShapeDtypeStruct((256, D), BF),
        in_specs=[pl.BlockSpec(memory_space=pltpu.VMEM)] * len(args),
        out_specs=pl.BlockSpec(memory_space=pltpu.VMEM),
        scratch_shapes=[
            pltpu.VMEM((ROWS, EXT), F32),
            pltpu.VMEM((4, 288, N_FFT), BF),
            pltpu.VMEM((4, 288, N_FFT), BF),
            pltpu.VMEM((4, 288, 128), BF),
            pltpu.VMEM((544, 640), BF),
            pltpu.VMEM((8, 128, CH), BF),
            pltpu.VMEM((544, 41 * CH), BF),
            pltpu.VMEM((256, 20 * CH), BF),
        ],
        compiler_params=pltpu.CompilerParams(vmem_limit_bytes=VMEM_LIMIT),
        name="front",
    )(*args)


def passed_along(block, axis, distance):
    devices = range(lax.axis_size(axis))
    route = [(i - distance, i) for i in devices if i - distance in devices]
    return lax.ppermute(block, axis, route)


def layer_norm(rows):
    values = rows.astype(F32)
    mean = jnp.mean(values, axis=-1, keepdims=True)
    centered = values - mean
    variance = jnp.mean(centered * centered, axis=-1, keepdims=True)
    return (centered * lax.rsqrt(variance + EPS_NORM)).astype(BF)


def frame_mask(begin, span, owners, group, blocks):
    block = jnp.arange(blocks, dtype=jnp.int32)
    offset = jnp.arange(W, dtype=jnp.int32)
    frame = (block[None, :, None] * group + owners[:, None, None]) * W + offset[None, None, :]
    sample = frame * (4 * HOP)
    return ((sample >= begin) & (sample < begin + span)).reshape(-1)


def on_device(
    audio, starts, lengths, slots, conv1_weight, conv2_weight, proj_weight, qkv_weight, out_weight
):
    streams = audio.shape[0]
    rim = passed_along(audio[:, SPAN - RIM :], ("dp", "seq"), 1)
    proj = lax.all_gather(proj_weight, "dp", axis=0, tiled=True)
    ordered = front(audio, rim, slots, conv1_weight, conv2_weight, proj).reshape(streams, W, D)
    received = lax.all_to_all(ordered, "dp", split_axis=0, concat_axis=0, tiled=True)
    rows_here = received.reshape(streams * W, D)
    local_count = rows_here.shape[0]
    mine = lax.axis_index("dp")
    group = lax.axis_size("seq")
    owner = lax.axis_index("seq")
    chosen = slots == mine
    begin = jnp.sum(jnp.where(chosen, starts, 0))
    span = jnp.sum(jnp.where(chosen, lengths, 0))
    valid = frame_mask(begin, span, jnp.reshape(owner, (1,)), group, streams)
    normed = layer_norm(rows_here)
    scale = HEAD_DIM ** (-0.5)
    weights_mix, weights_out = (
        lax.all_gather(qkv_weight, "dp", axis=0, tiled=True),
        lax.all_gather(out_weight, "dp", axis=1, tiled=True),
    )
    mixed = jnp.dot(normed, weights_mix, preferred_element_type=F32).astype(BF)
    queries = mixed[:, :D].reshape(local_count, HEADS, HEAD_DIM)
    key_piece = lax.all_gather(mixed[:, D:].reshape(1, local_count, 2 * D), "seq", axis=0, tiled=True)
    number = key_piece.shape[0]
    key_rows = key_piece[:, :, :D].reshape(number * local_count, HEADS, HEAD_DIM)
    value_rows = key_piece[:, :, D:].reshape(number * local_count, HEADS, HEAD_DIM)
    owners = jnp.arange(number, dtype=jnp.int32)
    key_valid = frame_mask(begin, span, owners, group, streams)
    scores = jnp.einsum("qhd,khd->hqk", queries, key_rows, preferred_element_type=F32) * scale
    masked = jnp.where(key_valid[None, None, :], scores, MASKED)
    peak = jnp.max(masked, axis=2)
    weights = jnp.where(key_valid[None, None, :], jnp.exp(masked - peak[:, :, None]), 0.0)
    total = jnp.sum(weights, axis=2)
    update = jnp.einsum("hqk,khd->hqd", weights.astype(BF), value_rows, preferred_element_type=F32)
    context = (update / total[:, :, None]).transpose(1, 0, 2).reshape(local_count, D).astype(BF)
    output = jnp.dot(context, weights_out, preferred_element_type=F32)
    regrouped = jnp.where(valid[:, None], rows_here, jnp.zeros_like(rows_here))
    attended = jnp.where(valid[:, None], output, 0.0).astype(BF)
    return regrouped.reshape(1, streams, 1, W, D), attended.reshape(1, streams, 1, W, D)


def solution(mesh):
    in_specs = (
        P(None, ("dp", "seq")), P(), P(), P(), P(), P(), P("dp", None), P("dp", None), P(None, "dp"),
    )
    out_specs = (P("dp", None, "seq", None, None), P("dp", None, "seq", None, None))
    return jax.shard_map(
        on_device, mesh=mesh, in_specs=in_specs, out_specs=out_specs, check_vma=False
    )
```

```python
import functools
import math

import jax
import jax.numpy as jnp
import numpy as np
from jax import lax
from jax.experimental import pallas as pl
from jax.experimental.pallas import tpu as pltpu
from jax.sharding import PartitionSpec as P

D = 1024
HEADS = 8
HEAD_DIM = 128
MELS = 80
N_FFT = 512
HOP = 160
W = 8
CH = 256
ROWS = 32
RIM = 896
SPAN = 5120
EXT = 6272
BF = jnp.bfloat16
F32 = jnp.float32

SAMPLE_RATE = 16000.0
EPS_LOG = 1e-06
EPS_NORM = 1e-05
MASKED = -1e30
VMEM_LIMIT = 62 * 1024 * 1024


def mel_table(size, bands):
    count = size // 2 + 1
    highest = 2595.0 * math.log10(1.0 + SAMPLE_RATE / 1400.0)
    points = np.linspace(0.0, highest, bands + 2)
    edges = 700.0 * (10.0 ** (points / 2595.0) - 1.0)
    edges[0] = 0.0
    edges[-1] = SAMPLE_RATE / 2.0
    frequency = np.arange(count) * (SAMPLE_RATE / size)
    lower = edges[:-2][None, :]
    middle = edges[1:-1][None, :]
    upper = edges[2:][None, :]
    rising = (frequency[:, None] - lower) / (middle - lower)
    falling = (upper - frequency[:, None]) / (upper - middle)
    return np.maximum(0.0, np.minimum(rising, falling)).astype(np.float32)


def split_high_low(table):
    high = np.asarray(table, np.float64).astype(BF)
    low = (np.asarray(table, np.float64) - high.astype(np.float64)).astype(BF)
    return high, low


def spectrum_tables():
    sample = np.arange(N_FFT)
    angle = (sample[:, None] * np.arange(N_FFT // 2)[None, :] % N_FFT) * (2.0 * math.pi / N_FFT)
    window = 0.5 - 0.5 * np.cos(sample * (2.0 * math.pi / N_FFT))
    return split_high_low(np.concatenate([np.cos(angle), np.sin(angle)], axis=1) * window[:, None])


def filter_tables():
    padded = np.zeros((N_FFT // 2, 128), np.float64)
    padded[:, :MELS] = mel_table(N_FFT, MELS)[: N_FFT // 2]
    return split_high_low(padded)


def patch_table():
    table = np.zeros((3 * 128, 40 * 16), np.float32)
    for g in range(40):
        for a in range(3):
            for b in range(3):
                band = 2 * g - 1 + b
                if 0 <= band < MELS:
                    table[a * 128 + band, g * 16 + 3 * a + b] = 1.0
    return table.astype(BF)


def mm(a, b):
    return jnp.dot(a, b, preferred_element_type=F32)


def halves(value):
    high = value.astype(BF)
    return high, (value - high.astype(F32)).astype(BF)


def frame_step(p, ext, frames_high, frames_low):
    window = ext[:, pl.ds(pl.multiple_of(p * 640, 128), 1152)]
    rows = pl.ds(pl.multiple_of(p * 32, 32), 32)
    for q in range(4):
        start = 64 + HOP * q
        base, offset = start // 128 * 128, start % 128
        if offset:
            piece = pltpu.roll(window[:, base : base + 640], 640 - offset, 1)[:, :N_FFT]
        else:
            piece = window[:, base : base + N_FFT]
        high, low = halves(piece)
        frames_high[q, rows, :] = high
        frames_low[q, rows, :] = low


def mel_step(q, frames_high, frames_low, dft_high, dft_low, mel_high, mel_low, log_mel):
    high, low = frames_high[q], frames_low[q]
    spectrum = mm(high, dft_high[...]) + mm(high, dft_low[...]) + mm(low, dft_high[...])
    half = N_FFT // 2
    power = spectrum[:, :half] * spectrum[:, :half] + spectrum[:, half:] * spectrum[:, half:]
    high, low = halves(power)
    mel = mm(high, mel_high[...]) + mm(high, mel_low[...]) + mm(low, mel_high[...])
    log_mel[q] = jnp.log(mel + EPS_LOG).astype(BF)


def make_patches(log_mel, patch_map, patches):
    even = jnp.concatenate([log_mel[0], log_mel[1], log_mel[2]], axis=1)
    patches[:288, :] = mm(even, patch_map[...]).astype(BF)
    odd = jnp.concatenate([log_mel[2, :256], log_mel[3, :256], log_mel[0, 32:]], axis=1)
    patches[288:, :] = mm(odd, patch_map[...]).astype(BF)


def spread_taps(conv1, taps):
    taps[...] = jnp.zeros_like(taps)
    for j in range(8):
        taps[j, 16 * j : 16 * j + 16, :] = conv1[...]


def conv1_step(g, patches, taps, first):
    block, j = g // 8, g % 8
    lanes = pl.ds(pl.multiple_of(block * 128, 128), 128)
    result = mm(patches[:, lanes], taps[j])
    first[:, pl.ds(pl.multiple_of(g * CH + CH, CH), CH)] = jnp.maximum(result, 0.0).astype(BF)


def conv2_step(h, first, conv2, features):
    lanes = pl.ds(pl.multiple_of(h * 512, 512), 768)
    total = mm(first[0:256, lanes], conv2[0:768, :])
    total += mm(first[288:544, lanes], conv2[768:1536, :])
    total += mm(first[32:288, lanes], conv2[1536:2304, :])
    features[:, pl.ds(pl.multiple_of(h * CH, CH), CH)] = jnp.maximum(total, 0.0).astype(BF)


def to_rows(projected, slots_wide):
    out_index = lax.broadcasted_iota(jnp.int32, (256, 256), 0)
    in_index = lax.broadcasted_iota(jnp.int32, (256, 256), 1)
    same_row = slots_wide == out_index // 8
    same_frame = in_index // 32 == out_index % 8
    routing = jnp.where(same_row & same_frame, 1.0, 0.0).astype(BF)
    return mm(routing, projected).astype(BF)

MESH_ID = pl.DeviceIdType.MESH
PART = 2 * HEAD_DIM
WIDE = 3 * PART + D


class Ring:
    def __init__(self, source, buffer, send, recv, place):
        self.source, self.buffer, self.send, self.recv = source, buffer, send, recv
        self.core, self.a, self.b, self.sa, self.sb, self.sibling = place
        self.count = 0
        self.sent = []
        self.rows = buffer.shape[1]

    def shard(self, da, db):
        return lax.rem(self.a + da + 4, 4) * self.sa + lax.rem(self.b + db + 4, 4) * self.sb + self.core

    def part(self, index, half):
        if half is None:
            return self.buffer.at[index]
        step = self.rows // 2
        return self.buffer.at[index, pl.ds(half * step, step)]

    def put(self, index, half, target, slot, own=False):
        copy = pltpu.make_async_remote_copy(
            src_ref=self.source if own else self.part(index, half),
            dst_ref=self.part(index, half),
            send_sem=self.send.at[self.count],
            recv_sem=self.recv.at[slot],
            device_id={"dp": target},
            device_id_type=MESH_ID,
        )
        copy.start()
        self.count += 1
        self.sent.append(copy)

    def got(self, index, half, slot):
        pltpu.make_async_remote_copy(
            src_ref=self.part(index, half),
            dst_ref=self.part(index, half),
            send_sem=self.send.at[0],
            recv_sem=self.recv.at[slot],
            device_id={"dp": self.sibling},
            device_id_type=MESH_ID,
        ).wait_recv()

    def to_b(self, da, own=False):
        index = self.shard(da, 0)
        base = 4 + 4 * (da + 1)
        self.put(index, None, self.shard(0, 1), base, own)
        self.put(index, None, self.shard(0, -1), base + 1, own)
        self.put(index, None, self.sibling, 20 + 4 * (da + 1) + 1, own)

    def begin(self):
        index = self.shard(0, 0)
        self.put(index, None, self.shard(1, 0), 0, True)
        self.put(index, None, self.shard(-1, 0), 1, True)
        self.to_b(0, True)

    def pass_a(self):
        for da, half, slot in ((-1, 0, 0), (1, 1, 1)):
            index = self.shard(da, 0)
            self.got(index, None, slot)
            self.put(index, half, self.shard(-da, 0), 2 + slot)
            self.to_b(da)

    def end_a(self):
        index = self.shard(2, 0)
        self.got(index, 0, 2)
        self.got(index, 1, 3)
        self.to_b(2)

    def pass_b(self, da):
        base = 4 + 4 * (da + 1)
        for db, half, slot in ((-1, 0, 0), (1, 1, 1)):
            index = self.shard(da, db)
            self.got(index, None, base + slot)
            self.put(index, half, self.shard(0, -db), base + 2 + slot)
            self.put(index, None, self.sibling, 20 + 4 * (da + 1) + db + 1)

    def end_b(self, da):
        base = 4 + 4 * (da + 1)
        index = self.shard(da, 2)
        self.got(index, 0, base + 2)
        self.got(index, 1, base + 3)
        self.put(index, None, self.sibling, 20 + 4 * (da + 1) + 3)

    def from_sibling(self):
        for slot in range(16):
            self.got(self.sibling, None, 20 + slot)

    def drain(self):
        for copy in self.sent:
            copy.wait_send()


def normalised(values):
    mean = jnp.mean(values, axis=-1, keepdims=True)
    centered = values - mean
    variance = jnp.mean(centered * centered, axis=-1, keepdims=True)
    return (centered * lax.rsqrt(variance + EPS_NORM)).astype(BF)


def nt(a, b):
    return lax.dot_general(a, b, (((1,), (1,)), ((), ())), preferred_element_type=F32)


def whole_kernel(
    audio_in, starts, lengths, slots, conv1_in, conv2_in, proj_in, qkv_in, out_in,
    dft_high_in, dft_low_in, mel_high_in, mel_low_in, patch_in,
    regrouped, attended,
    ext, frames_high, frames_low, log_mel, patches, taps, first, features,
    conv2, dft_high, dft_low, mel_high, mel_low, patch_map,
    proj, wide, rows_out, rows_all, mixed, context_out, context_in,
    local_sem, halo_sem, proj_send, proj_recv, wide_send, wide_recv,
    row_send, row_recv, z_send, z_recv, context_send, context_recv,
):
    me, z = lax.axis_index("dp"), lax.axis_index("seq")
    x, y, core = me // 8, me // 2 % 4, me % 2
    sibling = me + 1 - 2 * core
    a, b = x * (1 - core) + y * core, y * (1 - core) + x * core
    sa, sb = 8 * (1 - core) + 2 * core, 2 * (1 - core) + 8 * core
    place = (core, a, b, sa, sb, sibling)
    line = me * 4 + z
    after, before = lax.rem(line + 1, 128), lax.rem(line + 127, 128)
    up, down = lax.rem(z + 1, 4), lax.rem(z + 3, 4)

    def local(source, target, index):
        copy = pltpu.make_async_copy(source, target, local_sem.at[index])
        copy.start()
        return copy

    loads = [
        local(source, target, index)
        for index, (source, target) in enumerate(
            (
                (audio_in, ext.at[:, pl.ds(RIM, SPAN)]),
                (dft_high_in, dft_high),
                (dft_low_in, dft_low),
                (mel_high_in, mel_high),
                (mel_low_in, mel_low),
                (patch_in, patch_map),
                (conv2_in, conv2),
                (proj_in, proj.at[me]),
            )
        )
    ]
    parts = [
        local(
            qkv_in.at[:, pl.ds(pl.multiple_of(third * D + z * PART, 128), PART)],
            wide.at[me, :, pl.ds(third * PART, PART)],
            8 + third,
        )
        for third in range(3)
    ]

    barrier = pltpu.get_barrier_semaphore()

    @pl.loop(1, 32)
    def _(offset):
        pl.semaphore_signal(
            barrier, inc=1, device_id={"dp": lax.rem(me + offset, 32)}, device_id_type=MESH_ID
        )

    for offset in range(1, 4):
        pl.semaphore_signal(
            barrier, inc=1, device_id={"seq": lax.rem(z + offset, 4)}, device_id_type=MESH_ID
        )
    for other in (after, before):
        pl.semaphore_signal(
            barrier, inc=1, device_id={"dp": other // 4, "seq": other % 4}, device_id_type=MESH_ID
        )
    spread_taps(conv1_in, taps)
    first[:, :CH] = jnp.zeros((544, CH), BF)
    ext[:, RIM + SPAN :] = jnp.zeros((ROWS, EXT - RIM - SPAN), F32)
    turn = jnp.where(
        lax.broadcasted_iota(jnp.int32, (32, 32), 0) == lax.broadcasted_iota(jnp.int32, (32, 32), 1), 1.0, 0.0
    ).astype(BF)
    wide[me, :, 3 * PART :] = nt(turn, out_in[...]).astype(BF)
    pl.semaphore_wait(barrier, 36)

    halo = pltpu.make_async_remote_copy(
        src_ref=audio_in.at[:, pl.ds(SPAN - RIM, RIM)],
        dst_ref=ext.at[:, pl.ds(0, RIM)],
        send_sem=halo_sem.at[0],
        recv_sem=halo_sem.at[1],
        device_id={"dp": after // 4, "seq": after % 4},
        device_id_type=MESH_ID,
    )
    halo.start()
    ring = Ring(proj_in, proj, proj_send, proj_recv, place)
    ring.begin()

    loads[0].wait()
    halo.wait_recv()

    @pl.when(line == 0)
    def _():
        ext[:, :RIM] = jnp.zeros((ROWS, RIM), F32)

    @pl.loop(0, 9)
    def _(p):
        frame_step(p, ext, frames_high, frames_low)

    for load in loads[1:5]:
        load.wait()

    @pl.loop(0, 4)
    def _(q):
        mel_step(q, frames_high, frames_low, dft_high, dft_low, mel_high, mel_low, log_mel)

    loads[5].wait()
    make_patches(log_mel, patch_map, patches)

    def conv1_run(low, high):
        @pl.loop(low, high)
        def _(g):
            conv1_step(g, patches, taps, first)

    def conv2_run(low, high):
        @pl.loop(low, high)
        def _(h):
            conv2_step(h, first, conv2, features)

    conv1_run(0, 8)
    ring.pass_a()
    conv1_run(8, 16)
    ring.pass_b(0)
    conv1_run(16, 32)
    ring.end_a()
    conv1_run(32, 40)
    loads[6].wait()
    conv2_run(0, 4)
    ring.pass_b(-1)
    conv2_run(4, 8)
    ring.end_b(0)
    ring.pass_b(1)
    conv2_run(8, 12)
    conv2_run(12, 16)
    ring.pass_b(2)
    ring.end_b(-1)
    conv2_run(16, 20)
    ring.end_b(1)
    ring.end_b(2)
    ring.from_sibling()
    loads[7].wait()

    projected = mm(features[...], proj[...].reshape(20 * CH, D)).astype(BF)
    tile_map = jnp.where(
        lax.broadcasted_iota(jnp.int32, (32, 256), 1) % 32 == lax.broadcasted_iota(jnp.int32, (32, 256), 0),
        1.0, 0.0,
    ).astype(BF)
    slot_values = jnp.broadcast_to(slots[...].astype(F32), (8, 32)).astype(BF)
    slots_wide = mm(slot_values, tile_map)[0:1, :].astype(jnp.int32)
    out_index = lax.broadcasted_iota(jnp.int32, (256, 256), 0)
    in_index = lax.broadcasted_iota(jnp.int32, (256, 256), 1)
    routing = jnp.where((slots_wide == out_index // 8) & (in_index // 32 == out_index % 8), 1.0, 0.0).astype(BF)
    rows_out[...] = mm(routing, projected).reshape(32, 8, D).astype(BF)

    def row_copy(offset):
        target = lax.rem(me + offset, 32)
        return pltpu.make_async_remote_copy(
            src_ref=rows_out.at[target],
            dst_ref=rows_all.at[z, me],
            send_sem=row_send.at[offset],
            recv_sem=row_recv.at[me],
            device_id={"dp": target},
            device_id_type=MESH_ID,
        )

    @pl.loop(1, 32)
    def _(offset):
        row_copy(offset).start()

    mine = local(rows_out.at[me], rows_all.at[z, me], 11)
    for part in parts:
        part.wait()
    wide_ring = Ring(wide.at[me], wide, wide_send, wide_recv, place)
    wide_ring.begin()
    mine.wait()

    def z_copy(origin, chunk, upwards, index):
        block = rows_all.at[origin, pl.ds(pl.multiple_of(chunk * 8, 8), 8)]
        return pltpu.make_async_remote_copy(
            src_ref=block,
            dst_ref=block,
            send_sem=z_send.at[index],
            recv_sem=z_recv.at[index],
            device_id={"seq": up if upwards else down},
            device_id_type=MESH_ID,
        )

    z_copies = []
    chunks = [lax.rem(x + index, 4) for index in range(4)]
    for index in range(4):
        @pl.loop(0, 8)
        def _(step):
            source = chunks[index] * 8 + step

            @pl.when(source != me)
            def _():
                block = rows_all.at[z, source]
                pltpu.make_async_remote_copy(
                    src_ref=block,
                    dst_ref=block,
                    send_sem=row_send.at[0],
                    recv_sem=row_recv.at[source],
                    device_id={"dp": sibling},
                    device_id_type=MESH_ID,
                ).wait_recv()

        for direction in range(2):
            copy = z_copy(z, chunks[index], direction == 0, 6 * direction + index)
            copy.start()
            z_copies.append(copy)

    def z_wait(origin, chunk, index):
        z_copy(origin, chunk, True, index).wait_recv()

    def z_forward(index):
        z_wait(down, chunks[index], index)
        z_wait(up, chunks[index], 6 + index)
        if index < 2:
            copy = z_copy(down, chunks[index], True, 4 + index)
        else:
            copy = z_copy(up, chunks[index], False, 6 + 2 + index)
        copy.start()
        z_copies.append(copy)

    wide_ring.pass_a()
    z_forward(0)
    wide_ring.pass_b(0)
    wide_ring.end_a()
    z_forward(1)
    wide_ring.end_b(0)
    wide_ring.pass_b(-1)
    wide_ring.pass_b(1)
    z_forward(2)
    wide_ring.pass_b(2)
    wide_ring.end_b(-1)
    wide_ring.end_b(1)
    wide_ring.end_b(2)
    z_forward(3)
    wide_ring.from_sibling()

    def mix(origin):
        values = rows_all[origin].astype(F32).reshape(256, D)
        result = mm(normalised(values), wide[:, :, : 3 * PART].reshape(D, 3 * PART))
        mixed[pl.ds(pl.multiple_of(origin * 256, 256), 256), :] = result.astype(BF)

    mix(z)
    mix(down)
    mix(up)
    opposite = lax.rem(z + 2, 4)
    for index in range(2):
        z_wait(opposite, chunks[index], 4 + index)
        z_wait(opposite, chunks[2 + index], 6 + 4 + index)
    mix(opposite)

    chosen = slots[...] == me
    begin = jnp.sum(jnp.where(chosen, starts[...].astype(F32), 0.0), axis=1, keepdims=True)
    span = jnp.sum(jnp.where(chosen, lengths[...].astype(F32), 0.0), axis=1, keepdims=True)

    def valid_of(owner, index):
        frame = (index // 8 * 4 + owner) * 8 + index % 8
        sample = (frame * (4 * HOP)).astype(F32)
        return (sample >= begin) & (sample < begin + span)

    key_index = lax.broadcasted_iota(jnp.int32, (1, 1024), 1)
    key_valid = valid_of(key_index // 256, key_index % 256)
    scale = HEAD_DIM ** (-0.5)

    def context_copy(step):
        target = lax.rem(z + 3 - step, 4)
        return pltpu.make_async_remote_copy(
            src_ref=context_out.at[target],
            dst_ref=context_in.at[z],
            send_sem=context_send.at[step],
            recv_sem=context_recv.at[z],
            device_id={"seq": target},
            device_id_type=MESH_ID,
        )

    @pl.loop(0, 4)
    def _(step):
        target = lax.rem(z + 3 - step, 4)
        rows = pl.ds(pl.multiple_of(target * 256, 256), 256)
        for head in range(2):
            lanes = slice(head * HEAD_DIM, (head + 1) * HEAD_DIM)
            query = mixed[rows, lanes]
            key = mixed[:, PART + head * HEAD_DIM : PART + (head + 1) * HEAD_DIM]
            value = mixed[:, 2 * PART + head * HEAD_DIM : 2 * PART + (head + 1) * HEAD_DIM]
            masked = jnp.where(key_valid, nt(query, key) * scale, MASKED)
            weights = jnp.where(
                key_valid, jnp.exp(masked - jnp.max(masked, axis=1, keepdims=True)), 0.0
            )
            total = jnp.sum(weights, axis=1, keepdims=True)
            context_out[target, :, lanes] = (mm(weights.astype(BF), value) / total).astype(BF)

        @pl.when(step < 3)
        def _():
            context_copy(step).start()

    context_in[z] = context_out[z]
    for offset in range(1, 4):
        other = lax.rem(z + offset, 4)
        pltpu.make_async_remote_copy(
            src_ref=context_in.at[other],
            dst_ref=context_in.at[other],
            send_sem=context_send.at[3],
            recv_sem=context_recv.at[other],
            device_id={"seq": up},
            device_id_type=MESH_ID,
        ).wait_recv()

    output = jnp.zeros((256, D), F32)
    for part in range(4):
        start = 3 * PART + part * PART
        output += nt(context_in[part], wide[:, :, start : start + PART].reshape(D, PART))
    row_valid = valid_of(z, lax.broadcasted_iota(jnp.int32, (256, 1), 0))
    attended[...] = jnp.where(row_valid, output, 0.0).reshape(32, 8, D).astype(BF)
    own = rows_all[z].astype(F32).reshape(256, D)
    regrouped[...] = jnp.where(row_valid, own, 0.0).reshape(32, 8, D).astype(BF)

    halo.wait_send()
    ring.drain()
    wide_ring.drain()

    @pl.loop(1, 32)
    def _(offset):
        row_copy(offset).wait_send()

    for copy in z_copies:
        copy.wait_send()

    @pl.loop(0, 3)
    def _(step):
        context_copy(step).wait_send()


def on_device(
    audio, starts, lengths, slots, conv1_weight, conv2_weight, proj_weight, qkv_weight, out_weight
):
    args = (
        audio, starts.reshape(1, 32), lengths.reshape(1, 32), slots.reshape(1, 32),
        jnp.pad(conv1_weight, ((0, 7), (0, 0))), conv2_weight, proj_weight, qkv_weight, out_weight,
        *spectrum_tables(), *filter_tables(), patch_table(),
    )
    vmem, anywhere = pl.BlockSpec(memory_space=pltpu.VMEM), pl.BlockSpec(memory_space=pl.ANY)
    dma = pltpu.SemaphoreType.DMA
    shape = jax.ShapeDtypeStruct((32, 8, D), BF)
    regrouped, attended = pl.pallas_call(
        whole_kernel,
        out_shape=(shape, shape),
        in_specs=[
            anywhere, vmem, vmem, vmem, vmem, anywhere, anywhere, anywhere, vmem,
            anywhere, anywhere, anywhere, anywhere, anywhere,
        ],
        out_specs=(vmem, vmem),
        scratch_shapes=[
            pltpu.VMEM((ROWS, EXT), F32),
            pltpu.VMEM((4, 288, N_FFT), BF),
            pltpu.VMEM((4, 288, N_FFT), BF),
            pltpu.VMEM((4, 288, 128), BF),
            pltpu.VMEM((544, 640), BF),
            pltpu.VMEM((8, 128, CH), BF),
            pltpu.VMEM((544, 41 * CH), BF),
            pltpu.VMEM((256, 20 * CH), BF),
            pltpu.VMEM((9 * CH, CH), BF),
            pltpu.VMEM((N_FFT, N_FFT), BF),
            pltpu.VMEM((N_FFT, N_FFT), BF),
            pltpu.VMEM((N_FFT // 2, 128), BF),
            pltpu.VMEM((N_FFT // 2, 128), BF),
            pltpu.VMEM((384, 640), BF),
            pltpu.VMEM((32, 160, D), BF),
            pltpu.VMEM((32, 32, WIDE), BF),
            pltpu.VMEM((32, 8, D), BF),
            pltpu.VMEM((4, 32, 8, D), BF),
            pltpu.VMEM((1024, 3 * PART), BF),
            pltpu.VMEM((4, 256, PART), BF),
            pltpu.VMEM((4, 256, PART), BF),
            dma((12,)), dma((2,)),
            dma((36,)), dma((36,)), dma((36,)), dma((36,)),
            dma((32,)), dma((32,)), dma((12,)), dma((12,)), dma((4,)), dma((4,)),
        ],
        compiler_params=pltpu.CompilerParams(
            vmem_limit_bytes=VMEM_LIMIT, collective_id=0, has_side_effects=True
        ),
        name="whole",
    )(*args)
    return regrouped.reshape(1, 32, 1, 8, D), attended.reshape(1, 32, 1, 8, D)


def solution(mesh):
    in_specs = (
        P(None, ("dp", "seq")), P(), P(), P(), P(), P(), P("dp", None), P("dp", None), P(None, "dp"),
    )
    out_specs = (P("dp", None, "seq", None, None), P("dp", None, "seq", None, None))
    return jax.shard_map(
        on_device, mesh=mesh, in_specs=in_specs, out_specs=out_specs, check_vma=False
    )
```

```python
import functools
import math

import jax
import jax.numpy as jnp
import numpy as np
from jax import lax
from jax.experimental import pallas as pl
from jax.experimental.pallas import tpu as pltpu
from jax.sharding import PartitionSpec as P

D = 1024
HEADS = 8
HEAD_DIM = 128
MELS = 80
N_FFT = 512
HOP = 160
W = 8
CH = 256
ROWS = 32
RIM = 896
SPAN = 5120
EXT = 6272
BF = jnp.bfloat16
F32 = jnp.float32

SAMPLE_RATE = 16000.0
EPS_LOG = 1e-06
EPS_NORM = 1e-05
MASKED = -1e30
VMEM_LIMIT = 62 * 1024 * 1024


def mel_table(size, bands):
    count = size // 2 + 1
    highest = 2595.0 * math.log10(1.0 + SAMPLE_RATE / 1400.0)
    points = np.linspace(0.0, highest, bands + 2)
    edges = 700.0 * (10.0 ** (points / 2595.0) - 1.0)
    edges[0] = 0.0
    edges[-1] = SAMPLE_RATE / 2.0
    frequency = np.arange(count) * (SAMPLE_RATE / size)
    lower = edges[:-2][None, :]
    middle = edges[1:-1][None, :]
    upper = edges[2:][None, :]
    rising = (frequency[:, None] - lower) / (middle - lower)
    falling = (upper - frequency[:, None]) / (upper - middle)
    return np.maximum(0.0, np.minimum(rising, falling)).astype(np.float32)


def split_high_low(table):
    high = np.asarray(table, np.float64).astype(BF)
    low = (np.asarray(table, np.float64) - high.astype(np.float64)).astype(BF)
    return high, low


def spectrum_tables():
    sample = np.arange(N_FFT)
    angle = (sample[:, None] * np.arange(N_FFT // 2)[None, :] % N_FFT) * (2.0 * math.pi / N_FFT)
    window = 0.5 - 0.5 * np.cos(sample * (2.0 * math.pi / N_FFT))
    return split_high_low(np.concatenate([np.cos(angle), np.sin(angle)], axis=1) * window[:, None])


def filter_tables():
    padded = np.zeros((N_FFT // 2, 128), np.float64)
    padded[:, :MELS] = mel_table(N_FFT, MELS)[: N_FFT // 2]
    return split_high_low(padded)


def patch_table():
    table = np.zeros((3 * 128, 40 * 16), np.float32)
    for g in range(40):
        for a in range(3):
            for b in range(3):
                band = 2 * g - 1 + b
                if 0 <= band < MELS:
                    table[a * 128 + band, g * 16 + 3 * a + b] = 1.0
    return table.astype(BF)


def mm(a, b):
    return jnp.dot(a, b, preferred_element_type=F32)


def halves(value):
    high = value.astype(BF)
    return high, (value - high.astype(F32)).astype(BF)


def frame_step(p, ext, frames_high, frames_low):
    window = ext[:, pl.ds(pl.multiple_of(p * 640, 128), 1152)]
    rows = pl.ds(pl.multiple_of(p * 32, 32), 32)
    for q in range(4):
        start = 64 + HOP * q
        base, offset = start // 128 * 128, start % 128
        if offset:
            piece = pltpu.roll(window[:, base : base + 640], 640 - offset, 1)[:, :N_FFT]
        else:
            piece = window[:, base : base + N_FFT]
        high, low = halves(piece)
        frames_high[q, rows, :] = high
        frames_low[q, rows, :] = low


def mel_of(high, low, dft_high, dft_low, mel_high, mel_low):
    spectrum = mm(high, dft_high[...]) + mm(high, dft_low[...]) + mm(low, dft_high[...])
    half = N_FFT // 2
    power = spectrum[:, :half] * spectrum[:, :half] + spectrum[:, half:] * spectrum[:, half:]
    high, low = halves(power)
    mel = mm(high, mel_high[...]) + mm(high, mel_low[...]) + mm(low, mel_high[...])
    return jnp.log(mel + EPS_LOG).astype(BF)


def late_patches(log_mel, patch_map, patches):
    even = jnp.concatenate([log_mel[0, 64:], log_mel[1, 64:], log_mel[2, 64:]], axis=1)
    patches[:224, :] = mm(even, patch_map[...]).astype(BF)
    odd = jnp.concatenate([log_mel[2, 64:256], log_mel[3, 64:256], log_mel[0, 96:]], axis=1)
    patches[224:416, :] = mm(odd, patch_map[...]).astype(BF)


def early_patches(log_mel, patch_map, patches):
    even = jnp.concatenate([log_mel[0, :64], log_mel[1, :64], log_mel[2, :64]], axis=1)
    odd = jnp.concatenate([log_mel[2, :64], log_mel[3, :64], log_mel[0, 32:96]], axis=1)
    patches[416:, :] = mm(jnp.concatenate([even, odd], axis=0), patch_map[...]).astype(BF)


def spread_taps(conv1, taps):
    taps[...] = jnp.zeros_like(taps)
    for j in range(8):
        taps[j, 16 * j : 16 * j + 9, :] = conv1[...]


def conv1_step(block, j, late, patches, taps, first):
    lanes = slice(block * 128, block * 128 + 128)
    target = pl.ds(pl.multiple_of((block * 8 + j + 1) * CH, CH), CH)
    rows, count = (slice(0, 416), 224) if late else (slice(416, 544), 64)
    result = jnp.maximum(mm(patches[rows, lanes], taps[j]), 0.0).astype(BF)
    first[slice(64, 288) if late else slice(0, 64), target] = result[:count]
    first[slice(352, 544) if late else slice(288, 352), target] = result[count:]


def conv2_step(h, first, conv2, features):
    lanes = pl.ds(pl.multiple_of(h * 512, 512), 768)
    total = mm(first[0:256, lanes], conv2[0:768, :])
    total += mm(first[288:544, lanes], conv2[768:1536, :])
    total += mm(first[32:288, lanes], conv2[1536:2304, :])
    features[:, pl.ds(pl.multiple_of(h * CH, CH), CH)] = jnp.maximum(total, 0.0).astype(BF)


def to_rows(projected, slots_wide):
    out_index = lax.broadcasted_iota(jnp.int32, (256, 256), 0)
    in_index = lax.broadcasted_iota(jnp.int32, (256, 256), 1)
    same_row = slots_wide == out_index // 8
    same_frame = in_index // 32 == out_index % 8
    routing = jnp.where(same_row & same_frame, 1.0, 0.0).astype(BF)
    return mm(routing, projected).astype(BF)

MESH_ID = pl.DeviceIdType.MESH
PART = 2 * HEAD_DIM
WIDE = 3 * PART + D


class Ring:
    def __init__(self, source, buffer, send, recv, place):
        self.source, self.buffer, self.send, self.recv = source, buffer, send, recv
        self.core, self.a, self.b, self.sa, self.sb, self.sibling = place
        self.count = 0
        self.sent = []
        self.rows = buffer.shape[1]

    def shard(self, da, db):
        return lax.rem(self.a + da + 4, 4) * self.sa + lax.rem(self.b + db + 4, 4) * self.sb + self.core

    def part(self, index, half):
        if half is None:
            return self.buffer.at[index]
        step = self.rows // 2
        return self.buffer.at[index, pl.ds(half * step, step)]

    def put(self, index, half, target, slot, own=False):
        copy = pltpu.make_async_remote_copy(
            src_ref=self.source if own else self.part(index, half),
            dst_ref=self.part(index, half),
            send_sem=self.send.at[self.count],
            recv_sem=self.recv.at[slot],
            device_id={"dp": target},
            device_id_type=MESH_ID,
        )
        copy.start()
        self.count += 1
        self.sent.append(copy)

    def got(self, index, half, slot):
        pltpu.make_async_remote_copy(
            src_ref=self.part(index, half),
            dst_ref=self.part(index, half),
            send_sem=self.send.at[0],
            recv_sem=self.recv.at[slot],
            device_id={"dp": self.sibling},
            device_id_type=MESH_ID,
        ).wait_recv()

    def to_b(self, da, own=False):
        index = self.shard(da, 0)
        base = 4 + 4 * (da + 1)
        self.put(index, None, self.shard(0, 1), base, own)
        self.put(index, None, self.shard(0, -1), base + 1, own)
        self.put(index, None, self.sibling, 20 + 4 * (da + 1) + 1, own)

    def begin(self):
        index = self.shard(0, 0)
        self.put(index, None, self.shard(1, 0), 0, True)
        self.put(index, None, self.shard(-1, 0), 1, True)
        self.to_b(0, True)

    def pass_a(self):
        for da, half, slot in ((-1, 0, 0), (1, 1, 1)):
            index = self.shard(da, 0)
            self.got(index, None, slot)
            self.put(index, half, self.shard(-da, 0), 2 + slot)
            self.to_b(da)

    def end_a(self):
        index = self.shard(2, 0)
        self.got(index, 0, 2)
        self.got(index, 1, 3)
        self.to_b(2)

    def pass_b(self, da):
        base = 4 + 4 * (da + 1)
        for db, half, slot in ((-1, 0, 0), (1, 1, 1)):
            index = self.shard(da, db)
            self.got(index, None, base + slot)
            self.put(index, half, self.shard(0, -db), base + 2 + slot)
            self.put(index, None, self.sibling, 20 + 4 * (da + 1) + db + 1)

    def end_b(self, da):
        base = 4 + 4 * (da + 1)
        index = self.shard(da, 2)
        self.got(index, 0, base + 2)
        self.got(index, 1, base + 3)
        self.put(index, None, self.sibling, 20 + 4 * (da + 1) + 3)

    def from_sibling(self):
        for slot in range(16):
            self.got(self.sibling, None, 20 + slot)

    def drain(self):
        for copy in self.sent:
            copy.wait_send()


def normalised(values):
    mean = jnp.mean(values, axis=-1, keepdims=True)
    centered = values - mean
    variance = jnp.mean(centered * centered, axis=-1, keepdims=True)
    return (centered * lax.rsqrt(variance + EPS_NORM)).astype(BF)


def nt(a, b):
    return lax.dot_general(a, b, (((1,), (1,)), ((), ())), preferred_element_type=F32)


def whole_kernel(
    audio_in, starts, lengths, slots, conv1_in, conv2_in, proj_in, qkv_in, out_in,
    dft_high_in, dft_low_in, mel_high_in, mel_low_in, patch_in,
    regrouped, attended,
    ext, frames_high, frames_low, log_mel, patches, taps, first, features,
    conv2, dft_high, dft_low, mel_high, mel_low, patch_map,
    proj, wide, rows_out, rows_all, mixed, context_out, context_in,
    local_sem, halo_sem, proj_send, proj_recv, wide_send, wide_recv,
    row_send, row_recv, z_send, z_recv, context_send, context_recv,
):
    me, z = lax.axis_index("dp"), lax.axis_index("seq")
    x, y, core = me // 8, me // 2 % 4, me % 2
    sibling = me + 1 - 2 * core
    a, b = x * (1 - core) + y * core, y * (1 - core) + x * core
    sa, sb = 8 * (1 - core) + 2 * core, 2 * (1 - core) + 8 * core
    place = (core, a, b, sa, sb, sibling)
    line = me * 4 + z
    after, before = lax.rem(line + 1, 128), lax.rem(line + 127, 128)
    up, down = lax.rem(z + 1, 4), lax.rem(z + 3, 4)

    def local(source, target, index):
        copy = pltpu.make_async_copy(source, target, local_sem.at[index])
        copy.start()
        return copy

    loads = [
        local(source, target, index)
        for index, (source, target) in enumerate(
            (
                (audio_in, ext.at[:, pl.ds(RIM, SPAN)]),
                (dft_high_in, dft_high),
                (dft_low_in, dft_low),
                (mel_high_in, mel_high),
                (mel_low_in, mel_low),
                (patch_in, patch_map),
                (conv2_in, conv2),
                (proj_in, proj.at[me]),
            )
        )
    ]
    parts = [local(out_in, wide.at[me, :, pl.ds(3 * PART, D)], 12)] + [
        local(
            qkv_in.at[:, pl.ds(pl.multiple_of(third * D + z * PART, 128), PART)],
            wide.at[me, :, pl.ds(third * PART, PART)],
            8 + third,
        )
        for third in range(3)
    ]

    barrier = pltpu.get_barrier_semaphore()

    @pl.loop(1, 32)
    def _(offset):
        pl.semaphore_signal(
            barrier, inc=1, device_id={"dp": lax.rem(me + offset, 32)}, device_id_type=MESH_ID
        )

    for offset in range(1, 4):
        pl.semaphore_signal(
            barrier, inc=1, device_id={"seq": lax.rem(z + offset, 4)}, device_id_type=MESH_ID
        )
    for other in (after, before):
        pl.semaphore_signal(
            barrier, inc=1, device_id={"dp": other // 4, "seq": other % 4}, device_id_type=MESH_ID
        )
    spread_taps(conv1_in, taps)
    first[:, :CH] = jnp.zeros((544, CH), BF)
    ext[:, RIM + SPAN :] = jnp.zeros((ROWS, EXT - RIM - SPAN), F32)
    pl.semaphore_wait(barrier, 36)
    halo = pltpu.make_async_remote_copy(
        src_ref=audio_in.at[:, pl.ds(SPAN - RIM, RIM)],
        dst_ref=ext.at[:, pl.ds(0, RIM)],
        send_sem=halo_sem.at[0],
        recv_sem=halo_sem.at[1],
        device_id={"dp": after // 4, "seq": after % 4},
        device_id_type=MESH_ID,
    )
    halo.start()
    ring = Ring(proj_in, proj, proj_send, proj_recv, place)
    ring.begin()

    loads[0].wait()

    @pl.loop(2, 9)
    def _(p):
        frame_step(p, ext, frames_high, frames_low)

    for load in loads[1:5]:
        load.wait()
    tables = (dft_high, dft_low, mel_high, mel_low)

    for q in range(4):
        log_mel[q, 64:, :] = mel_of(frames_high[q, 64:, :], frames_low[q, 64:, :], *tables)

    loads[5].wait()
    late_patches(log_mel, patch_map, patches)

    def conv1_run(late):
        @pl.loop(0, 8)
        def _(j):
            for block in range(5):
                conv1_step(block, j, late, patches, taps, first)

    def conv2_run(low, high):
        @pl.loop(low, high)
        def _(group):
            for i in range(4):
                conv2_step(group * 4 + i, first, conv2, features)

    conv1_run(True)
    ring.pass_a()
    ring.pass_b(0)
    halo.wait_recv()

    @pl.when(line == 0)
    def _():
        ext[:, :RIM] = jnp.zeros((ROWS, RIM), F32)

    @pl.loop(0, 2)
    def _(p):
        frame_step(p, ext, frames_high, frames_low)

    early = mel_of(
        frames_high[:, :64, :].reshape(256, N_FFT), frames_low[:, :64, :].reshape(256, N_FFT), *tables
    )
    for q in range(4):
        log_mel[q, :64, :] = early[64 * q : 64 * q + 64]
    early_patches(log_mel, patch_map, patches)
    conv1_run(False)
    ring.end_a()
    loads[6].wait()
    conv2_run(0, 2)
    ring.pass_b(-1)
    ring.pass_b(1)
    ring.end_b(0)
    conv2_run(2, 4)
    ring.pass_b(2)
    conv2_run(4, 5)
    ring.end_b(-1)
    ring.end_b(1)
    ring.end_b(2)
    for part in parts:
        part.wait()
    wide_ring = Ring(wide.at[me], wide, wide_send, wide_recv, place)
    wide_ring.begin()
    tile_map = jnp.where(
        lax.broadcasted_iota(jnp.int32, (32, 256), 1) % 32 == lax.broadcasted_iota(jnp.int32, (32, 256), 0),
        1.0, 0.0,
    ).astype(BF)
    slot_values = jnp.broadcast_to(slots[...].astype(F32), (8, 32)).astype(BF)
    slots_wide = mm(slot_values, tile_map)[0:1, :].astype(jnp.int32)
    out_index = lax.broadcasted_iota(jnp.int32, (256, 256), 0)
    in_index = lax.broadcasted_iota(jnp.int32, (256, 256), 1)
    routing = jnp.where((slots_wide == out_index // 8) & (in_index // 32 == out_index % 8), 1.0, 0.0).astype(BF)
    ring.from_sibling()
    loads[7].wait()

    projected = mm(features[...], proj[...].reshape(20 * CH, D)).astype(BF)
    rows_out[...] = mm(routing, projected).reshape(32, 8, D).astype(BF)

    def row_copy(offset):
        target = lax.rem(x + 4 - offset // 8, 4) * 8 + lax.rem(me + offset, 8)
        return pltpu.make_async_remote_copy(
            src_ref=rows_out.at[target],
            dst_ref=rows_all.at[z, me],
            send_sem=row_send.at[offset],
            recv_sem=row_recv.at[me],
            device_id={"dp": target},
            device_id_type=MESH_ID,
        )

    @pl.loop(1, 32)
    def _(offset):
        row_copy(offset).start()

    mine = local(rows_out.at[me], rows_all.at[z, me], 11)
    wide_ring.pass_a()
    wide_ring.pass_b(0)
    mine.wait()

    def z_copy(origin, chunk, upwards, index):
        block = rows_all.at[origin, pl.ds(pl.multiple_of(chunk * 8, 8), 8)]
        return pltpu.make_async_remote_copy(
            src_ref=block,
            dst_ref=block,
            send_sem=z_send.at[index],
            recv_sem=z_recv.at[index],
            device_id={"seq": up if upwards else down},
            device_id_type=MESH_ID,
        )

    z_copies = []
    chunks = [lax.rem(x + index, 4) for index in range(4)]
    for index in range(4):
        @pl.loop(0, 8)
        def _(step):
            source = chunks[index] * 8 + step

            @pl.when(source != me)
            def _():
                block = rows_all.at[z, source]
                pltpu.make_async_remote_copy(
                    src_ref=block,
                    dst_ref=block,
                    send_sem=row_send.at[0],
                    recv_sem=row_recv.at[source],
                    device_id={"dp": sibling},
                    device_id_type=MESH_ID,
                ).wait_recv()

        for direction in range(2):
            copy = z_copy(z, chunks[index], direction == 0, 6 * direction + index)
            copy.start()
            z_copies.append(copy)

    def z_wait(origin, chunk, index):
        z_copy(origin, chunk, True, index).wait_recv()

    def z_forward(index):
        z_wait(down, chunks[index], index)
        z_wait(up, chunks[index], 6 + index)
        if index < 2:
            copy = z_copy(down, chunks[index], True, 4 + index)
        else:
            copy = z_copy(up, chunks[index], False, 6 + 2 + index)
        copy.start()
        z_copies.append(copy)

    wide_ring.end_a()
    z_forward(0)
    wide_ring.end_b(0)
    wide_ring.pass_b(-1)
    wide_ring.pass_b(1)
    z_forward(1)
    wide_ring.pass_b(2)
    wide_ring.end_b(-1)
    z_forward(2)
    wide_ring.end_b(1)
    wide_ring.end_b(2)
    z_forward(3)
    wide_ring.from_sibling()

    def mix(origin):
        values = rows_all[origin].astype(F32).reshape(256, D)
        result = mm(normalised(values), wide[:, :, : 3 * PART].reshape(D, 3 * PART))
        mixed[pl.ds(pl.multiple_of(origin * 256, 256), 256), :] = result.astype(BF)

    mix(z)
    mix(down)
    mix(up)
    opposite = lax.rem(z + 2, 4)
    for index in range(2):
        z_wait(opposite, chunks[index], 4 + index)
        z_wait(opposite, chunks[2 + index], 6 + 4 + index)
    mix(opposite)

    chosen = slots[...] == me
    begin = jnp.sum(jnp.where(chosen, starts[...].astype(F32), 0.0), axis=1, keepdims=True)
    span = jnp.sum(jnp.where(chosen, lengths[...].astype(F32), 0.0), axis=1, keepdims=True)

    def valid_of(owner, index):
        frame = (index // 8 * 4 + owner) * 8 + index % 8
        sample = (frame * (4 * HOP)).astype(F32)
        return (sample >= begin) & (sample < begin + span)

    key_index = lax.broadcasted_iota(jnp.int32, (1, 1024), 1)
    bias = jnp.where(valid_of(key_index // 256, key_index % 256), 0.0, MASKED)
    scale = HEAD_DIM ** (-0.5) * math.log2(math.e)

    def context_target(step):
        return lax.rem(z + 2 + step - step // 2 * (2 * step - 1), 4)

    def context_copy(step):
        target = context_target(step)
        return pltpu.make_async_remote_copy(
            src_ref=context_out.at[target],
            dst_ref=context_in.at[z],
            send_sem=context_send.at[step],
            recv_sem=context_recv.at[z],
            device_id={"seq": target},
            device_id_type=MESH_ID,
        )

    @pl.loop(0, 4)
    def _(step):
        target = context_target(step)
        rows = pl.ds(pl.multiple_of(target * 256, 256), 256)
        for head in range(2):
            lanes = slice(head * HEAD_DIM, (head + 1) * HEAD_DIM)
            query = mixed[rows, lanes]
            key = mixed[:, PART + head * HEAD_DIM : PART + (head + 1) * HEAD_DIM]
            value = mixed[:, 2 * PART + head * HEAD_DIM : 2 * PART + (head + 1) * HEAD_DIM]
            scores = nt(query, key) * scale + bias
            weights = jnp.exp2(scores - jnp.max(scores, axis=1, keepdims=True))
            total = jnp.sum(weights, axis=1, keepdims=True)
            context_out[target, :, lanes] = (mm(weights.astype(BF), value) / total).astype(BF)

        @pl.when(step < 3)
        def _():
            context_copy(step).start()

    context_in[z] = context_out[z]
    for offset in range(1, 4):
        other = lax.rem(z + offset, 4)
        pltpu.make_async_remote_copy(
            src_ref=context_in.at[other],
            dst_ref=context_in.at[other],
            send_sem=context_send.at[3],
            recv_sem=context_recv.at[other],
            device_id={"seq": up},
            device_id_type=MESH_ID,
        ).wait_recv()

    output = jnp.zeros((256, D), F32)
    for part in range(4):
        start = 3 * PART + part * PART
        output += nt(context_in[part], wide[:, :, start : start + PART].reshape(D, PART))
    row_valid = valid_of(z, lax.broadcasted_iota(jnp.int32, (256, 1), 0))
    attended[...] = jnp.where(row_valid, output, 0.0).reshape(32, 8, D).astype(BF)
    own = rows_all[z].astype(F32).reshape(256, D)
    regrouped[...] = jnp.where(row_valid, own, 0.0).reshape(32, 8, D).astype(BF)

    halo.wait_send()
    ring.drain()
    wide_ring.drain()

    @pl.loop(1, 32)
    def _(offset):
        row_copy(offset).wait_send()

    for copy in z_copies:
        copy.wait_send()

    @pl.loop(0, 3)
    def _(step):
        context_copy(step).wait_send()


def on_device(
    audio, starts, lengths, slots, conv1_weight, conv2_weight, proj_weight, qkv_weight, out_weight
):
    args = (
        audio, starts.reshape(1, 32), lengths.reshape(1, 32), slots.reshape(1, 32),
        conv1_weight, conv2_weight, proj_weight, qkv_weight, out_weight.T,
        *spectrum_tables(), *filter_tables(), patch_table(),
    )
    vmem, anywhere = pl.BlockSpec(memory_space=pltpu.VMEM), pl.BlockSpec(memory_space=pl.ANY)
    dma = pltpu.SemaphoreType.DMA
    shape = jax.ShapeDtypeStruct((32, 8, D), BF)
    regrouped, attended = pl.pallas_call(
        whole_kernel,
        out_shape=(shape, shape),
        in_specs=[
            anywhere, vmem, vmem, vmem, vmem, anywhere, anywhere, anywhere, anywhere,
            anywhere, anywhere, anywhere, anywhere, anywhere,
        ],
        out_specs=(vmem, vmem),
        scratch_shapes=[
            pltpu.VMEM((ROWS, EXT), F32),
            pltpu.VMEM((4, 288, N_FFT), BF),
            pltpu.VMEM((4, 288, N_FFT), BF),
            pltpu.VMEM((4, 288, 128), BF),
            pltpu.VMEM((544, 640), BF),
            pltpu.VMEM((8, 128, CH), BF),
            pltpu.VMEM((544, 41 * CH), BF),
            pltpu.VMEM((256, 20 * CH), BF),
            pltpu.VMEM((9 * CH, CH), BF),
            pltpu.VMEM((N_FFT, N_FFT), BF),
            pltpu.VMEM((N_FFT, N_FFT), BF),
            pltpu.VMEM((N_FFT // 2, 128), BF),
            pltpu.VMEM((N_FFT // 2, 128), BF),
            pltpu.VMEM((384, 640), BF),
            pltpu.VMEM((32, 160, D), BF),
            pltpu.VMEM((32, 32, WIDE), BF),
            pltpu.VMEM((32, 8, D), BF),
            pltpu.VMEM((4, 32, 8, D), BF),
            pltpu.VMEM((1024, 3 * PART), BF),
            pltpu.VMEM((4, 256, PART), BF),
            pltpu.VMEM((4, 256, PART), BF),
            dma((13,)), dma((2,)),
            dma((36,)), dma((36,)), dma((36,)), dma((36,)),
            dma((32,)), dma((32,)), dma((12,)), dma((12,)), dma((4,)), dma((4,)),
        ],
        compiler_params=pltpu.CompilerParams(
            vmem_limit_bytes=VMEM_LIMIT, collective_id=0, has_side_effects=True
        ),
        name="whole",
    )(*args)
    return regrouped.reshape(1, 32, 1, 8, D), attended.reshape(1, 32, 1, 8, D)


def solution(mesh):
    in_specs = (
        P(None, ("dp", "seq")), P(), P(), P(), P(), P(), P("dp", None), P("dp", None), P(None, "dp"),
    )
    out_specs = (P("dp", None, "seq", None, None), P("dp", None, "seq", None, None))
    return jax.shard_map(
        on_device, mesh=mesh, in_specs=in_specs, out_specs=out_specs, check_vma=False
    )
```

```python
import functools
import math

import jax
import jax.numpy as jnp
import numpy as np
from jax import lax
from jax.experimental import pallas as pl
from jax.experimental.pallas import tpu as pltpu
from jax.sharding import PartitionSpec as P

D = 1024
HEADS = 8
HEAD_DIM = 128
MELS = 80
N_FFT = 512
HOP = 160
W = 8
CH = 256
ROWS = 32
RIM = 896
SPAN = 5120
EXT = 6272
BF = jnp.bfloat16
F32 = jnp.float32

SAMPLE_RATE = 16000.0
EPS_LOG = 1e-06
EPS_NORM = 1e-05
MASKED = -1e30
VMEM_LIMIT = 62 * 1024 * 1024


def mel_table(size, bands):
    count = size // 2 + 1
    highest = 2595.0 * math.log10(1.0 + SAMPLE_RATE / 1400.0)
    points = np.linspace(0.0, highest, bands + 2)
    edges = 700.0 * (10.0 ** (points / 2595.0) - 1.0)
    edges[0] = 0.0
    edges[-1] = SAMPLE_RATE / 2.0
    frequency = np.arange(count) * (SAMPLE_RATE / size)
    lower = edges[:-2][None, :]
    middle = edges[1:-1][None, :]
    upper = edges[2:][None, :]
    rising = (frequency[:, None] - lower) / (middle - lower)
    falling = (upper - frequency[:, None]) / (upper - middle)
    return np.maximum(0.0, np.minimum(rising, falling)).astype(np.float32)


def split_high_low(table):
    high = np.asarray(table, np.float64).astype(BF)
    low = (np.asarray(table, np.float64) - high.astype(np.float64)).astype(BF)
    return high, low


def spectrum_tables():
    sample = np.arange(N_FFT)
    angle = (sample[:, None] * np.arange(N_FFT // 2)[None, :] % N_FFT) * (2.0 * math.pi / N_FFT)
    window = 0.5 - 0.5 * np.cos(sample * (2.0 * math.pi / N_FFT))
    return split_high_low(np.concatenate([np.cos(angle), np.sin(angle)], axis=1) * window[:, None])


def filter_tables():
    padded = np.zeros((N_FFT // 2, 128), np.float64)
    padded[:, :MELS] = mel_table(N_FFT, MELS)[: N_FFT // 2]
    return split_high_low(padded)


def patch_table():
    table = np.zeros((3 * 128, 40 * 16), np.float32)
    for g in range(40):
        for a in range(3):
            for b in range(3):
                band = 2 * g - 1 + b
                if 0 <= band < MELS:
                    table[a * 128 + band, g * 16 + 3 * a + b] = 1.0
    return table.astype(BF)


def mm(a, b):
    return jnp.dot(a, b, preferred_element_type=F32)


def halves(value):
    high = value.astype(BF)
    return high, (value - high.astype(F32)).astype(BF)


def frame_step(p, ext, frames_high, frames_low):
    window = ext[:, pl.ds(pl.multiple_of(p * 640, 128), 1152)]
    rows = pl.ds(pl.multiple_of(p * 32, 32), 32)
    for q in range(4):
        start = 64 + HOP * q
        base, offset = start // 128 * 128, start % 128
        if offset:
            piece = pltpu.roll(window[:, base : base + 640], 640 - offset, 1)[:, :N_FFT]
        else:
            piece = window[:, base : base + N_FFT]
        high, low = halves(piece)
        frames_high[q, rows, :] = high
        frames_low[q, rows, :] = low


def mel_of(high, low, dft_high, dft_low, mel_high, mel_low):
    spectrum = mm(high, dft_high[...]) + mm(high, dft_low[...]) + mm(low, dft_high[...])
    half = N_FFT // 2
    power = spectrum[:, :half] * spectrum[:, :half] + spectrum[:, half:] * spectrum[:, half:]
    high, low = halves(power)
    mel = mm(high, mel_high[...]) + mm(high, mel_low[...]) + mm(low, mel_high[...])
    return jnp.log(mel + EPS_LOG).astype(BF)


def late_patches(log_mel, patch_map, patches):
    even = jnp.concatenate([log_mel[0, 64:], log_mel[1, 64:], log_mel[2, 64:]], axis=1)
    patches[:224, :] = mm(even, patch_map[...]).astype(BF)
    odd = jnp.concatenate([log_mel[2, 64:256], log_mel[3, 64:256], log_mel[0, 96:]], axis=1)
    patches[224:416, :] = mm(odd, patch_map[...]).astype(BF)


def early_patches(log_mel, patch_map, patches):
    even = jnp.concatenate([log_mel[0, :64], log_mel[1, :64], log_mel[2, :64]], axis=1)
    odd = jnp.concatenate([log_mel[2, :64], log_mel[3, :64], log_mel[0, 32:96]], axis=1)
    patches[416:, :] = mm(jnp.concatenate([even, odd], axis=0), patch_map[...]).astype(BF)


def spread_taps(conv1, taps):
    taps[...] = jnp.zeros_like(taps)
    for j in range(8):
        taps[j, 16 * j : 16 * j + 9, :] = conv1[...]


def conv1_step(block, j, late, patches, taps, first):
    lanes = slice(block * 128, block * 128 + 128)
    target = pl.ds(pl.multiple_of((block * 8 + j + 1) * CH, CH), CH)
    rows, count = (slice(0, 416), 224) if late else (slice(416, 544), 64)
    result = jnp.maximum(mm(patches[rows, lanes], taps[j]), 0.0).astype(BF)
    first[slice(64, 288) if late else slice(0, 64), target] = result[:count]
    first[slice(352, 544) if late else slice(288, 352), target] = result[count:]


def conv2_step(h, first, conv2, features):
    lanes = pl.ds(pl.multiple_of(h * 512, 512), 768)
    total = mm(first[0:256, lanes], conv2[0:768, :])
    total += mm(first[288:544, lanes], conv2[768:1536, :])
    total += mm(first[32:288, lanes], conv2[1536:2304, :])
    features[:, pl.ds(pl.multiple_of(h * CH, CH), CH)] = jnp.maximum(total, 0.0).astype(BF)


def to_rows(projected, slots_wide):
    out_index = lax.broadcasted_iota(jnp.int32, (256, 256), 0)
    in_index = lax.broadcasted_iota(jnp.int32, (256, 256), 1)
    same_row = slots_wide == out_index // 8
    same_frame = in_index // 32 == out_index % 8
    routing = jnp.where(same_row & same_frame, 1.0, 0.0).astype(BF)
    return mm(routing, projected).astype(BF)

MESH_ID = pl.DeviceIdType.MESH
PART = 2 * HEAD_DIM
PAIR = 2 * PART
WIDE = 3 * PAIR + D


class Ring:
    def __init__(self, source, buffer, send, recv, place):
        self.source, self.buffer, self.send, self.recv = source, buffer, send, recv
        self.core, self.a, self.b, self.sa, self.sb, self.sibling = place
        self.count = 0
        self.sent = []
        self.rows = buffer.shape[1]

    def shard(self, da, db):
        return lax.rem(self.a + da + 4, 4) * self.sa + lax.rem(self.b + db + 4, 4) * self.sb + self.core

    def part(self, index, half):
        if half is None:
            return self.buffer.at[index]
        step = self.rows // 2
        return self.buffer.at[index, pl.ds(half * step, step)]

    def put(self, index, half, target, slot, own=False):
        copy = pltpu.make_async_remote_copy(
            src_ref=self.source if own else self.part(index, half),
            dst_ref=self.part(index, half),
            send_sem=self.send.at[self.count],
            recv_sem=self.recv.at[slot],
            device_id={"dp": target},
            device_id_type=MESH_ID,
        )
        copy.start()
        self.count += 1
        self.sent.append(copy)

    def got(self, index, half, slot):
        pltpu.make_async_remote_copy(
            src_ref=self.part(index, half),
            dst_ref=self.part(index, half),
            send_sem=self.send.at[0],
            recv_sem=self.recv.at[slot],
            device_id={"dp": self.sibling},
            device_id_type=MESH_ID,
        ).wait_recv()

    def to_b(self, da, own=False):
        index = self.shard(da, 0)
        base = 4 + 4 * (da + 1)
        self.put(index, None, self.shard(0, 1), base, own)
        self.put(index, None, self.shard(0, -1), base + 1, own)
        self.put(index, None, self.sibling, 20 + 4 * (da + 1) + 1, own)

    def begin(self):
        index = self.shard(0, 0)
        self.put(index, None, self.shard(1, 0), 0, True)
        self.put(index, None, self.shard(-1, 0), 1, True)
        self.to_b(0, True)

    def pass_a(self):
        for da, half, slot in ((-1, 0, 0), (1, 1, 1)):
            index = self.shard(da, 0)
            self.got(index, None, slot)
            self.put(index, half, self.shard(-da, 0), 2 + slot)
            self.to_b(da)

    def end_a(self):
        index = self.shard(2, 0)
        self.got(index, 0, 2)
        self.got(index, 1, 3)
        self.to_b(2)

    def pass_b(self, da):
        base = 4 + 4 * (da + 1)
        for db, half, slot in ((-1, 0, 0), (1, 1, 1)):
            index = self.shard(da, db)
            self.got(index, None, base + slot)
            self.put(index, half, self.shard(0, -db), base + 2 + slot)
            self.put(index, None, self.sibling, 20 + 4 * (da + 1) + db + 1)

    def end_b(self, da):
        base = 4 + 4 * (da + 1)
        index = self.shard(da, 2)
        self.got(index, 0, base + 2)
        self.got(index, 1, base + 3)
        self.put(index, None, self.sibling, 20 + 4 * (da + 1) + 3)

    def from_sibling(self):
        for slot in range(16):
            self.got(self.sibling, None, 20 + slot)

    def drain(self):
        for copy in self.sent:
            copy.wait_send()


def normalised(values):
    mean = jnp.mean(values, axis=-1, keepdims=True)
    centered = values - mean
    variance = jnp.mean(centered * centered, axis=-1, keepdims=True)
    return (centered * lax.rsqrt(variance + EPS_NORM)).astype(BF)


def nt(a, b):
    return lax.dot_general(a, b, (((1,), (1,)), ((), ())), preferred_element_type=F32)


def whole_kernel(
    audio_in, starts, lengths, slots, conv1_in, conv2_in, proj_in, qkv_in, out_in,
    dft_high_in, dft_low_in, mel_high_in, mel_low_in, patch_in,
    regrouped, attended,
    ext, frames_high, frames_low, log_mel, patches, taps, first, features,
    conv2, dft_high, dft_low, mel_high, mel_low, patch_map,
    proj, wide, rows_out, rows_own, rows_all, mixed, context_out, context_in,
    local_sem, halo_sem, proj_send, proj_recv, wide_send, wide_recv,
    row_send, row_recv, z_send, z_recv, pass_send, pass_recv, keep_sem, context_send, context_recv,
):
    me, z = lax.axis_index("dp"), lax.axis_index("seq")
    x, y, core = me // 8, me // 2 % 4, me % 2
    sibling = me + 1 - 2 * core
    a, b = x * (1 - core) + y * core, y * (1 - core) + x * core
    sa, sb = 8 * (1 - core) + 2 * core, 2 * (1 - core) + 8 * core
    place = (core, a, b, sa, sb, sibling)
    line = me * 4 + z
    after, before = lax.rem(line + 1, 128), lax.rem(line + 127, 128)
    keeper = core == z // 2
    helper = core != z // 2
    row = me - core + z // 2
    partner, cross = z + 1 - 2 * (z % 2), 3 - z
    beyond = 3 - partner
    pair = z % 2 * 2 + core

    def local(source, target, index):
        copy = pltpu.make_async_copy(source, target, local_sem.at[index])
        copy.start()
        return copy

    loads = [
        local(source, target, index)
        for index, (source, target) in enumerate(
            (
                (audio_in, ext.at[:, pl.ds(RIM, SPAN)]),
                (dft_high_in, dft_high),
                (dft_low_in, dft_low),
                (mel_high_in, mel_high),
                (mel_low_in, mel_low),
                (patch_in, patch_map),
                (conv2_in, conv2),
                (proj_in, proj.at[me]),
            )
        )
    ]
    parts = [local(out_in, wide.at[me, :, pl.ds(3 * PAIR, D)], 12)] + [
        local(
            qkv_in.at[:, pl.ds(pl.multiple_of(third * D + z % 2 * PAIR, 128), PAIR)],
            wide.at[me, :, pl.ds(third * PAIR, PAIR)],
            8 + third,
        )
        for third in range(3)
    ]

    barrier = pltpu.get_barrier_semaphore()

    @pl.loop(1, 32)
    def _(offset):
        pl.semaphore_signal(
            barrier, inc=1, device_id={"dp": lax.rem(me + offset, 32)}, device_id_type=MESH_ID
        )

    for offset in range(1, 4):
        pl.semaphore_signal(
            barrier, inc=1, device_id={"seq": lax.rem(z + offset, 4)}, device_id_type=MESH_ID
        )
    for offset in range(1, 4):
        pl.semaphore_signal(
            barrier,
            inc=1,
            device_id={"dp": sibling, "seq": lax.rem(z + offset, 4)},
            device_id_type=MESH_ID,
        )
    for other in (after, before):
        pl.semaphore_signal(
            barrier, inc=1, device_id={"dp": other // 4, "seq": other % 4}, device_id_type=MESH_ID
        )
    spread_taps(conv1_in, taps)
    first[:, :CH] = jnp.zeros((544, CH), BF)
    ext[:, RIM + SPAN :] = jnp.zeros((ROWS, EXT - RIM - SPAN), F32)
    pl.semaphore_wait(barrier, 39)
    halo = pltpu.make_async_remote_copy(
        src_ref=audio_in.at[:, pl.ds(SPAN - RIM, RIM)],
        dst_ref=ext.at[:, pl.ds(0, RIM)],
        send_sem=halo_sem.at[0],
        recv_sem=halo_sem.at[1],
        device_id={"dp": after // 4, "seq": after % 4},
        device_id_type=MESH_ID,
    )
    halo.start()
    ring = Ring(proj_in, proj, proj_send, proj_recv, place)
    ring.begin()

    loads[0].wait()

    @pl.loop(2, 9)
    def _(p):
        frame_step(p, ext, frames_high, frames_low)

    for load in loads[1:5]:
        load.wait()
    tables = (dft_high, dft_low, mel_high, mel_low)

    for q in range(4):
        log_mel[q, 64:, :] = mel_of(frames_high[q, 64:, :], frames_low[q, 64:, :], *tables)

    loads[5].wait()
    late_patches(log_mel, patch_map, patches)

    def conv1_run(late):
        @pl.loop(0, 8)
        def _(j):
            for block in range(5):
                conv1_step(block, j, late, patches, taps, first)

    def conv2_run(low, high):
        @pl.loop(low, high)
        def _(group):
            for i in range(4):
                conv2_step(group * 4 + i, first, conv2, features)

    conv1_run(True)
    ring.pass_a()
    ring.pass_b(0)
    halo.wait_recv()

    @pl.when(line == 0)
    def _():
        ext[:, :RIM] = jnp.zeros((ROWS, RIM), F32)

    @pl.loop(0, 2)
    def _(p):
        frame_step(p, ext, frames_high, frames_low)

    early = mel_of(
        frames_high[:, :64, :].reshape(256, N_FFT), frames_low[:, :64, :].reshape(256, N_FFT), *tables
    )
    for q in range(4):
        log_mel[q, :64, :] = early[64 * q : 64 * q + 64]
    early_patches(log_mel, patch_map, patches)
    conv1_run(False)
    ring.end_a()
    loads[6].wait()
    conv2_run(0, 2)
    ring.pass_b(-1)
    ring.pass_b(1)
    ring.end_b(0)
    conv2_run(2, 4)
    ring.pass_b(2)
    conv2_run(4, 5)
    ring.end_b(-1)
    ring.end_b(1)
    ring.end_b(2)
    for part in parts:
        part.wait()
    wide_ring = Ring(wide.at[me], wide, wide_send, wide_recv, place)
    wide_ring.begin()
    tile_map = jnp.where(
        lax.broadcasted_iota(jnp.int32, (32, 256), 1) % 32 == lax.broadcasted_iota(jnp.int32, (32, 256), 0),
        1.0, 0.0,
    ).astype(BF)
    slot_values = jnp.broadcast_to(slots[...].astype(F32), (8, 32)).astype(BF)
    slots_wide = mm(slot_values, tile_map)[0:1, :].astype(jnp.int32)
    out_index = lax.broadcasted_iota(jnp.int32, (256, 256), 0)
    in_index = lax.broadcasted_iota(jnp.int32, (256, 256), 1)
    routing = jnp.where((slots_wide == out_index // 8) & (in_index // 32 == out_index % 8), 1.0, 0.0).astype(BF)
    ring.from_sibling()
    loads[7].wait()

    projected = mm(features[...], proj[...].reshape(20 * CH, D)).astype(BF)
    rows_out[...] = mm(routing, projected).reshape(32, 8, D).astype(BF)

    def row_copy(offset):
        target = lax.rem(x + 4 - offset // 8, 4) * 8 + lax.rem(me + offset, 8)
        return pltpu.make_async_remote_copy(
            src_ref=rows_out.at[target],
            dst_ref=rows_own.at[me],
            send_sem=row_send.at[offset],
            recv_sem=row_recv.at[me],
            device_id={"dp": target},
            device_id_type=MESH_ID,
        )

    @pl.loop(1, 32)
    def _(offset):
        row_copy(offset).start()

    mine = local(rows_out.at[me], rows_own.at[me], 11)
    wide_ring.pass_a()
    wide_ring.pass_b(0)
    mine.wait()

    chunks = [lax.rem(x + index, 4) for index in range(4)]
    origins = (z, partner, cross, beyond)

    def part_of(buffer, index):
        return buffer.at[pl.ds(pl.multiple_of(chunks[index] * 8, 8), 8)]

    def row_part(origin, index):
        return rows_all.at[origin, pl.ds(pl.multiple_of(chunks[index] * 8, 8), 8)]

    def to_plane(source, origin, index, base, plane):
        return pltpu.make_async_remote_copy(
            src_ref=source,
            dst_ref=row_part(origin, index),
            send_sem=z_send.at[base + index],
            recv_sem=z_recv.at[base + index],
            device_id={"seq": plane},
            device_id_type=MESH_ID,
        )

    def to_sibling(source, place, index):
        return pltpu.make_async_remote_copy(
            src_ref=source,
            dst_ref=row_part(origins[place], index),
            send_sem=pass_send.at[4 * place + index],
            recv_sem=pass_recv.at[4 * place + index],
            device_id={"dp": sibling},
            device_id_type=MESH_ID,
        )

    def arrived(place, index, base):
        block = row_part(origins[place], index)
        to_plane(block, origins[place], index, base, partner).wait_recv()
        return block

    def own_to_partner(index):
        return to_plane(part_of(rows_own, index), z, index, 0, partner)

    def own_across(index):
        return to_plane(part_of(rows_own, index), z, index, 4, cross)

    def cross_to_partner(index):
        return to_plane(row_part(cross, index), cross, index, 8, partner)

    def own_copy(index):
        return pltpu.make_async_copy(part_of(rows_own, index), row_part(z, index), keep_sem.at[index])

    for index in range(4):
        @pl.loop(0, 8)
        def _(step):
            source = chunks[index] * 8 + step

            @pl.when(source != me)
            def _():
                block = rows_own.at[source]
                pltpu.make_async_remote_copy(
                    src_ref=block,
                    dst_ref=block,
                    send_sem=row_send.at[0],
                    recv_sem=row_recv.at[source],
                    device_id={"dp": sibling},
                    device_id_type=MESH_ID,
                ).wait_recv()

        @pl.when(keeper)
        def _():
            own_to_partner(index).start()
            to_sibling(part_of(rows_own, index), 0, index).start()
            own_copy(index).start()

        @pl.when(helper)
        def _():
            own_across(index).start()

    def pass_cross(index):
        @pl.when(keeper)
        def _():
            block = arrived(2, index, 4)
            cross_to_partner(index).start()
            to_sibling(block, 2, index).start()

    def pass_partner(index):
        @pl.when(keeper)
        def _():
            to_sibling(arrived(1, index, 0), 1, index).start()

    def pass_beyond(index):
        @pl.when(keeper)
        def _():
            to_sibling(arrived(3, index, 8), 3, index).start()

    pass_cross(0)
    wide_ring.end_a()
    pass_cross(1)
    pass_partner(0)
    wide_ring.end_b(0)
    pass_cross(2)
    pass_partner(1)
    wide_ring.pass_b(-1)
    pass_cross(3)
    pass_partner(2)
    wide_ring.pass_b(1)
    pass_partner(3)
    wide_ring.pass_b(2)
    pass_beyond(0)
    wide_ring.end_b(-1)
    wide_ring.end_b(1)
    pass_beyond(1)
    wide_ring.end_b(2)
    wide_ring.from_sibling()

    @pl.when(keeper)
    def _():
        for index in range(4):
            own_copy(index).wait()

    def helped(place):
        @pl.when(helper)
        def _():
            for index in range(4):
                to_sibling(row_part(origins[place], index), place, index).wait_recv()

    def mix(origin):
        values = rows_all[origin].astype(F32).reshape(256, D)
        normed = normalised(values)
        rows = pl.ds(pl.multiple_of(origin * 256, 256), 256)
        for third in range(3):
            lanes = pl.ds(pl.multiple_of(third * PAIR + core * PART, 128), PART)
            result = mm(normed, wide[:, :, lanes].reshape(D, PART))
            mixed[rows, third * PART : third * PART + PART] = result.astype(BF)

    helped(0)
    mix(z)
    pass_beyond(2)
    helped(1)
    mix(partner)
    helped(2)
    mix(cross)
    pass_beyond(3)
    helped(3)
    mix(beyond)

    def bounds(owner):
        chosen = slots[...] == owner
        begin = jnp.sum(jnp.where(chosen, starts[...].astype(F32), 0.0), axis=1, keepdims=True)
        span = jnp.sum(jnp.where(chosen, lengths[...].astype(F32), 0.0), axis=1, keepdims=True)
        return begin, begin + span

    def valid_of(owner, index, limits):
        frame = (index // 8 * 4 + owner) * 8 + index % 8
        sample = (frame * (4 * HOP)).astype(F32)
        return (sample >= limits[0]) & (sample < limits[1])

    key_index = lax.broadcasted_iota(jnp.int32, (1, 1024), 1)
    bias = jnp.where(valid_of(key_index // 256, key_index % 256, bounds(row)), 0.0, MASKED)
    scale = HEAD_DIM ** (-0.5) * math.log2(math.e)

    def context_target(step):
        return lax.rem(z + 2 + step - step // 2 * (2 * step - 1), 4)

    def context_copy(step):
        target = context_target(step)
        return pltpu.make_async_remote_copy(
            src_ref=context_out.at[target],
            dst_ref=context_in.at[pair],
            send_sem=context_send.at[step],
            recv_sem=context_recv.at[pair],
            device_id={"dp": row, "seq": target},
            device_id_type=MESH_ID,
        )

    @pl.loop(0, 4)
    def _(step):
        target = context_target(step)
        rows = pl.ds(pl.multiple_of(target * 256, 256), 256)
        for head in range(2):
            lanes = slice(head * HEAD_DIM, (head + 1) * HEAD_DIM)
            query = mixed[rows, lanes]
            key = mixed[:, PART + head * HEAD_DIM : PART + (head + 1) * HEAD_DIM]
            value = mixed[:, 2 * PART + head * HEAD_DIM : 2 * PART + (head + 1) * HEAD_DIM]
            scores = nt(query, key) * scale + bias
            weights = jnp.exp2(scores - jnp.max(scores, axis=1, keepdims=True))
            total = jnp.sum(weights, axis=1, keepdims=True)
            context_out[target, :, lanes] = (mm(weights.astype(BF), value) / total).astype(BF)

        @pl.when(step < 3)
        def _():
            context_copy(step).start()

    @pl.when(keeper)
    def _():
        context_in[pair] = context_out[z]

    @pl.when(helper)
    def _():
        context_copy(3).start()

    def context_wait(other):
        pltpu.make_async_remote_copy(
            src_ref=context_in.at[other],
            dst_ref=context_in.at[other],
            send_sem=context_send.at[3],
            recv_sem=context_recv.at[other],
            device_id={"dp": row, "seq": cross},
            device_id_type=MESH_ID,
        ).wait_recv()

    for offset in range(1, 4):
        context_wait(lax.rem(pair + offset, 4))

    @pl.when(helper)
    def _():
        context_wait(pair)

    output = jnp.zeros((256, D), F32)
    for part in range(4):
        start = 3 * PAIR + part * PART
        output += nt(context_in[part], wide[:, :, start : start + PART].reshape(D, PART))
    row_valid = valid_of(z, lax.broadcasted_iota(jnp.int32, (256, 1), 0), bounds(me))
    attended[...] = jnp.where(row_valid, output, 0.0).reshape(32, 8, D).astype(BF)
    own = rows_own[...].astype(F32).reshape(256, D)
    regrouped[...] = jnp.where(row_valid, own, 0.0).reshape(32, 8, D).astype(BF)

    halo.wait_send()
    ring.drain()
    wide_ring.drain()

    @pl.loop(1, 32)
    def _(offset):
        row_copy(offset).wait_send()

    @pl.when(keeper)
    def _():
        for index in range(4):
            own_to_partner(index).wait_send()
            cross_to_partner(index).wait_send()
            for place in range(4):
                to_sibling(part_of(rows_own, index), place, index).wait_send()

    @pl.when(helper)
    def _():
        for index in range(4):
            own_across(index).wait_send()
        context_copy(3).wait_send()

    @pl.loop(0, 3)
    def _(step):
        context_copy(step).wait_send()


def on_device(
    audio, starts, lengths, slots, conv1_weight, conv2_weight, proj_weight, qkv_weight, out_weight
):
    args = (
        audio, starts.reshape(1, 32), lengths.reshape(1, 32), slots.reshape(1, 32),
        conv1_weight, conv2_weight, proj_weight, qkv_weight, out_weight.T,
        *spectrum_tables(), *filter_tables(), patch_table(),
    )
    vmem, anywhere = pl.BlockSpec(memory_space=pltpu.VMEM), pl.BlockSpec(memory_space=pl.ANY)
    dma = pltpu.SemaphoreType.DMA
    shape = jax.ShapeDtypeStruct((32, 8, D), BF)
    regrouped, attended = pl.pallas_call(
        whole_kernel,
        out_shape=(shape, shape),
        in_specs=[
            anywhere, vmem, vmem, vmem, vmem, anywhere, anywhere, anywhere, anywhere,
            anywhere, anywhere, anywhere, anywhere, anywhere,
        ],
        out_specs=(vmem, vmem),
        scratch_shapes=[
            pltpu.VMEM((ROWS, EXT), F32),
            pltpu.VMEM((4, 288, N_FFT), BF),
            pltpu.VMEM((4, 288, N_FFT), BF),
            pltpu.VMEM((4, 288, 128), BF),
            pltpu.VMEM((544, 640), BF),
            pltpu.VMEM((8, 128, CH), BF),
            pltpu.VMEM((544, 41 * CH), BF),
            pltpu.VMEM((256, 20 * CH), BF),
            pltpu.VMEM((9 * CH, CH), BF),
            pltpu.VMEM((N_FFT, N_FFT), BF),
            pltpu.VMEM((N_FFT, N_FFT), BF),
            pltpu.VMEM((N_FFT // 2, 128), BF),
            pltpu.VMEM((N_FFT // 2, 128), BF),
            pltpu.VMEM((384, 640), BF),
            pltpu.VMEM((32, 160, D), BF),
            pltpu.VMEM((32, 32, WIDE), BF),
            pltpu.VMEM((32, 8, D), BF),
            pltpu.VMEM((32, 8, D), BF),
            pltpu.VMEM((4, 32, 8, D), BF),
            pltpu.VMEM((1024, 3 * PART), BF),
            pltpu.VMEM((4, 256, PART), BF),
            pltpu.VMEM((4, 256, PART), BF),
            dma((13,)), dma((2,)),
            dma((36,)), dma((36,)), dma((36,)), dma((36,)),
            dma((32,)), dma((32,)), dma((12,)), dma((12,)), dma((16,)), dma((16,)), dma((4,)), dma((4,)), dma((4,)),
        ],
        compiler_params=pltpu.CompilerParams(
            vmem_limit_bytes=VMEM_LIMIT, collective_id=0, has_side_effects=True
        ),
        name="whole",
    )(*args)
    return regrouped.reshape(1, 32, 1, 8, D), attended.reshape(1, 32, 1, 8, D)


def solution(mesh):
    in_specs = (
        P(None, ("dp", "seq")), P(), P(), P(), P(), P(), P("dp", None), P("dp", None), P(None, "dp"),
    )
    out_specs = (P("dp", None, "seq", None, None), P("dp", None, "seq", None, None))
    return jax.shard_map(
        on_device, mesh=mesh, in_specs=in_specs, out_specs=out_specs, check_vma=False
    )
```

```python
import functools
import math

import jax
import jax.numpy as jnp
import numpy as np
from jax import lax
from jax.experimental import pallas as pl
from jax.experimental.pallas import tpu as pltpu
from jax.sharding import PartitionSpec as P

D = 1024
HEADS = 8
HEAD_DIM = 128
MELS = 80
N_FFT = 512
HOP = 160
W = 8
CH = 256
ROWS = 32
RIM = 896
SPAN = 5120
EXT = 6272
BF = jnp.bfloat16
F32 = jnp.float32

SAMPLE_RATE = 16000.0
EPS_LOG = 1e-06
EPS_NORM = 1e-05
MASKED = -1e30
VMEM_LIMIT = 56 * 1024 * 1024


def mel_table(size, bands):
    count = size // 2 + 1
    highest = 2595.0 * math.log10(1.0 + SAMPLE_RATE / 1400.0)
    points = np.linspace(0.0, highest, bands + 2)
    edges = 700.0 * (10.0 ** (points / 2595.0) - 1.0)
    edges[0] = 0.0
    edges[-1] = SAMPLE_RATE / 2.0
    frequency = np.arange(count) * (SAMPLE_RATE / size)
    lower = edges[:-2][None, :]
    middle = edges[1:-1][None, :]
    upper = edges[2:][None, :]
    rising = (frequency[:, None] - lower) / (middle - lower)
    falling = (upper - frequency[:, None]) / (upper - middle)
    return np.maximum(0.0, np.minimum(rising, falling)).astype(np.float32)


def split_high_low(table):
    high = np.asarray(table, np.float64).astype(BF)
    low = (np.asarray(table, np.float64) - high.astype(np.float64)).astype(BF)
    return high, low


def spectrum_tables():
    sample = np.arange(N_FFT)
    angle = (sample[:, None] * np.arange(N_FFT // 2)[None, :] % N_FFT) * (2.0 * math.pi / N_FFT)
    window = 0.5 - 0.5 * np.cos(sample * (2.0 * math.pi / N_FFT))
    return split_high_low(np.concatenate([np.cos(angle), np.sin(angle)], axis=1) * window[:, None])


def filter_tables():
    padded = np.zeros((N_FFT // 2, 128), np.float64)
    padded[:, :MELS] = mel_table(N_FFT, MELS)[: N_FFT // 2]
    return split_high_low(padded)


def patch_table():
    table = np.zeros((3 * 128, 40 * 16), np.float32)
    for g in range(40):
        for a in range(3):
            for b in range(3):
                band = 2 * g - 1 + b
                if 0 <= band < MELS:
                    table[a * 128 + band, g * 16 + 3 * a + b] = 1.0
    return table.astype(BF)


def mm(a, b):
    return jnp.dot(a, b, preferred_element_type=F32)


def halves(value):
    high = value.astype(BF)
    return high, (value - high.astype(F32)).astype(BF)


def frame_step(p, ext, frames_high, frames_low):
    window = ext[:, pl.ds(pl.multiple_of(p * 640, 128), 1152)]
    rows = pl.ds(pl.multiple_of(p * 32, 32), 32)
    for q in range(4):
        start = 64 + HOP * q
        base, offset = start // 128 * 128, start % 128
        if offset:
            piece = pltpu.roll(window[:, base : base + 640], 640 - offset, 1)[:, :N_FFT]
        else:
            piece = window[:, base : base + N_FFT]
        high, low = halves(piece)
        frames_high[q, rows, :] = high
        frames_low[q, rows, :] = low


def mel_of(high, low, dft_high, dft_low, mel_high, mel_low):
    spectrum = mm(high, dft_high[...]) + mm(high, dft_low[...]) + mm(low, dft_high[...])
    half = N_FFT // 2
    power = spectrum[:, :half] * spectrum[:, :half] + spectrum[:, half:] * spectrum[:, half:]
    high, low = halves(power)
    mel = mm(high, mel_high[...]) + mm(high, mel_low[...]) + mm(low, mel_high[...])
    return jnp.log(mel + EPS_LOG).astype(BF)


def late_patches(log_mel, patch_map, patches):
    even = jnp.concatenate([log_mel[0, 64:], log_mel[1, 64:], log_mel[2, 64:]], axis=1)
    patches[:224, :] = mm(even, patch_map[...]).astype(BF)
    odd = jnp.concatenate([log_mel[2, 64:256], log_mel[3, 64:256], log_mel[0, 96:]], axis=1)
    patches[224:416, :] = mm(odd, patch_map[...]).astype(BF)


def early_patches(log_mel, patch_map, patches):
    even = jnp.concatenate([log_mel[0, :64], log_mel[1, :64], log_mel[2, :64]], axis=1)
    odd = jnp.concatenate([log_mel[2, :64], log_mel[3, :64], log_mel[0, 32:96]], axis=1)
    patches[416:, :] = mm(jnp.concatenate([even, odd], axis=0), patch_map[...]).astype(BF)


def spread_taps(conv1, taps):
    taps[...] = jnp.zeros_like(taps)
    for j in range(8):
        taps[j, 16 * j : 16 * j + 9, :] = conv1[...]


def conv1_step(block, j, late, patches, taps, first):
    lanes = slice(block * 128, block * 128 + 128)
    target = pl.ds(pl.multiple_of((block * 8 + j + 1) * CH, CH), CH)
    rows, count = (slice(0, 416), 224) if late else (slice(416, 544), 64)
    result = jnp.maximum(mm(patches[rows, lanes], taps[j]), 0.0).astype(BF)
    first[slice(64, 288) if late else slice(0, 64), target] = result[:count]
    first[slice(352, 544) if late else slice(288, 352), target] = result[count:]


def conv2_step(h, first, conv2, features):
    lanes = pl.ds(pl.multiple_of(h * 512, 512), 768)
    total = mm(first[0:256, lanes], conv2[0:768, :])
    total += mm(first[288:544, lanes], conv2[768:1536, :])
    total += mm(first[32:288, lanes], conv2[1536:2304, :])
    features[:, pl.ds(pl.multiple_of(h * CH, CH), CH)] = jnp.maximum(total, 0.0).astype(BF)


def to_rows(projected, slots_wide):
    out_index = lax.broadcasted_iota(jnp.int32, (256, 256), 0)
    in_index = lax.broadcasted_iota(jnp.int32, (256, 256), 1)
    same_row = slots_wide == out_index // 8
    same_frame = in_index // 32 == out_index % 8
    routing = jnp.where(same_row & same_frame, 1.0, 0.0).astype(BF)
    return mm(routing, projected).astype(BF)

MESH_ID = pl.DeviceIdType.MESH
PART = 2 * HEAD_DIM
PAIR = 2 * PART
WIDE = 3 * PAIR + D


class Ring:
    def __init__(self, source, buffer, send, recv, place):
        self.source, self.buffer, self.send, self.recv = source, buffer, send, recv
        self.core, self.a, self.b, self.sa, self.sb, self.sibling = place
        self.count = 0
        self.sent = []
        self.rows = buffer.shape[1]

    def shard(self, da, db):
        return lax.rem(self.a + da + 4, 4) * self.sa + lax.rem(self.b + db + 4, 4) * self.sb + self.core

    def part(self, index, half):
        if half is None:
            return self.buffer.at[index]
        step = self.rows // 2
        return self.buffer.at[index, pl.ds(half * step, step)]

    def origin(self, half):
        step = self.rows // 2
        return self.source if half is None else self.source.at[pl.ds(half * step, step)]

    def put(self, index, half, target, slot, own=False):
        copy = pltpu.make_async_remote_copy(
            src_ref=self.origin(half) if own else self.part(index, half),
            dst_ref=self.part(index, half),
            send_sem=self.send.at[self.count],
            recv_sem=self.recv.at[slot],
            device_id={"dp": target},
            device_id_type=MESH_ID,
        )
        copy.start()
        self.count += 1
        self.sent.append(copy)

    def got(self, index, half, slot):
        pltpu.make_async_remote_copy(
            src_ref=self.part(index, half),
            dst_ref=self.part(index, half),
            send_sem=self.send.at[0],
            recv_sem=self.recv.at[slot],
            device_id={"dp": self.sibling},
            device_id_type=MESH_ID,
        ).wait_recv()

    def to_both(self, index, above, below, base, line, own=False):
        for target, half, slot in ((above, 0, 0), (below, 1, 1)):
            self.put(index, half, target, base + slot, own)
            self.put(index, 1 - half, target, 36 + 2 * line + slot, own)

    def pass_both(self, lower, upper, above, below, base):
        self.got(lower, 0, base)
        self.put(lower, 0, above, base + 2)
        self.got(upper, 1, base + 1)
        self.put(upper, 1, below, base + 3)

    def to_b(self, da, own=False):
        index = self.shard(da, 0)
        self.to_both(index, self.shard(0, 1), self.shard(0, -1), 4 + 4 * (da + 1), da + 2, own)
        self.put(index, None, self.sibling, 20 + 4 * (da + 1) + 1, own)

    def begin(self):
        self.to_both(self.shard(0, 0), self.shard(1, 0), self.shard(-1, 0), 0, 0, True)

    def pass_a(self):
        self.pass_both(self.shard(-1, 0), self.shard(1, 0), self.shard(1, 0), self.shard(-1, 0), 0)
        self.got(self.shard(-1, 0), 1, 36)
        self.to_b(-1)
        self.got(self.shard(1, 0), 0, 37)
        self.to_b(1)

    def end_a(self):
        index = self.shard(2, 0)
        self.got(index, 0, 2)
        self.got(index, 1, 3)
        self.to_b(2)

    def pass_b(self, da):
        lower, upper, slot = self.shard(da, -1), self.shard(da, 1), 36 + 2 * (da + 2)
        self.pass_both(lower, upper, self.shard(0, 1), self.shard(0, -1), 4 + 4 * (da + 1))
        self.got(lower, 1, slot)
        self.put(lower, None, self.sibling, 20 + 4 * (da + 1))
        self.got(upper, 0, slot + 1)
        self.put(upper, None, self.sibling, 20 + 4 * (da + 1) + 2)

    def end_b(self, da):
        base = 4 + 4 * (da + 1)
        index = self.shard(da, 2)
        self.got(index, 0, base + 2)
        self.got(index, 1, base + 3)
        self.put(index, None, self.sibling, 20 + 4 * (da + 1) + 3)

    def from_sibling(self):
        for slot in range(16):
            self.got(self.sibling, None, 20 + slot)

    def drain(self):
        for copy in self.sent:
            copy.wait_send()


def normalised(values):
    mean = jnp.mean(values, axis=-1, keepdims=True)
    centered = values - mean
    variance = jnp.mean(centered * centered, axis=-1, keepdims=True)
    return (centered * lax.rsqrt(variance + EPS_NORM)).astype(BF)


def nt(a, b):
    return lax.dot_general(a, b, (((1,), (1,)), ((), ())), preferred_element_type=F32)


def whole_kernel(
    audio_in, starts_in, lengths_in, slots_in, conv1_in, conv2_in, proj_in, qkv_in, out_in,
    dft_high_in, dft_low_in, mel_high_in, mel_low_in, patch_in,
    regrouped, attended,
    ext, frames_high, frames_low, log_mel, patches, taps, first, features,
    starts, lengths, slots, conv1, conv2, dft_high, dft_low, mel_high, mel_low, patch_map,
    proj, wide, rows_out, rows_own, rows_all, mixed, context_out, context_in,
    local_sem, halo_sem, proj_send, proj_recv, wide_send, wide_recv,
    row_send, row_recv, z_send, z_recv, pass_send, pass_recv, keep_sem, context_send, context_recv,
):
    me, z = lax.axis_index("dp"), lax.axis_index("seq")
    x, y, core = me // 8, me // 2 % 4, me % 2
    sibling = me + 1 - 2 * core
    a, b = x * (1 - core) + y * core, y * (1 - core) + x * core
    sa, sb = 8 * (1 - core) + 2 * core, 2 * (1 - core) + 8 * core
    place = (core, a, b, sa, sb, sibling)
    line = me * 4 + z
    after, before = lax.rem(line + 1, 128), lax.rem(line + 127, 128)
    keeper = core == z // 2
    helper = core != z // 2
    row = me - core + z // 2
    partner, cross = z + 1 - 2 * (z % 2), 3 - z
    beyond = 3 - partner
    pair = z % 2 * 2 + core

    def local(source, target, index):
        copy = pltpu.make_async_copy(source, target, local_sem.at[index])
        copy.start()
        return copy

    loads = [
        local(source, target, index)
        for index, (source, target) in enumerate(
            (
                (audio_in, ext.at[:, pl.ds(RIM, SPAN)]),
                (dft_high_in, dft_high),
                (dft_low_in, dft_low),
                (mel_high_in, mel_high),
                (mel_low_in, mel_low),
                (patch_in, patch_map),
                (conv2_in, conv2),
                (proj_in, proj.at[me]),
            )
        )
    ]
    parts = [local(out_in, wide.at[me, :, pl.ds(3 * PAIR, D)], 12)] + [
        local(
            qkv_in.at[:, pl.ds(pl.multiple_of(third * D + z % 2 * PAIR, 128), PAIR)],
            wide.at[me, :, pl.ds(third * PAIR, PAIR)],
            8 + third,
        )
        for third in range(3)
    ]

    small = [
        local(source, target, 13 + index)
        for index, (source, target) in enumerate(
            ((conv1_in, conv1), (starts_in, starts), (lengths_in, lengths), (slots_in, slots))
        )
    ]
    barrier = pltpu.get_barrier_semaphore()

    @pl.loop(1, 32)
    def _(offset):
        pl.semaphore_signal(
            barrier, inc=1, device_id={"dp": lax.rem(me + offset, 32)}, device_id_type=MESH_ID
        )

    for offset in range(1, 4):
        pl.semaphore_signal(
            barrier, inc=1, device_id={"seq": lax.rem(z + offset, 4)}, device_id_type=MESH_ID
        )
    for offset in range(1, 4):
        pl.semaphore_signal(
            barrier,
            inc=1,
            device_id={"dp": sibling, "seq": lax.rem(z + offset, 4)},
            device_id_type=MESH_ID,
        )
    for other in (after, before):
        pl.semaphore_signal(
            barrier, inc=1, device_id={"dp": other // 4, "seq": other % 4}, device_id_type=MESH_ID
        )
    for load in small:
        load.wait()
    spread_taps(conv1, taps)
    first[:, :CH] = jnp.zeros((544, CH), BF)
    ext[:, RIM + SPAN :] = jnp.zeros((ROWS, EXT - RIM - SPAN), F32)
    pl.semaphore_wait(barrier, 39)
    halo = pltpu.make_async_remote_copy(
        src_ref=audio_in.at[:, pl.ds(SPAN - RIM, RIM)],
        dst_ref=ext.at[:, pl.ds(0, RIM)],
        send_sem=halo_sem.at[0],
        recv_sem=halo_sem.at[1],
        device_id={"dp": after // 4, "seq": after % 4},
        device_id_type=MESH_ID,
    )
    halo.start()
    ring = Ring(proj_in, proj, proj_send, proj_recv, place)
    ring.begin()

    loads[0].wait()

    @pl.loop(2, 9)
    def _(p):
        frame_step(p, ext, frames_high, frames_low)

    for load in loads[1:5]:
        load.wait()
    tables = (dft_high, dft_low, mel_high, mel_low)

    for q in range(4):
        if q == 1:
            ring.to_b(0, True)
        log_mel[q, 64:, :] = mel_of(frames_high[q, 64:, :], frames_low[q, 64:, :], *tables)

    loads[5].wait()
    late_patches(log_mel, patch_map, patches)

    def conv1_run(late):
        @pl.loop(0, 8)
        def _(j):
            for block in range(5):
                conv1_step(block, j, late, patches, taps, first)

    def conv2_run(low, high):
        @pl.loop(low, high)
        def _(group):
            for i in range(4):
                conv2_step(group * 4 + i, first, conv2, features)

    ring.pass_a()
    conv1_run(True)
    ring.pass_b(0)
    halo.wait_recv()

    @pl.when(line == 0)
    def _():
        ext[:, :RIM] = jnp.zeros((ROWS, RIM), F32)

    @pl.loop(0, 2)
    def _(p):
        frame_step(p, ext, frames_high, frames_low)

    early = mel_of(
        frames_high[:, :64, :].reshape(256, N_FFT), frames_low[:, :64, :].reshape(256, N_FFT), *tables
    )
    for q in range(4):
        log_mel[q, :64, :] = early[64 * q : 64 * q + 64]
    early_patches(log_mel, patch_map, patches)
    conv1_run(False)
    ring.end_a()
    loads[6].wait()
    conv2_run(0, 2)
    ring.pass_b(-1)
    ring.pass_b(1)
    ring.end_b(0)
    conv2_run(2, 4)
    ring.pass_b(2)
    conv2_run(4, 5)
    ring.end_b(-1)
    ring.end_b(1)
    ring.end_b(2)
    for part in parts:
        part.wait()
    wide_ring = Ring(wide.at[me], wide, wide_send, wide_recv, place)
    wide_ring.begin()
    wide_ring.to_b(0, True)
    tile_map = jnp.where(
        lax.broadcasted_iota(jnp.int32, (32, 256), 1) % 32 == lax.broadcasted_iota(jnp.int32, (32, 256), 0),
        1.0, 0.0,
    ).astype(BF)
    slot_values = jnp.broadcast_to(slots[...].astype(F32), (8, 32)).astype(BF)
    slots_wide = mm(slot_values, tile_map)[0:1, :].astype(jnp.int32)
    out_index = lax.broadcasted_iota(jnp.int32, (256, 256), 0)
    in_index = lax.broadcasted_iota(jnp.int32, (256, 256), 1)
    routing = jnp.where((slots_wide == out_index // 8) & (in_index // 32 == out_index % 8), 1.0, 0.0).astype(BF)
    ring.from_sibling()
    loads[7].wait()

    projected = mm(features[...], proj[...].reshape(20 * CH, D)).astype(BF)
    rows_out[...] = mm(routing, projected).reshape(32, 8, D).astype(BF)

    def row_copy(offset):
        target = lax.rem(x + 4 - offset // 8, 4) * 8 + lax.rem(me + offset, 8)
        return pltpu.make_async_remote_copy(
            src_ref=rows_out.at[target],
            dst_ref=rows_own.at[me],
            send_sem=row_send.at[offset],
            recv_sem=row_recv.at[me],
            device_id={"dp": target},
            device_id_type=MESH_ID,
        )

    @pl.loop(1, 32)
    def _(offset):
        row_copy(offset).start()

    mine = local(rows_out.at[me], rows_own.at[me], 11)
    wide_ring.pass_a()
    wide_ring.pass_b(0)
    mine.wait()

    chunks = [lax.rem(x + index, 4) for index in range(4)]
    origins = (z, partner, cross, beyond)

    def part_of(buffer, index):
        return buffer.at[pl.ds(pl.multiple_of(chunks[index] * 8, 8), 8)]

    def row_part(origin, index):
        return rows_all.at[origin, pl.ds(pl.multiple_of(chunks[index] * 8, 8), 8)]

    def to_plane(source, origin, index, base, plane):
        return pltpu.make_async_remote_copy(
            src_ref=source,
            dst_ref=row_part(origin, index),
            send_sem=z_send.at[base + index],
            recv_sem=z_recv.at[base + index],
            device_id={"seq": plane},
            device_id_type=MESH_ID,
        )

    def to_sibling(source, place, index):
        return pltpu.make_async_remote_copy(
            src_ref=source,
            dst_ref=row_part(origins[place], index),
            send_sem=pass_send.at[4 * place + index],
            recv_sem=pass_recv.at[4 * place + index],
            device_id={"dp": sibling},
            device_id_type=MESH_ID,
        )

    def arrived(place, index, base):
        block = row_part(origins[place], index)
        to_plane(block, origins[place], index, base, partner).wait_recv()
        return block

    def own_to_partner(index):
        return to_plane(part_of(rows_own, index), z, index, 0, partner)

    def own_across(index):
        return to_plane(part_of(rows_own, index), z, index, 4, cross)

    def cross_to_partner(index):
        return to_plane(row_part(cross, index), cross, index, 8, partner)

    def own_copy(index):
        return pltpu.make_async_copy(part_of(rows_own, index), row_part(z, index), keep_sem.at[index])

    for index in range(4):
        @pl.loop(0, 8)
        def _(step):
            source = chunks[index] * 8 + step

            @pl.when(source != me)
            def _():
                block = rows_own.at[source]
                pltpu.make_async_remote_copy(
                    src_ref=block,
                    dst_ref=block,
                    send_sem=row_send.at[0],
                    recv_sem=row_recv.at[source],
                    device_id={"dp": sibling},
                    device_id_type=MESH_ID,
                ).wait_recv()

        @pl.when(keeper)
        def _():
            own_to_partner(index).start()
            to_sibling(part_of(rows_own, index), 0, index).start()
            own_copy(index).start()

        @pl.when(helper)
        def _():
            own_across(index).start()

    def pass_cross(index):
        @pl.when(keeper)
        def _():
            block = arrived(2, index, 4)
            cross_to_partner(index).start()
            to_sibling(block, 2, index).start()

    def pass_partner(index):
        @pl.when(keeper)
        def _():
            to_sibling(arrived(1, index, 0), 1, index).start()

    def pass_beyond(index):
        @pl.when(keeper)
        def _():
            to_sibling(arrived(3, index, 8), 3, index).start()

    pass_cross(0)
    wide_ring.end_a()
    pass_cross(1)
    pass_partner(0)
    wide_ring.end_b(0)
    pass_cross(2)
    pass_partner(1)
    wide_ring.pass_b(-1)
    pass_cross(3)
    pass_partner(2)
    wide_ring.pass_b(1)
    pass_partner(3)
    wide_ring.pass_b(2)
    pass_beyond(0)
    wide_ring.end_b(-1)
    wide_ring.end_b(1)
    pass_beyond(1)
    wide_ring.end_b(2)
    wide_ring.from_sibling()

    @pl.when(keeper)
    def _():
        for index in range(4):
            own_copy(index).wait()

    def helped(place):
        @pl.when(helper)
        def _():
            for index in range(4):
                to_sibling(row_part(origins[place], index), place, index).wait_recv()

    def mix(origin):
        values = rows_all[origin].astype(F32).reshape(256, D)
        normed = normalised(values)
        rows = pl.ds(pl.multiple_of(origin * 256, 256), 256)
        for third in range(3):
            lanes = pl.ds(pl.multiple_of(third * PAIR + core * PART, 128), PART)
            result = mm(normed, wide[:, :, lanes].reshape(D, PART))
            mixed[rows, third * PART : third * PART + PART] = result.astype(BF)

    helped(0)
    mix(z)
    pass_beyond(2)
    helped(1)
    mix(partner)
    helped(2)
    mix(cross)
    pass_beyond(3)
    helped(3)
    mix(beyond)

    def bounds(owner):
        chosen = slots[...] == owner
        begin = jnp.sum(jnp.where(chosen, starts[...].astype(F32), 0.0), axis=1, keepdims=True)
        span = jnp.sum(jnp.where(chosen, lengths[...].astype(F32), 0.0), axis=1, keepdims=True)
        return begin, begin + span

    def valid_of(owner, index, limits):
        frame = (index // 8 * 4 + owner) * 8 + index % 8
        sample = (frame * (4 * HOP)).astype(F32)
        return (sample >= limits[0]) & (sample < limits[1])

    key_index = lax.broadcasted_iota(jnp.int32, (1, 1024), 1)
    bias = jnp.where(valid_of(key_index // 256, key_index % 256, bounds(row)), 0.0, MASKED)
    scale = HEAD_DIM ** (-0.5) * math.log2(math.e)

    def context_target(step):
        return lax.rem(z + 2 + step - step // 2 * (2 * step - 1), 4)

    def context_copy(step):
        target = context_target(step)
        return pltpu.make_async_remote_copy(
            src_ref=context_out.at[target],
            dst_ref=context_in.at[pair],
            send_sem=context_send.at[step],
            recv_sem=context_recv.at[pair],
            device_id={"dp": row, "seq": target},
            device_id_type=MESH_ID,
        )

    @pl.loop(0, 4)
    def _(step):
        target = context_target(step)
        rows = pl.ds(pl.multiple_of(target * 256, 256), 256)
        for head in range(2):
            lanes = slice(head * HEAD_DIM, (head + 1) * HEAD_DIM)
            query = mixed[rows, lanes]
            key = mixed[:, PART + head * HEAD_DIM : PART + (head + 1) * HEAD_DIM]
            value = mixed[:, 2 * PART + head * HEAD_DIM : 2 * PART + (head + 1) * HEAD_DIM]
            scores = nt(query, key) * scale + bias
            weights = jnp.exp2(scores - jnp.max(scores, axis=1, keepdims=True))
            total = jnp.sum(weights, axis=1, keepdims=True)
            context_out[target, :, lanes] = (mm(weights.astype(BF), value) / total).astype(BF)

        @pl.when(step < 3)
        def _():
            context_copy(step).start()

    @pl.when(keeper)
    def _():
        context_in[pair] = context_out[z]

    @pl.when(helper)
    def _():
        context_copy(3).start()

    def context_wait(other):
        pltpu.make_async_remote_copy(
            src_ref=context_in.at[other],
            dst_ref=context_in.at[other],
            send_sem=context_send.at[3],
            recv_sem=context_recv.at[other],
            device_id={"dp": row, "seq": cross},
            device_id_type=MESH_ID,
        ).wait_recv()

    for offset in range(1, 4):
        context_wait(lax.rem(pair + offset, 4))

    @pl.when(helper)
    def _():
        context_wait(pair)

    output = jnp.zeros((256, D), F32)
    for part in range(4):
        start = 3 * PAIR + part * PART
        output += nt(context_in[part], wide[:, :, start : start + PART].reshape(D, PART))
    row_valid = valid_of(z, lax.broadcasted_iota(jnp.int32, (256, 1), 0), bounds(me))
    attended[...] = jnp.where(row_valid, output, 0.0).reshape(32, 8, D).astype(BF)
    own = rows_own[...].astype(F32).reshape(256, D)
    regrouped[...] = jnp.where(row_valid, own, 0.0).reshape(32, 8, D).astype(BF)

    halo.wait_send()
    ring.drain()
    wide_ring.drain()

    @pl.loop(1, 32)
    def _(offset):
        row_copy(offset).wait_send()

    @pl.when(keeper)
    def _():
        for index in range(4):
            own_to_partner(index).wait_send()
            cross_to_partner(index).wait_send()
            for place in range(4):
                to_sibling(part_of(rows_own, index), place, index).wait_send()

    @pl.when(helper)
    def _():
        for index in range(4):
            own_across(index).wait_send()
        context_copy(3).wait_send()

    @pl.loop(0, 3)
    def _(step):
        context_copy(step).wait_send()


def on_device(
    audio, starts, lengths, slots, conv1_weight, conv2_weight, proj_weight, qkv_weight, out_weight
):
    args = (
        audio, starts.reshape(1, 32), lengths.reshape(1, 32), slots.reshape(1, 32),
        conv1_weight, conv2_weight, proj_weight, qkv_weight, out_weight.T,
        *spectrum_tables(), *filter_tables(), patch_table(),
    )
    vmem = pl.BlockSpec(memory_space=pltpu.VMEM)
    dma = pltpu.SemaphoreType.DMA
    shape = jax.ShapeDtypeStruct((32, 8, D), BF)
    regrouped, attended = pl.pallas_call(
        whole_kernel,
        out_shape=(shape, shape),
        in_specs=[pl.BlockSpec(memory_space=pltpu.HBM)] * 14,
        out_specs=(vmem, vmem),
        scratch_shapes=[
            pltpu.VMEM((ROWS, EXT), F32),
            pltpu.VMEM((4, 288, N_FFT), BF),
            pltpu.VMEM((4, 288, N_FFT), BF),
            pltpu.VMEM((4, 288, 128), BF),
            pltpu.VMEM((544, 640), BF),
            pltpu.VMEM((8, 128, CH), BF),
            pltpu.VMEM((544, 41 * CH), BF),
            pltpu.VMEM((256, 20 * CH), BF),
            pltpu.VMEM((1, 32), jnp.int32),
            pltpu.VMEM((1, 32), jnp.int32),
            pltpu.VMEM((1, 32), jnp.int32),
            pltpu.VMEM((9, CH), BF),
            pltpu.VMEM((9 * CH, CH), BF),
            pltpu.VMEM((N_FFT, N_FFT), BF),
            pltpu.VMEM((N_FFT, N_FFT), BF),
            pltpu.VMEM((N_FFT // 2, 128), BF),
            pltpu.VMEM((N_FFT // 2, 128), BF),
            pltpu.VMEM((384, 640), BF),
            pltpu.VMEM((32, 160, D), BF),
            pltpu.VMEM((32, 32, WIDE), BF),
            pltpu.VMEM((32, 8, D), BF),
            pltpu.VMEM((32, 8, D), BF),
            pltpu.VMEM((4, 32, 8, D), BF),
            pltpu.VMEM((1024, 3 * PART), BF),
            pltpu.VMEM((4, 256, PART), BF),
            pltpu.VMEM((4, 256, PART), BF),
            dma((17,)), dma((2,)),
            dma((46,)), dma((46,)), dma((46,)), dma((46,)),
            dma((32,)), dma((32,)), dma((12,)), dma((12,)), dma((16,)), dma((16,)), dma((4,)), dma((4,)), dma((4,)),
        ],
        compiler_params=pltpu.CompilerParams(
            vmem_limit_bytes=VMEM_LIMIT, collective_id=0, has_side_effects=True
        ),
        name="whole",
    )(*args)
    return regrouped.reshape(1, 32, 1, 8, D), attended.reshape(1, 32, 1, 8, D)


def solution(mesh):
    in_specs = (
        P(None, ("dp", "seq")), P(), P(), P(), P(), P(), P("dp", None), P("dp", None), P(None, "dp"),
    )
    out_specs = (P("dp", None, "seq", None, None), P("dp", None, "seq", None, None))
    return jax.shard_map(
        on_device, mesh=mesh, in_specs=in_specs, out_specs=out_specs, check_vma=False
    )
```

```python
import functools
import math

import jax
import jax.numpy as jnp
import numpy as np
from jax import lax
from jax.experimental import pallas as pl
from jax.experimental.pallas import tpu as pltpu
from jax.sharding import PartitionSpec as P

D = 1024
HEADS = 8
HEAD_DIM = 128
MELS = 80
N_FFT = 512
HOP = 160
W = 8
CH = 256
ROWS = 32
RIM = 896
SPAN = 5120
EXT = 6272
BF = jnp.bfloat16
F32 = jnp.float32

SAMPLE_RATE = 16000.0
EPS_LOG = 1e-06
EPS_NORM = 1e-05
MASKED = -1e30
VMEM_LIMIT = 56 * 1024 * 1024


def mel_table(size, bands):
    count = size // 2 + 1
    highest = 2595.0 * math.log10(1.0 + SAMPLE_RATE / 1400.0)
    points = np.linspace(0.0, highest, bands + 2)
    edges = 700.0 * (10.0 ** (points / 2595.0) - 1.0)
    edges[0] = 0.0
    edges[-1] = SAMPLE_RATE / 2.0
    frequency = np.arange(count) * (SAMPLE_RATE / size)
    lower = edges[:-2][None, :]
    middle = edges[1:-1][None, :]
    upper = edges[2:][None, :]
    rising = (frequency[:, None] - lower) / (middle - lower)
    falling = (upper - frequency[:, None]) / (upper - middle)
    return np.maximum(0.0, np.minimum(rising, falling)).astype(np.float32)


def split_high_low(table):
    high = np.asarray(table, np.float64).astype(BF)
    low = (np.asarray(table, np.float64) - high.astype(np.float64)).astype(BF)
    return high, low


def spectrum_tables():
    sample = np.arange(N_FFT)
    angle = (sample[:, None] * np.arange(N_FFT // 2)[None, :] % N_FFT) * (2.0 * math.pi / N_FFT)
    window = 0.5 - 0.5 * np.cos(sample * (2.0 * math.pi / N_FFT))
    return split_high_low(np.concatenate([np.cos(angle), np.sin(angle)], axis=1) * window[:, None])


def filter_tables():
    padded = np.zeros((N_FFT // 2, 128), np.float64)
    padded[:, :MELS] = mel_table(N_FFT, MELS)[: N_FFT // 2]
    return split_high_low(padded)


def patch_table():
    table = np.zeros((3 * 128, 40 * 16), np.float32)
    for g in range(40):
        for a in range(3):
            for b in range(3):
                band = 2 * g - 1 + b
                if 0 <= band < MELS:
                    table[a * 128 + band, g * 16 + 3 * a + b] = 1.0
    return table.astype(BF)


def mm(a, b):
    return jnp.dot(a, b, preferred_element_type=F32)


def halves(value):
    high = value.astype(BF)
    return high, (value - high.astype(F32)).astype(BF)


def frame_step(p, ext, frames_high, frames_low):
    window = ext[:, pl.ds(pl.multiple_of(p * 640, 128), 1152)]
    rows = pl.ds(pl.multiple_of(p * 32, 32), 32)
    for q in range(4):
        start = 64 + HOP * q
        base, offset = start // 128 * 128, start % 128
        if offset:
            piece = pltpu.roll(window[:, base : base + 640], 640 - offset, 1)[:, :N_FFT]
        else:
            piece = window[:, base : base + N_FFT]
        high, low = halves(piece)
        frames_high[q, rows, :] = high
        frames_low[q, rows, :] = low


def mel_of(high, low, dft_high, dft_low, mel_high, mel_low):
    spectrum = mm(high, dft_high[...]) + mm(high, dft_low[...]) + mm(low, dft_high[...])
    half = N_FFT // 2
    power = spectrum[:, :half] * spectrum[:, :half] + spectrum[:, half:] * spectrum[:, half:]
    high, low = halves(power)
    mel = mm(high, mel_high[...]) + mm(high, mel_low[...]) + mm(low, mel_high[...])
    return jnp.log(mel + EPS_LOG).astype(BF)


def late_patches(log_mel, patch_map, patches):
    even = jnp.concatenate([log_mel[0, 64:], log_mel[1, 64:], log_mel[2, 64:]], axis=1)
    patches[:224, :] = mm(even, patch_map[...]).astype(BF)
    odd = jnp.concatenate([log_mel[2, 64:256], log_mel[3, 64:256], log_mel[0, 96:]], axis=1)
    patches[224:416, :] = mm(odd, patch_map[...]).astype(BF)


def early_patches(log_mel, patch_map, patches):
    even = jnp.concatenate([log_mel[0, :64], log_mel[1, :64], log_mel[2, :64]], axis=1)
    odd = jnp.concatenate([log_mel[2, :64], log_mel[3, :64], log_mel[0, 32:96]], axis=1)
    patches[416:, :] = mm(jnp.concatenate([even, odd], axis=0), patch_map[...]).astype(BF)


def spread_taps(conv1, taps):
    taps[...] = jnp.zeros_like(taps)
    for j in range(8):
        taps[j, 16 * j : 16 * j + 9, :] = conv1[...]


def conv1_step(block, j, late, patches, taps, first):
    lanes = slice(block * 128, block * 128 + 128)
    target = pl.ds(pl.multiple_of((block * 8 + j + 1) * CH, CH), CH)
    rows, count = (slice(0, 416), 224) if late else (slice(416, 544), 64)
    result = jnp.maximum(mm(patches[rows, lanes], taps[j]), 0.0).astype(BF)
    first[slice(64, 288) if late else slice(0, 64), target] = result[:count]
    first[slice(352, 544) if late else slice(288, 352), target] = result[count:]


def conv2_step(h, first, conv2, features):
    lanes = pl.ds(pl.multiple_of(h * 512, 512), 768)
    total = mm(first[0:256, lanes], conv2[0:768, :])
    total += mm(first[288:544, lanes], conv2[768:1536, :])
    total += mm(first[32:288, lanes], conv2[1536:2304, :])
    features[:, pl.ds(pl.multiple_of(h * CH, CH), CH)] = jnp.maximum(total, 0.0).astype(BF)


def to_rows(projected, slots_wide):
    out_index = lax.broadcasted_iota(jnp.int32, (256, 256), 0)
    in_index = lax.broadcasted_iota(jnp.int32, (256, 256), 1)
    same_row = slots_wide == out_index // 8
    same_frame = in_index // 32 == out_index % 8
    routing = jnp.where(same_row & same_frame, 1.0, 0.0).astype(BF)
    return mm(routing, projected).astype(BF)

MESH_ID = pl.DeviceIdType.MESH
PART = 2 * HEAD_DIM
PAIR = 2 * PART
WIDE = 3 * PAIR + D


class Ring:
    def __init__(self, source, buffer, send, recv, place):
        self.source, self.buffer, self.send, self.recv = source, buffer, send, recv
        self.core, self.a, self.b, self.sa, self.sb, self.sibling = place
        self.count = 0
        self.sent = []
        self.rows = buffer.shape[1]

    def shard(self, da, db):
        return lax.rem(self.a + da + 4, 4) * self.sa + lax.rem(self.b + db + 4, 4) * self.sb + self.core

    def part(self, index, half):
        if half is None:
            return self.buffer.at[index]
        step = self.rows // 2
        return self.buffer.at[index, pl.ds(half * step, step)]

    def origin(self, half):
        step = self.rows // 2
        return self.source if half is None else self.source.at[pl.ds(half * step, step)]

    def put(self, index, half, target, slot, own=False):
        copy = pltpu.make_async_remote_copy(
            src_ref=self.origin(half) if own else self.part(index, half),
            dst_ref=self.part(index, half),
            send_sem=self.send.at[self.count],
            recv_sem=self.recv.at[slot],
            device_id={"dp": target},
            device_id_type=MESH_ID,
        )
        copy.start()
        self.count += 1
        self.sent.append(copy)

    def got(self, index, half, slot):
        pltpu.make_async_remote_copy(
            src_ref=self.part(index, half),
            dst_ref=self.part(index, half),
            send_sem=self.send.at[0],
            recv_sem=self.recv.at[slot],
            device_id={"dp": self.sibling},
            device_id_type=MESH_ID,
        ).wait_recv()

    def to_both(self, index, above, below, base, line, own=False):
        for target, half, slot in ((above, 0, 0), (below, 1, 1)):
            self.put(index, half, target, base + slot, own)
            self.put(index, 1 - half, target, 36 + 2 * line + slot, own)

    def pass_both(self, lower, upper, above, below, base):
        self.got(lower, 0, base)
        self.put(lower, 0, above, base + 2)
        self.got(upper, 1, base + 1)
        self.put(upper, 1, below, base + 3)

    def to_b(self, da, own=False):
        index = self.shard(da, 0)
        self.to_both(index, self.shard(0, 1), self.shard(0, -1), 4 + 4 * (da + 1), da + 2, own)
        self.put(index, None, self.sibling, 20 + 4 * (da + 1) + 1, own)

    def begin(self):
        self.to_both(self.shard(0, 0), self.shard(1, 0), self.shard(-1, 0), 0, 0, True)

    def pass_a(self):
        self.pass_both(self.shard(-1, 0), self.shard(1, 0), self.shard(1, 0), self.shard(-1, 0), 0)
        self.got(self.shard(-1, 0), 1, 36)
        self.to_b(-1)
        self.got(self.shard(1, 0), 0, 37)
        self.to_b(1)

    def end_a(self):
        index = self.shard(2, 0)
        self.got(index, 0, 2)
        self.got(index, 1, 3)
        self.to_b(2)

    def pass_b(self, da):
        lower, upper, slot = self.shard(da, -1), self.shard(da, 1), 36 + 2 * (da + 2)
        self.pass_both(lower, upper, self.shard(0, 1), self.shard(0, -1), 4 + 4 * (da + 1))
        self.got(lower, 1, slot)
        self.put(lower, None, self.sibling, 20 + 4 * (da + 1))
        self.got(upper, 0, slot + 1)
        self.put(upper, None, self.sibling, 20 + 4 * (da + 1) + 2)

    def end_b(self, da):
        base = 4 + 4 * (da + 1)
        index = self.shard(da, 2)
        self.got(index, 0, base + 2)
        self.got(index, 1, base + 3)
        self.put(index, None, self.sibling, 20 + 4 * (da + 1) + 3)

    def from_sibling(self):
        for slot in range(16):
            self.got(self.sibling, None, 20 + slot)

    def drain(self):
        for copy in self.sent:
            copy.wait_send()


def normalised(values):
    mean = jnp.mean(values, axis=-1, keepdims=True)
    centered = values - mean
    variance = jnp.mean(centered * centered, axis=-1, keepdims=True)
    return (centered * lax.rsqrt(variance + EPS_NORM)).astype(BF)


def nt(a, b):
    return lax.dot_general(a, b, (((1,), (1,)), ((), ())), preferred_element_type=F32)


def whole_kernel(
    audio_in, starts_in, lengths_in, slots_in, conv1_in, conv2_in, proj_in, qkv_in, out_in,
    dft_high_in, dft_low_in, mel_high_in, mel_low_in, patch_in,
    regrouped, attended,
    ext, frames_high, frames_low, log_mel, patches, taps, first, features,
    starts, lengths, slots, conv1, conv2, dft_high, dft_low, mel_high, mel_low, patch_map,
    proj, wide, rows_out, rows_own, rows_all, normed, mixed, context_out, context_in,
    local_sem, halo_sem, proj_send, proj_recv, wide_send, wide_recv,
    row_send, row_recv, z_send, z_recv, pass_send, pass_recv, keep_sem, context_send, context_recv,
):
    me, z = lax.axis_index("dp"), lax.axis_index("seq")
    x, y, core = me // 8, me // 2 % 4, me % 2
    sibling = me + 1 - 2 * core
    a, b = x * (1 - core) + y * core, y * (1 - core) + x * core
    sa, sb = 8 * (1 - core) + 2 * core, 2 * (1 - core) + 8 * core
    place = (core, a, b, sa, sb, sibling)
    line = me * 4 + z
    after, before = lax.rem(line + 1, 128), lax.rem(line + 127, 128)
    keeper = core == z // 2
    helper = core != z // 2
    row = me - core + z // 2
    partner, cross = z + 1 - 2 * (z % 2), 3 - z
    beyond = 3 - partner
    pair = z % 2 * 2 + core

    def local(source, target, index):
        copy = pltpu.make_async_copy(source, target, local_sem.at[index])
        copy.start()
        return copy

    loads = [
        local(source, target, index)
        for index, (source, target) in enumerate(
            (
                (audio_in, ext.at[:, pl.ds(RIM, SPAN)]),
                (dft_high_in, dft_high),
                (dft_low_in, dft_low),
                (mel_high_in, mel_high),
                (mel_low_in, mel_low),
                (patch_in, patch_map),
                (conv2_in, conv2),
                (proj_in, proj.at[me]),
            )
        )
    ]
    parts = [local(out_in, wide.at[me, :, pl.ds(3 * PAIR, D)], 12)] + [
        local(
            qkv_in.at[:, pl.ds(pl.multiple_of(third * D + z % 2 * PAIR, 128), PAIR)],
            wide.at[me, :, pl.ds(third * PAIR, PAIR)],
            8 + third,
        )
        for third in range(3)
    ]

    small = [
        local(source, target, 13 + index)
        for index, (source, target) in enumerate(
            ((conv1_in, conv1), (starts_in, starts), (lengths_in, lengths), (slots_in, slots))
        )
    ]
    barrier = pltpu.get_barrier_semaphore()

    @pl.loop(1, 32)
    def _(offset):
        pl.semaphore_signal(
            barrier, inc=1, device_id={"dp": lax.rem(me + offset, 32)}, device_id_type=MESH_ID
        )

    for offset in range(1, 4):
        pl.semaphore_signal(
            barrier, inc=1, device_id={"seq": lax.rem(z + offset, 4)}, device_id_type=MESH_ID
        )
    for offset in range(1, 4):
        pl.semaphore_signal(
            barrier,
            inc=1,
            device_id={"dp": sibling, "seq": lax.rem(z + offset, 4)},
            device_id_type=MESH_ID,
        )
    for other in (after, before):
        pl.semaphore_signal(
            barrier, inc=1, device_id={"dp": other // 4, "seq": other % 4}, device_id_type=MESH_ID
        )
    for load in small:
        load.wait()
    spread_taps(conv1, taps)
    first[:, :CH] = jnp.zeros((544, CH), BF)
    ext[:, RIM + SPAN :] = jnp.zeros((ROWS, EXT - RIM - SPAN), F32)
    pl.semaphore_wait(barrier, 39)
    halo = pltpu.make_async_remote_copy(
        src_ref=audio_in.at[:, pl.ds(SPAN - RIM, RIM)],
        dst_ref=ext.at[:, pl.ds(0, RIM)],
        send_sem=halo_sem.at[0],
        recv_sem=halo_sem.at[1],
        device_id={"dp": after // 4, "seq": after % 4},
        device_id_type=MESH_ID,
    )
    halo.start()
    ring = Ring(proj_in, proj, proj_send, proj_recv, place)
    ring.begin()

    loads[0].wait()

    @pl.loop(2, 9)
    def _(p):
        frame_step(p, ext, frames_high, frames_low)

    for load in loads[1:5]:
        load.wait()
    tables = (dft_high, dft_low, mel_high, mel_low)

    for q in range(4):
        if q == 1:
            ring.to_b(0, True)
        log_mel[q, 64:, :] = mel_of(frames_high[q, 64:, :], frames_low[q, 64:, :], *tables)

    loads[5].wait()
    late_patches(log_mel, patch_map, patches)

    def conv1_run(late):
        @pl.loop(0, 8)
        def _(j):
            for block in range(5):
                conv1_step(block, j, late, patches, taps, first)

    def conv2_run(low, high):
        @pl.loop(low, high)
        def _(group):
            for i in range(4):
                conv2_step(group * 4 + i, first, conv2, features)

    ring.pass_a()
    conv1_run(True)
    ring.pass_b(0)
    halo.wait_recv()

    @pl.when(line == 0)
    def _():
        ext[:, :RIM] = jnp.zeros((ROWS, RIM), F32)

    @pl.loop(0, 2)
    def _(p):
        frame_step(p, ext, frames_high, frames_low)

    early = mel_of(
        frames_high[:, :64, :].reshape(256, N_FFT), frames_low[:, :64, :].reshape(256, N_FFT), *tables
    )
    for q in range(4):
        log_mel[q, :64, :] = early[64 * q : 64 * q + 64]
    early_patches(log_mel, patch_map, patches)
    conv1_run(False)
    ring.end_a()
    loads[6].wait()
    conv2_run(0, 2)
    ring.pass_b(-1)
    ring.pass_b(1)
    ring.end_b(0)
    conv2_run(2, 4)
    ring.pass_b(2)
    conv2_run(4, 5)
    ring.end_b(-1)
    ring.end_b(1)
    ring.end_b(2)
    for part in parts:
        part.wait()
    wide_ring = Ring(wide.at[me], wide, wide_send, wide_recv, place)
    wide_ring.begin()
    wide_ring.to_b(0, True)
    tile_map = jnp.where(
        lax.broadcasted_iota(jnp.int32, (32, 256), 1) % 32 == lax.broadcasted_iota(jnp.int32, (32, 256), 0),
        1.0, 0.0,
    ).astype(BF)
    slot_values = jnp.broadcast_to(slots[...].astype(F32), (8, 32)).astype(BF)
    slots_wide = mm(slot_values, tile_map)[0:1, :].astype(jnp.int32)
    out_index = lax.broadcasted_iota(jnp.int32, (256, 256), 0)
    in_index = lax.broadcasted_iota(jnp.int32, (256, 256), 1)
    routing = jnp.where((slots_wide == out_index // 8) & (in_index // 32 == out_index % 8), 1.0, 0.0).astype(BF)
    ring.from_sibling()
    loads[7].wait()

    projected = mm(features[...], proj[...].reshape(20 * CH, D)).astype(BF)
    rows_out[...] = mm(routing, projected).reshape(32, 8, D).astype(BF)

    def row_copy(offset):
        target = lax.rem(x + 4 - offset // 8, 4) * 8 + lax.rem(me + offset, 8)
        return pltpu.make_async_remote_copy(
            src_ref=rows_out.at[target],
            dst_ref=rows_own.at[me],
            send_sem=row_send.at[offset],
            recv_sem=row_recv.at[me],
            device_id={"dp": target},
            device_id_type=MESH_ID,
        )

    @pl.loop(1, 32)
    def _(offset):
        row_copy(offset).start()

    mine = local(rows_out.at[me], rows_own.at[me], 11)
    wide_ring.pass_a()
    wide_ring.pass_b(0)
    mine.wait()

    chunks = [lax.rem(x + index, 4) for index in range(4)]
    origins = (z, partner, cross, beyond)

    def part_of(buffer, index):
        return buffer.at[pl.ds(pl.multiple_of(chunks[index] * 8, 8), 8)]

    def row_part(origin, index):
        return rows_all.at[origin, pl.ds(pl.multiple_of(chunks[index] * 8, 8), 8)]

    def to_plane(source, origin, index, base, plane):
        return pltpu.make_async_remote_copy(
            src_ref=source,
            dst_ref=row_part(origin, index),
            send_sem=z_send.at[base + index],
            recv_sem=z_recv.at[base + index],
            device_id={"seq": plane},
            device_id_type=MESH_ID,
        )

    def to_sibling(source, place, index):
        return pltpu.make_async_remote_copy(
            src_ref=source,
            dst_ref=row_part(origins[place], index),
            send_sem=pass_send.at[4 * place + index],
            recv_sem=pass_recv.at[4 * place + index],
            device_id={"dp": sibling},
            device_id_type=MESH_ID,
        )

    def arrived(place, index, base):
        block = row_part(origins[place], index)
        to_plane(block, origins[place], index, base, partner).wait_recv()
        return block

    def own_to_partner(index):
        return to_plane(part_of(rows_own, index), z, index, 0, partner)

    def own_across(index):
        return to_plane(part_of(rows_own, index), z, index, 4, cross)

    def cross_to_partner(index):
        return to_plane(row_part(cross, index), cross, index, 8, partner)

    def own_copy(index):
        return pltpu.make_async_copy(part_of(rows_own, index), row_part(z, index), keep_sem.at[index])

    for index in range(4):
        @pl.loop(0, 8)
        def _(step):
            source = chunks[index] * 8 + step

            @pl.when(source != me)
            def _():
                block = rows_own.at[source]
                pltpu.make_async_remote_copy(
                    src_ref=block,
                    dst_ref=block,
                    send_sem=row_send.at[0],
                    recv_sem=row_recv.at[source],
                    device_id={"dp": sibling},
                    device_id_type=MESH_ID,
                ).wait_recv()

        @pl.when(keeper)
        def _():
            own_to_partner(index).start()
            to_sibling(part_of(rows_own, index), 0, index).start()
            own_copy(index).start()

        @pl.when(helper)
        def _():
            own_across(index).start()

    def pass_cross(index):
        @pl.when(keeper)
        def _():
            block = arrived(2, index, 4)
            cross_to_partner(index).start()
            to_sibling(block, 2, index).start()

    def pass_partner(index):
        @pl.when(keeper)
        def _():
            to_sibling(arrived(1, index, 0), 1, index).start()

    def pass_beyond(index):
        @pl.when(keeper)
        def _():
            to_sibling(arrived(3, index, 8), 3, index).start()

    def helped(place):
        @pl.when(helper)
        def _():
            for index in range(4):
                to_sibling(row_part(origins[place], index), place, index).wait_recv()

    def norm(origin):
        rows = pl.ds(pl.multiple_of(origin * 256, 256), 256)
        normed[rows, :] = normalised(rows_all[origin].astype(F32).reshape(256, D))

    pass_cross(0)
    wide_ring.end_a()
    pass_cross(1)
    pass_partner(0)
    wide_ring.end_b(0)
    pass_cross(2)
    pass_partner(1)
    wide_ring.pass_b(-1)
    pass_cross(3)
    pass_partner(2)
    wide_ring.pass_b(1)
    pass_partner(3)

    @pl.when(keeper)
    def _():
        for index in range(4):
            own_copy(index).wait()

    helped(0)
    norm(z)
    wide_ring.pass_b(2)
    pass_beyond(0)
    wide_ring.end_b(-1)
    wide_ring.end_b(1)
    pass_beyond(1)
    helped(1)
    norm(partner)
    pass_beyond(2)
    wide_ring.end_b(2)
    helped(2)
    norm(cross)
    pass_beyond(3)
    wide_ring.from_sibling()
    helped(3)
    norm(beyond)
    for third in range(3):
        lanes = pl.ds(pl.multiple_of(third * PAIR + core * PART, 128), PART)
        result = mm(normed[...], wide[:, :, lanes].reshape(D, PART))
        mixed[:, third * PART : third * PART + PART] = result.astype(BF)

    def bounds(owner):
        chosen = slots[...] == owner
        begin = jnp.sum(jnp.where(chosen, starts[...].astype(F32), 0.0), axis=1, keepdims=True)
        span = jnp.sum(jnp.where(chosen, lengths[...].astype(F32), 0.0), axis=1, keepdims=True)
        return begin, begin + span

    def valid_of(owner, index, limits):
        frame = (index // 8 * 4 + owner) * 8 + index % 8
        sample = (frame * (4 * HOP)).astype(F32)
        return (sample >= limits[0]) & (sample < limits[1])

    key_index = lax.broadcasted_iota(jnp.int32, (1, 1024), 1)
    bias = jnp.where(valid_of(key_index // 256, key_index % 256, bounds(row)), 0.0, MASKED)
    scale = HEAD_DIM ** (-0.5) * math.log2(math.e)

    def context_target(step):
        return lax.rem(z + 2 + step - step // 2 * (2 * step - 1), 4)

    def context_copy(step):
        target = context_target(step)
        return pltpu.make_async_remote_copy(
            src_ref=context_out.at[target],
            dst_ref=context_in.at[pair],
            send_sem=context_send.at[step],
            recv_sem=context_recv.at[pair],
            device_id={"dp": row, "seq": target},
            device_id_type=MESH_ID,
        )

    @pl.loop(0, 4)
    def _(step):
        target = context_target(step)
        rows = pl.ds(pl.multiple_of(target * 256, 256), 256)
        for head in range(2):
            lanes = slice(head * HEAD_DIM, (head + 1) * HEAD_DIM)
            query = mixed[rows, lanes]
            key = mixed[:, PART + head * HEAD_DIM : PART + (head + 1) * HEAD_DIM]
            value = mixed[:, 2 * PART + head * HEAD_DIM : 2 * PART + (head + 1) * HEAD_DIM]
            scores = nt(query, key) * scale + bias
            weights = jnp.exp2(scores - jnp.max(scores, axis=1, keepdims=True))
            total = jnp.sum(weights, axis=1, keepdims=True)
            context_out[target, :, lanes] = (mm(weights.astype(BF), value) / total).astype(BF)

        @pl.when(step < 3)
        def _():
            context_copy(step).start()

    @pl.when(keeper)
    def _():
        context_in[pair] = context_out[z]

    @pl.when(helper)
    def _():
        context_copy(3).start()

    def context_wait(other):
        pltpu.make_async_remote_copy(
            src_ref=context_in.at[other],
            dst_ref=context_in.at[other],
            send_sem=context_send.at[3],
            recv_sem=context_recv.at[other],
            device_id={"dp": row, "seq": cross},
            device_id_type=MESH_ID,
        ).wait_recv()

    for offset in range(1, 4):
        context_wait(lax.rem(pair + offset, 4))

    @pl.when(helper)
    def _():
        context_wait(pair)

    output = jnp.zeros((256, D), F32)
    for part in range(4):
        start = 3 * PAIR + part * PART
        output += nt(context_in[part], wide[:, :, start : start + PART].reshape(D, PART))
    row_valid = valid_of(z, lax.broadcasted_iota(jnp.int32, (256, 1), 0), bounds(me))
    attended[...] = jnp.where(row_valid, output, 0.0).reshape(32, 8, D).astype(BF)
    own = rows_own[...].astype(F32).reshape(256, D)
    regrouped[...] = jnp.where(row_valid, own, 0.0).reshape(32, 8, D).astype(BF)

    halo.wait_send()
    ring.drain()
    wide_ring.drain()

    @pl.loop(1, 32)
    def _(offset):
        row_copy(offset).wait_send()

    @pl.when(keeper)
    def _():
        for index in range(4):
            own_to_partner(index).wait_send()
            cross_to_partner(index).wait_send()
            for place in range(4):
                to_sibling(part_of(rows_own, index), place, index).wait_send()

    @pl.when(helper)
    def _():
        for index in range(4):
            own_across(index).wait_send()
        context_copy(3).wait_send()

    @pl.loop(0, 3)
    def _(step):
        context_copy(step).wait_send()


def on_device(
    audio, starts, lengths, slots, conv1_weight, conv2_weight, proj_weight, qkv_weight, out_weight
):
    args = (
        audio, starts.reshape(1, 32), lengths.reshape(1, 32), slots.reshape(1, 32),
        conv1_weight, conv2_weight, proj_weight, qkv_weight, out_weight.T,
        *spectrum_tables(), *filter_tables(), patch_table(),
    )
    vmem = pl.BlockSpec(memory_space=pltpu.VMEM)
    dma = pltpu.SemaphoreType.DMA
    shape = jax.ShapeDtypeStruct((32, 8, D), BF)
    regrouped, attended = pl.pallas_call(
        whole_kernel,
        out_shape=(shape, shape),
        in_specs=[pl.BlockSpec(memory_space=pltpu.HBM)] * 14,
        out_specs=(vmem, vmem),
        scratch_shapes=[
            pltpu.VMEM((ROWS, EXT), F32),
            pltpu.VMEM((4, 288, N_FFT), BF),
            pltpu.VMEM((4, 288, N_FFT), BF),
            pltpu.VMEM((4, 288, 128), BF),
            pltpu.VMEM((544, 640), BF),
            pltpu.VMEM((8, 128, CH), BF),
            pltpu.VMEM((544, 41 * CH), BF),
            pltpu.VMEM((256, 20 * CH), BF),
            pltpu.VMEM((1, 32), jnp.int32),
            pltpu.VMEM((1, 32), jnp.int32),
            pltpu.VMEM((1, 32), jnp.int32),
            pltpu.VMEM((9, CH), BF),
            pltpu.VMEM((9 * CH, CH), BF),
            pltpu.VMEM((N_FFT, N_FFT), BF),
            pltpu.VMEM((N_FFT, N_FFT), BF),
            pltpu.VMEM((N_FFT // 2, 128), BF),
            pltpu.VMEM((N_FFT // 2, 128), BF),
            pltpu.VMEM((384, 640), BF),
            pltpu.VMEM((32, 160, D), BF),
            pltpu.VMEM((32, 32, WIDE), BF),
            pltpu.VMEM((32, 8, D), BF),
            pltpu.VMEM((32, 8, D), BF),
            pltpu.VMEM((4, 32, 8, D), BF),
            pltpu.VMEM((1024, D), BF),
            pltpu.VMEM((1024, 3 * PART), BF),
            pltpu.VMEM((4, 256, PART), BF),
            pltpu.VMEM((4, 256, PART), BF),
            dma((17,)), dma((2,)),
            dma((46,)), dma((46,)), dma((46,)), dma((46,)),
            dma((32,)), dma((32,)), dma((12,)), dma((12,)), dma((16,)), dma((16,)), dma((4,)), dma((4,)), dma((4,)),
        ],
        compiler_params=pltpu.CompilerParams(
            vmem_limit_bytes=VMEM_LIMIT, collective_id=0, has_side_effects=True
        ),
        name="whole",
    )(*args)
    return regrouped.reshape(1, 32, 1, 8, D), attended.reshape(1, 32, 1, 8, D)


def solution(mesh):
    in_specs = (
        P(None, ("dp", "seq")), P(), P(), P(), P(), P(), P("dp", None), P("dp", None), P(None, "dp"),
    )
    out_specs = (P("dp", None, "seq", None, None), P("dp", None, "seq", None, None))
    return jax.shard_map(
        on_device, mesh=mesh, in_specs=in_specs, out_specs=out_specs, check_vma=False
    )
```

```python
import functools
import math

import jax
import jax.numpy as jnp
import numpy as np
from jax import lax
from jax.experimental import pallas as pl
from jax.experimental.pallas import tpu as pltpu
from jax.sharding import PartitionSpec as P

D = 1024
HEADS = 8
HEAD_DIM = 128
MELS = 80
N_FFT = 512
HOP = 160
W = 8
CH = 256
ROWS = 32
RIM = 896
SPAN = 5120
EXT = 6272
BF = jnp.bfloat16
F32 = jnp.float32

SAMPLE_RATE = 16000.0
EPS_LOG = 1e-06
EPS_NORM = 1e-05
MASKED = -1e30
VMEM_LIMIT = 56 * 1024 * 1024


def mel_table(size, bands):
    count = size // 2 + 1
    highest = 2595.0 * math.log10(1.0 + SAMPLE_RATE / 1400.0)
    points = np.linspace(0.0, highest, bands + 2)
    edges = 700.0 * (10.0 ** (points / 2595.0) - 1.0)
    edges[0] = 0.0
    edges[-1] = SAMPLE_RATE / 2.0
    frequency = np.arange(count) * (SAMPLE_RATE / size)
    lower = edges[:-2][None, :]
    middle = edges[1:-1][None, :]
    upper = edges[2:][None, :]
    rising = (frequency[:, None] - lower) / (middle - lower)
    falling = (upper - frequency[:, None]) / (upper - middle)
    return np.maximum(0.0, np.minimum(rising, falling)).astype(np.float32)


def split_high_low(table):
    high = np.asarray(table, np.float64).astype(BF)
    low = (np.asarray(table, np.float64) - high.astype(np.float64)).astype(BF)
    return high, low


def spectrum_tables():
    sample = np.arange(N_FFT)
    angle = (sample[:, None] * np.arange(N_FFT // 2)[None, :] % N_FFT) * (2.0 * math.pi / N_FFT)
    window = 0.5 - 0.5 * np.cos(sample * (2.0 * math.pi / N_FFT))
    return split_high_low(np.concatenate([np.cos(angle), np.sin(angle)], axis=1) * window[:, None])


def filter_tables():
    padded = np.zeros((N_FFT // 2, 128), np.float64)
    padded[:, :MELS] = mel_table(N_FFT, MELS)[: N_FFT // 2]
    return split_high_low(padded)


def patch_table():
    table = np.zeros((3 * 128, 40 * 16), np.float32)
    for g in range(40):
        for a in range(3):
            for b in range(3):
                band = 2 * g - 1 + b
                if 0 <= band < MELS:
                    table[a * 128 + band, g * 16 + 3 * a + b] = 1.0
    return table.astype(BF)


def mm(a, b):
    return jnp.dot(a, b, preferred_element_type=F32)


def halves(value):
    high = value.astype(BF)
    return high, (value - high.astype(F32)).astype(BF)


def frame_step(p, ext, frames_high, frames_low):
    window = ext[:, pl.ds(pl.multiple_of(p * 640, 128), 1152)]
    rows = pl.ds(pl.multiple_of(p * 32, 32), 32)
    for q in range(4):
        start = 64 + HOP * q
        base, offset = start // 128 * 128, start % 128
        if offset:
            piece = pltpu.roll(window[:, base : base + 640], 640 - offset, 1)[:, :N_FFT]
        else:
            piece = window[:, base : base + N_FFT]
        high, low = halves(piece)
        frames_high[q, rows, :] = high
        frames_low[q, rows, :] = low


def mel_of(high, low, dft_high, dft_low, mel_high, mel_low):
    spectrum = mm(high, dft_high[...]) + mm(high, dft_low[...]) + mm(low, dft_high[...])
    half = N_FFT // 2
    power = spectrum[:, :half] * spectrum[:, :half] + spectrum[:, half:] * spectrum[:, half:]
    high, low = halves(power)
    mel = mm(high, mel_high[...]) + mm(high, mel_low[...]) + mm(low, mel_high[...])
    return jnp.log(mel + EPS_LOG).astype(BF)


def late_patches(log_mel, patch_map, patches):
    even = jnp.concatenate([log_mel[0, 64:], log_mel[1, 64:], log_mel[2, 64:]], axis=1)
    patches[:224, :] = mm(even, patch_map[...]).astype(BF)
    odd = jnp.concatenate([log_mel[2, 64:256], log_mel[3, 64:256], log_mel[0, 96:]], axis=1)
    patches[224:416, :] = mm(odd, patch_map[...]).astype(BF)


def early_patches(log_mel, patch_map, patches):
    even = jnp.concatenate([log_mel[0, :64], log_mel[1, :64], log_mel[2, :64]], axis=1)
    odd = jnp.concatenate([log_mel[2, :64], log_mel[3, :64], log_mel[0, 32:96]], axis=1)
    patches[416:, :] = mm(jnp.concatenate([even, odd], axis=0), patch_map[...]).astype(BF)


def spread_taps(conv1, taps):
    taps[...] = jnp.zeros_like(taps)
    for j in range(8):
        taps[j, 16 * j : 16 * j + 9, :] = conv1[...]


def conv1_step(block, j, late, patches, taps, first):
    lanes = slice(block * 128, block * 128 + 128)
    target = pl.ds(pl.multiple_of((block * 8 + j + 1) * CH, CH), CH)
    rows, count = (slice(0, 416), 224) if late else (slice(416, 544), 64)
    result = jnp.maximum(mm(patches[rows, lanes], taps[j]), 0.0).astype(BF)
    first[slice(64, 288) if late else slice(0, 64), target] = result[:count]
    first[slice(352, 544) if late else slice(288, 352), target] = result[count:]


def conv2_step(h, first, conv2, features):
    lanes = pl.ds(pl.multiple_of(h * 512, 512), 768)
    total = mm(first[0:256, lanes], conv2[0:768, :])
    total += mm(first[288:544, lanes], conv2[768:1536, :])
    total += mm(first[32:288, lanes], conv2[1536:2304, :])
    features[:, pl.ds(pl.multiple_of(h * CH, CH), CH)] = jnp.maximum(total, 0.0).astype(BF)


def to_rows(projected, slots_wide):
    out_index = lax.broadcasted_iota(jnp.int32, (256, 256), 0)
    in_index = lax.broadcasted_iota(jnp.int32, (256, 256), 1)
    same_row = slots_wide == out_index // 8
    same_frame = in_index // 32 == out_index % 8
    routing = jnp.where(same_row & same_frame, 1.0, 0.0).astype(BF)
    return mm(routing, projected).astype(BF)

MESH_ID = pl.DeviceIdType.MESH
PART = 2 * HEAD_DIM
PAIR = 2 * PART
WIDE = 3 * PAIR + D


class Ring:
    def __init__(self, source, buffer, send, recv, place):
        self.source, self.buffer, self.send, self.recv = source, buffer, send, recv
        self.core, self.a, self.b, self.sa, self.sb, self.sibling = place
        self.count = 0
        self.sent = []
        self.rows = buffer.shape[1]

    def shard(self, da, db):
        return lax.rem(self.a + da + 4, 4) * self.sa + lax.rem(self.b + db + 4, 4) * self.sb + self.core

    def part(self, index, half):
        if half is None:
            return self.buffer.at[index]
        step = self.rows // 2
        return self.buffer.at[index, pl.ds(half * step, step)]

    def origin(self, half):
        step = self.rows // 2
        return self.source if half is None else self.source.at[pl.ds(half * step, step)]

    def put(self, index, half, target, slot, own=False):
        copy = pltpu.make_async_remote_copy(
            src_ref=self.origin(half) if own else self.part(index, half),
            dst_ref=self.part(index, half),
            send_sem=self.send.at[self.count],
            recv_sem=self.recv.at[slot],
            device_id={"dp": target},
            device_id_type=MESH_ID,
        )
        copy.start()
        self.count += 1
        self.sent.append(copy)

    def got(self, index, half, slot):
        pltpu.make_async_remote_copy(
            src_ref=self.part(index, half),
            dst_ref=self.part(index, half),
            send_sem=self.send.at[0],
            recv_sem=self.recv.at[slot],
            device_id={"dp": self.sibling},
            device_id_type=MESH_ID,
        ).wait_recv()

    def to_both(self, index, above, below, base, line, own=False):
        for target, half, slot in ((above, 0, 0), (below, 1, 1)):
            self.put(index, half, target, base + slot, own)
            self.put(index, 1 - half, target, 36 + 2 * line + slot, own)

    def pass_both(self, lower, upper, above, below, base):
        self.got(lower, 0, base)
        self.put(lower, 0, above, base + 2)
        self.got(upper, 1, base + 1)
        self.put(upper, 1, below, base + 3)

    def to_b(self, da, own=False):
        index = self.shard(da, 0)
        self.to_both(index, self.shard(0, 1), self.shard(0, -1), 4 + 4 * (da + 1), da + 2, own)
        self.put(index, None, self.sibling, 20 + 4 * (da + 1) + 1, own)

    def begin(self):
        self.to_both(self.shard(0, 0), self.shard(1, 0), self.shard(-1, 0), 0, 0, True)

    def pass_a(self):
        self.pass_both(self.shard(-1, 0), self.shard(1, 0), self.shard(1, 0), self.shard(-1, 0), 0)
        self.got(self.shard(-1, 0), 1, 36)
        self.to_b(-1)
        self.got(self.shard(1, 0), 0, 37)
        self.to_b(1)

    def end_a(self):
        index = self.shard(2, 0)
        self.got(index, 0, 2)
        self.got(index, 1, 3)
        self.to_b(2)

    def pass_b(self, da):
        lower, upper, slot = self.shard(da, -1), self.shard(da, 1), 36 + 2 * (da + 2)
        self.pass_both(lower, upper, self.shard(0, 1), self.shard(0, -1), 4 + 4 * (da + 1))
        self.got(lower, 1, slot)
        self.put(lower, None, self.sibling, 20 + 4 * (da + 1))
        self.got(upper, 0, slot + 1)
        self.put(upper, None, self.sibling, 20 + 4 * (da + 1) + 2)

    def end_b(self, da):
        base = 4 + 4 * (da + 1)
        index = self.shard(da, 2)
        self.got(index, 0, base + 2)
        self.got(index, 1, base + 3)
        self.put(index, None, self.sibling, 20 + 4 * (da + 1) + 3)

    def from_sibling(self):
        for slot in range(16):
            self.got(self.sibling, None, 20 + slot)

    def drain(self):
        for copy in self.sent:
            copy.wait_send()


def normalised(values):
    mean = jnp.mean(values, axis=-1, keepdims=True)
    centered = values - mean
    variance = jnp.mean(centered * centered, axis=-1, keepdims=True)
    return (centered * lax.rsqrt(variance + EPS_NORM)).astype(BF)


def nt(a, b):
    return lax.dot_general(a, b, (((1,), (1,)), ((), ())), preferred_element_type=F32)


def whole_kernel(
    audio_in, starts_in, lengths_in, slots_in, conv1_in, conv2_in, proj_in, qkv_in, out_in,
    dft_high_in, dft_low_in, mel_high_in, mel_low_in, patch_in,
    regrouped, attended,
    ext, frames_high, frames_low, log_mel, patches, taps, first, features,
    starts, lengths, slots, conv1, conv2, dft_high, dft_low, mel_high, mel_low, patch_map,
    proj, wide, rows_out, rows_own, rows_all, normed, mixed, context_out, context_in,
    local_sem, halo_sem, proj_send, proj_recv, wide_send, wide_recv,
    row_send, row_recv, z_send, z_recv, pass_send, pass_recv, keep_sem, context_send, context_recv,
):
    me, z = lax.axis_index("dp"), lax.axis_index("seq")
    x, y, core = me // 8, me // 2 % 4, me % 2
    sibling = me + 1 - 2 * core
    a, b = x * (1 - core) + y * core, y * (1 - core) + x * core
    sa, sb = 8 * (1 - core) + 2 * core, 2 * (1 - core) + 8 * core
    place = (core, a, b, sa, sb, sibling)
    line = me * 4 + z
    after, before = lax.rem(line + 1, 128), lax.rem(line + 127, 128)
    keeper = core == z // 2
    helper = core != z // 2
    row = me - core + z // 2
    partner, cross = z + 1 - 2 * (z % 2), 3 - z
    beyond = 3 - partner
    pair = z % 2 * 2 + core

    def local(source, target, index):
        copy = pltpu.make_async_copy(source, target, local_sem.at[index])
        copy.start()
        return copy

    loads = [
        local(source, target, index)
        for index, (source, target) in enumerate(
            (
                (audio_in, ext.at[:, pl.ds(RIM, SPAN)]),
                (dft_high_in, dft_high),
                (dft_low_in, dft_low),
                (mel_high_in, mel_high),
                (mel_low_in, mel_low),
                (patch_in, patch_map),
                (conv2_in, conv2),
                (proj_in, proj.at[me]),
            )
        )
    ]
    parts = [local(out_in, wide.at[me, :, pl.ds(3 * PAIR, D)], 12)] + [
        local(
            qkv_in.at[:, pl.ds(pl.multiple_of(third * D + z % 2 * PAIR, 128), PAIR)],
            wide.at[me, :, pl.ds(third * PAIR, PAIR)],
            8 + third,
        )
        for third in range(3)
    ]

    small = [
        local(source, target, 13 + index)
        for index, (source, target) in enumerate(
            ((conv1_in, conv1), (starts_in, starts), (lengths_in, lengths), (slots_in, slots))
        )
    ]
    barrier = pltpu.get_barrier_semaphore()

    @pl.loop(1, 32)
    def _(offset):
        pl.semaphore_signal(
            barrier, inc=1, device_id={"dp": lax.rem(me + offset, 32)}, device_id_type=MESH_ID
        )

    for offset in range(1, 4):
        pl.semaphore_signal(
            barrier, inc=1, device_id={"seq": lax.rem(z + offset, 4)}, device_id_type=MESH_ID
        )
    for offset in range(1, 4):
        pl.semaphore_signal(
            barrier,
            inc=1,
            device_id={"dp": sibling, "seq": lax.rem(z + offset, 4)},
            device_id_type=MESH_ID,
        )
    for other in (after, before):
        pl.semaphore_signal(
            barrier, inc=1, device_id={"dp": other // 4, "seq": other % 4}, device_id_type=MESH_ID
        )
    for load in small:
        load.wait()
    spread_taps(conv1, taps)
    first[:, :CH] = jnp.zeros((544, CH), BF)
    ext[:, RIM + SPAN :] = jnp.zeros((ROWS, EXT - RIM - SPAN), F32)
    pl.semaphore_wait(barrier, 39)
    halo = pltpu.make_async_remote_copy(
        src_ref=audio_in.at[:, pl.ds(SPAN - RIM, RIM)],
        dst_ref=ext.at[:, pl.ds(0, RIM)],
        send_sem=halo_sem.at[0],
        recv_sem=halo_sem.at[1],
        device_id={"dp": after // 4, "seq": after % 4},
        device_id_type=MESH_ID,
    )
    halo.start()
    ring = Ring(proj_in, proj, proj_send, proj_recv, place)
    ring.begin()

    loads[0].wait()

    @pl.loop(2, 9)
    def _(p):
        frame_step(p, ext, frames_high, frames_low)

    for load in loads[1:5]:
        load.wait()
    tables = (dft_high, dft_low, mel_high, mel_low)

    for q in range(4):
        if q == 1:
            ring.to_b(0, True)
        log_mel[q, 64:, :] = mel_of(frames_high[q, 64:, :], frames_low[q, 64:, :], *tables)

    loads[5].wait()
    late_patches(log_mel, patch_map, patches)

    def conv1_run(late):
        @pl.loop(0, 8)
        def _(j):
            for block in range(5):
                conv1_step(block, j, late, patches, taps, first)

    def conv2_run(low, high):
        @pl.loop(low, high)
        def _(group):
            for i in range(4):
                conv2_step(group * 4 + i, first, conv2, features)

    ring.pass_a()
    conv1_run(True)
    ring.pass_b(0)
    halo.wait_recv()

    @pl.when(line == 0)
    def _():
        ext[:, :RIM] = jnp.zeros((ROWS, RIM), F32)

    @pl.loop(0, 2)
    def _(p):
        frame_step(p, ext, frames_high, frames_low)

    early = mel_of(
        frames_high[:, :64, :].reshape(256, N_FFT), frames_low[:, :64, :].reshape(256, N_FFT), *tables
    )
    for q in range(4):
        log_mel[q, :64, :] = early[64 * q : 64 * q + 64]
    early_patches(log_mel, patch_map, patches)
    conv1_run(False)
    ring.end_a()
    loads[6].wait()
    conv2_run(0, 2)
    ring.pass_b(-1)
    ring.pass_b(1)
    ring.end_b(0)
    conv2_run(2, 4)
    ring.pass_b(2)
    conv2_run(4, 5)
    ring.end_b(-1)
    ring.end_b(1)
    ring.end_b(2)
    for part in parts:
        part.wait()
    wide_ring = Ring(wide.at[me], wide, wide_send, wide_recv, place)
    wide_ring.begin()
    wide_ring.to_b(0, True)
    tile_map = jnp.where(
        lax.broadcasted_iota(jnp.int32, (32, 256), 1) % 32 == lax.broadcasted_iota(jnp.int32, (32, 256), 0),
        1.0, 0.0,
    ).astype(BF)
    slot_values = jnp.broadcast_to(slots[...].astype(F32), (8, 32)).astype(BF)
    slots_wide = mm(slot_values, tile_map)[0:1, :].astype(jnp.int32)
    out_index = lax.broadcasted_iota(jnp.int32, (256, 256), 0)
    in_index = lax.broadcasted_iota(jnp.int32, (256, 256), 1)
    routing = jnp.where((slots_wide == out_index // 8) & (in_index // 32 == out_index % 8), 1.0, 0.0).astype(BF)
    ring.from_sibling()
    loads[7].wait()

    def row_copy(offset, half):
        target = lax.rem(x + 4 - offset // 8, 4) * 8 + lax.rem(me + offset, 8)
        lanes = pl.ds(half * 512, 512)
        return pltpu.make_async_remote_copy(
            src_ref=rows_out.at[target, :, lanes],
            dst_ref=rows_own.at[me, :, lanes],
            send_sem=row_send.at[32 * half + offset],
            recv_sem=row_recv.at[me],
            device_id={"dp": target},
            device_id_type=MESH_ID,
        )

    for half in range(2):
        lanes = slice(half * 512, half * 512 + 512)
        projected = mm(features[...], proj[:, :, lanes].reshape(20 * CH, 512)).astype(BF)
        rows_out[:, :, lanes] = mm(routing, projected).reshape(32, 8, 512).astype(BF)

        @pl.loop(1, 32)
        def _(offset):
            row_copy(offset, half).start()

    mine = local(rows_out.at[me], rows_own.at[me], 11)
    wide_ring.pass_a()
    wide_ring.pass_b(0)
    mine.wait()

    chunks = [lax.rem(x + index, 4) for index in range(4)]
    origins = (z, partner, cross, beyond)

    def part_of(buffer, index):
        return buffer.at[pl.ds(pl.multiple_of(chunks[index] * 8, 8), 8)]

    def row_part(origin, index):
        return rows_all.at[origin, pl.ds(pl.multiple_of(chunks[index] * 8, 8), 8)]

    def to_plane(source, origin, index, base, plane):
        return pltpu.make_async_remote_copy(
            src_ref=source,
            dst_ref=row_part(origin, index),
            send_sem=z_send.at[base + index],
            recv_sem=z_recv.at[base + index],
            device_id={"seq": plane},
            device_id_type=MESH_ID,
        )

    def to_sibling(source, place, index):
        return pltpu.make_async_remote_copy(
            src_ref=source,
            dst_ref=row_part(origins[place], index),
            send_sem=pass_send.at[4 * place + index],
            recv_sem=pass_recv.at[4 * place + index],
            device_id={"dp": sibling},
            device_id_type=MESH_ID,
        )

    def arrived(place, index, base):
        block = row_part(origins[place], index)
        to_plane(block, origins[place], index, base, partner).wait_recv()
        return block

    def own_to_partner(index):
        return to_plane(part_of(rows_own, index), z, index, 0, partner)

    def own_across(index):
        return to_plane(part_of(rows_own, index), z, index, 4, cross)

    def cross_to_partner(index):
        return to_plane(row_part(cross, index), cross, index, 8, partner)

    def own_copy(index):
        return pltpu.make_async_copy(part_of(rows_own, index), row_part(z, index), keep_sem.at[index])

    for index in range(4):
        @pl.loop(0, 8)
        def _(step):
            source = chunks[index] * 8 + step

            @pl.when(source != me)
            def _():
                block = rows_own.at[source]
                pltpu.make_async_remote_copy(
                    src_ref=block,
                    dst_ref=block,
                    send_sem=row_send.at[0],
                    recv_sem=row_recv.at[source],
                    device_id={"dp": sibling},
                    device_id_type=MESH_ID,
                ).wait_recv()

        @pl.when(keeper)
        def _():
            own_to_partner(index).start()
            to_sibling(part_of(rows_own, index), 0, index).start()
            own_copy(index).start()

        @pl.when(helper)
        def _():
            own_across(index).start()

    def pass_cross(index):
        @pl.when(keeper)
        def _():
            block = arrived(2, index, 4)
            cross_to_partner(index).start()
            to_sibling(block, 2, index).start()

    def pass_partner(index):
        @pl.when(keeper)
        def _():
            to_sibling(arrived(1, index, 0), 1, index).start()

    def pass_beyond(index):
        @pl.when(keeper)
        def _():
            to_sibling(arrived(3, index, 8), 3, index).start()

    def helped(place):
        @pl.when(helper)
        def _():
            for index in range(4):
                to_sibling(row_part(origins[place], index), place, index).wait_recv()

    def norm(origin):
        rows = pl.ds(pl.multiple_of(origin * 256, 256), 256)
        normed[rows, :] = normalised(rows_all[origin].astype(F32).reshape(256, D))

    pass_cross(0)
    wide_ring.end_a()
    pass_cross(1)
    pass_partner(0)
    wide_ring.end_b(0)
    pass_cross(2)
    pass_partner(1)
    wide_ring.pass_b(-1)
    pass_cross(3)
    pass_partner(2)
    wide_ring.pass_b(1)
    pass_partner(3)

    @pl.when(keeper)
    def _():
        for index in range(4):
            own_copy(index).wait()

    helped(0)
    norm(z)
    wide_ring.pass_b(2)
    pass_beyond(0)
    wide_ring.end_b(-1)
    wide_ring.end_b(1)
    pass_beyond(1)
    helped(1)
    norm(partner)
    pass_beyond(2)
    wide_ring.end_b(2)
    helped(2)
    norm(cross)
    pass_beyond(3)
    wide_ring.from_sibling()
    helped(3)
    norm(beyond)
    for third in range(3):
        lanes = pl.ds(pl.multiple_of(third * PAIR + core * PART, 128), PART)
        result = mm(normed[...], wide[:, :, lanes].reshape(D, PART))
        mixed[:, third * PART : third * PART + PART] = result.astype(BF)

    def bounds(owner):
        chosen = slots[...] == owner
        begin = jnp.sum(jnp.where(chosen, starts[...].astype(F32), 0.0), axis=1, keepdims=True)
        span = jnp.sum(jnp.where(chosen, lengths[...].astype(F32), 0.0), axis=1, keepdims=True)
        return begin, begin + span

    def valid_of(owner, index, limits):
        frame = (index // 8 * 4 + owner) * 8 + index % 8
        sample = (frame * (4 * HOP)).astype(F32)
        return (sample >= limits[0]) & (sample < limits[1])

    key_index = lax.broadcasted_iota(jnp.int32, (1, 1024), 1)
    bias = jnp.where(valid_of(key_index // 256, key_index % 256, bounds(row)), 0.0, MASKED)
    scale = HEAD_DIM ** (-0.5) * math.log2(math.e)

    def context_target(step):
        return lax.rem(z + 2 + step - step // 2 * (2 * step - 1), 4)

    def context_copy(step, head):
        target = context_target(step)
        lanes = pl.ds(head * HEAD_DIM, HEAD_DIM)
        return pltpu.make_async_remote_copy(
            src_ref=context_out.at[target, :, lanes],
            dst_ref=context_in.at[pair, :, lanes],
            send_sem=context_send.at[2 * step + head],
            recv_sem=context_recv.at[pair],
            device_id={"dp": row, "seq": target},
            device_id_type=MESH_ID,
        )

    @pl.loop(0, 4)
    def _(step):
        target = context_target(step)
        rows = pl.ds(pl.multiple_of(target * 256, 256), 256)
        for head in range(2):
            lanes = slice(head * HEAD_DIM, (head + 1) * HEAD_DIM)
            query = mixed[rows, lanes]
            key = mixed[:, PART + head * HEAD_DIM : PART + (head + 1) * HEAD_DIM]
            value = mixed[:, 2 * PART + head * HEAD_DIM : 2 * PART + (head + 1) * HEAD_DIM]
            scores = nt(query, key) * scale + bias
            weights = jnp.exp2(scores - jnp.max(scores, axis=1, keepdims=True))
            total = jnp.sum(weights, axis=1, keepdims=True)
            context_out[target, :, lanes] = (mm(weights.astype(BF), value) / total).astype(BF)

            @pl.when((step < 3) | helper)
            def _():
                context_copy(step, head).start()

    @pl.when(keeper)
    def _():
        context_in[pair] = context_out[z]

    def context_wait(other):
        pltpu.make_async_remote_copy(
            src_ref=context_in.at[other],
            dst_ref=context_in.at[other],
            send_sem=context_send.at[3],
            recv_sem=context_recv.at[other],
            device_id={"dp": row, "seq": cross},
            device_id_type=MESH_ID,
        ).wait_recv()

    for offset in range(1, 4):
        context_wait(lax.rem(pair + offset, 4))

    @pl.when(helper)
    def _():
        context_wait(pair)

    output = jnp.zeros((256, D), F32)
    for part in range(4):
        start = 3 * PAIR + part * PART
        output += nt(context_in[part], wide[:, :, start : start + PART].reshape(D, PART))
    row_valid = valid_of(z, lax.broadcasted_iota(jnp.int32, (256, 1), 0), bounds(me))
    attended[...] = jnp.where(row_valid, output, 0.0).reshape(32, 8, D).astype(BF)
    own = rows_own[...].astype(F32).reshape(256, D)
    regrouped[...] = jnp.where(row_valid, own, 0.0).reshape(32, 8, D).astype(BF)

    halo.wait_send()
    ring.drain()
    wide_ring.drain()

    @pl.loop(1, 32)
    def _(offset):
        for half in range(2):
            row_copy(offset, half).wait_send()

    @pl.when(keeper)
    def _():
        for index in range(4):
            own_to_partner(index).wait_send()
            cross_to_partner(index).wait_send()
            for place in range(4):
                to_sibling(part_of(rows_own, index), place, index).wait_send()

    @pl.when(helper)
    def _():
        for index in range(4):
            own_across(index).wait_send()
        for head in range(2):
            context_copy(3, head).wait_send()

    @pl.loop(0, 3)
    def _(step):
        for head in range(2):
            context_copy(step, head).wait_send()


def on_device(
    audio, starts, lengths, slots, conv1_weight, conv2_weight, proj_weight, qkv_weight, out_weight
):
    args = (
        audio, starts.reshape(1, 32), lengths.reshape(1, 32), slots.reshape(1, 32),
        conv1_weight, conv2_weight, proj_weight, qkv_weight, out_weight.T,
        *spectrum_tables(), *filter_tables(), patch_table(),
    )
    vmem = pl.BlockSpec(memory_space=pltpu.VMEM)
    dma = pltpu.SemaphoreType.DMA
    shape = jax.ShapeDtypeStruct((32, 8, D), BF)
    regrouped, attended = pl.pallas_call(
        whole_kernel,
        out_shape=(shape, shape),
        in_specs=[pl.BlockSpec(memory_space=pltpu.HBM)] * 14,
        out_specs=(vmem, vmem),
        scratch_shapes=[
            pltpu.VMEM((ROWS, EXT), F32),
            pltpu.VMEM((4, 288, N_FFT), BF),
            pltpu.VMEM((4, 288, N_FFT), BF),
            pltpu.VMEM((4, 288, 128), BF),
            pltpu.VMEM((544, 640), BF),
            pltpu.VMEM((8, 128, CH), BF),
            pltpu.VMEM((544, 41 * CH), BF),
            pltpu.VMEM((256, 20 * CH), BF),
            pltpu.VMEM((1, 32), jnp.int32),
            pltpu.VMEM((1, 32), jnp.int32),
            pltpu.VMEM((1, 32), jnp.int32),
            pltpu.VMEM((9, CH), BF),
            pltpu.VMEM((9 * CH, CH), BF),
            pltpu.VMEM((N_FFT, N_FFT), BF),
            pltpu.VMEM((N_FFT, N_FFT), BF),
            pltpu.VMEM((N_FFT // 2, 128), BF),
            pltpu.VMEM((N_FFT // 2, 128), BF),
            pltpu.VMEM((384, 640), BF),
            pltpu.VMEM((32, 160, D), BF),
            pltpu.VMEM((32, 32, WIDE), BF),
            pltpu.VMEM((32, 8, D), BF),
            pltpu.VMEM((32, 8, D), BF),
            pltpu.VMEM((4, 32, 8, D), BF),
            pltpu.VMEM((1024, D), BF),
            pltpu.VMEM((1024, 3 * PART), BF),
            pltpu.VMEM((4, 256, PART), BF),
            pltpu.VMEM((4, 256, PART), BF),
            dma((17,)), dma((2,)),
            dma((46,)), dma((46,)), dma((46,)), dma((46,)),
            dma((64,)), dma((32,)), dma((12,)), dma((12,)), dma((16,)), dma((16,)), dma((4,)), dma((8,)), dma((4,)),
        ],
        compiler_params=pltpu.CompilerParams(
            vmem_limit_bytes=VMEM_LIMIT, collective_id=0, has_side_effects=True
        ),
        name="whole",
    )(*args)
    return regrouped.reshape(1, 32, 1, 8, D), attended.reshape(1, 32, 1, 8, D)


def solution(mesh):
    in_specs = (
        P(None, ("dp", "seq")), P(), P(), P(), P(), P(), P("dp", None), P("dp", None), P(None, "dp"),
    )
    out_specs = (P("dp", None, "seq", None, None), P("dp", None, "seq", None, None))
    return jax.shard_map(
        on_device, mesh=mesh, in_specs=in_specs, out_specs=out_specs, check_vma=False
    )
```

```python
import functools
import math

import jax
import jax.numpy as jnp
import numpy as np
from jax import lax
from jax.experimental import pallas as pl
from jax.experimental.pallas import tpu as pltpu
from jax.sharding import PartitionSpec as P

D = 1024
HEADS = 8
HEAD_DIM = 128
MELS = 80
N_FFT = 512
HOP = 160
W = 8
CH = 256
ROWS = 32
RIM = 896
SPAN = 5120
EXT = 6272
BF = jnp.bfloat16
F32 = jnp.float32

SAMPLE_RATE = 16000.0
EPS_LOG = 1e-06
EPS_NORM = 1e-05
MASKED = -1e30
VMEM_LIMIT = 56 * 1024 * 1024


def mel_table(size, bands):
    count = size // 2 + 1
    highest = 2595.0 * math.log10(1.0 + SAMPLE_RATE / 1400.0)
    points = np.linspace(0.0, highest, bands + 2)
    edges = 700.0 * (10.0 ** (points / 2595.0) - 1.0)
    edges[0] = 0.0
    edges[-1] = SAMPLE_RATE / 2.0
    frequency = np.arange(count) * (SAMPLE_RATE / size)
    lower = edges[:-2][None, :]
    middle = edges[1:-1][None, :]
    upper = edges[2:][None, :]
    rising = (frequency[:, None] - lower) / (middle - lower)
    falling = (upper - frequency[:, None]) / (upper - middle)
    return np.maximum(0.0, np.minimum(rising, falling)).astype(np.float32)


def split_high_low(table):
    high = np.asarray(table, np.float64).astype(BF)
    low = (np.asarray(table, np.float64) - high.astype(np.float64)).astype(BF)
    return high, low


def spectrum_tables():
    sample = np.arange(N_FFT)
    angle = (sample[:, None] * np.arange(N_FFT // 2)[None, :] % N_FFT) * (2.0 * math.pi / N_FFT)
    window = 0.5 - 0.5 * np.cos(sample * (2.0 * math.pi / N_FFT))
    return split_high_low(np.concatenate([np.cos(angle), np.sin(angle)], axis=1) * window[:, None])


def filter_tables():
    padded = np.zeros((N_FFT // 2, 128), np.float64)
    padded[:, :MELS] = mel_table(N_FFT, MELS)[: N_FFT // 2]
    return split_high_low(padded)


def patch_table():
    table = np.zeros((3 * 128, 40 * 16), np.float32)
    for g in range(40):
        for a in range(3):
            for b in range(3):
                band = 2 * g - 1 + b
                if 0 <= band < MELS:
                    table[a * 128 + band, g * 16 + 3 * a + b] = 1.0
    return table.astype(BF)


def mm(a, b):
    return jnp.dot(a, b, preferred_element_type=F32)


def halves(value):
    high = value.astype(BF)
    return high, (value - high.astype(F32)).astype(BF)


def frame_step(p, ext, frames_high, frames_low):
    window = ext[:, pl.ds(pl.multiple_of(p * 640, 128), 1152)]
    rows = pl.ds(pl.multiple_of(p * 32, 32), 32)
    for q in range(4):
        start = 64 + HOP * q
        base, offset = start // 128 * 128, start % 128
        if offset:
            piece = pltpu.roll(window[:, base : base + 640], 640 - offset, 1)[:, :N_FFT]
        else:
            piece = window[:, base : base + N_FFT]
        high, low = halves(piece)
        frames_high[q, rows, :] = high
        frames_low[q, rows, :] = low


def mel_of(high, low, dft_high, dft_low, mel_high, mel_low):
    spectrum = mm(high, dft_high[...]) + mm(high, dft_low[...]) + mm(low, dft_high[...])
    half = N_FFT // 2
    power = spectrum[:, :half] * spectrum[:, :half] + spectrum[:, half:] * spectrum[:, half:]
    high, low = halves(power)
    mel = mm(high, mel_high[...]) + mm(high, mel_low[...]) + mm(low, mel_high[...])
    return jnp.log(mel + EPS_LOG).astype(BF)


def late_patches(log_mel, patch_map, patches):
    even = jnp.concatenate([log_mel[0, 64:], log_mel[1, 64:], log_mel[2, 64:]], axis=1)
    patches[:224, :] = mm(even, patch_map[...]).astype(BF)
    odd = jnp.concatenate([log_mel[2, 64:256], log_mel[3, 64:256], log_mel[0, 96:]], axis=1)
    patches[224:416, :] = mm(odd, patch_map[...]).astype(BF)


def early_patches(log_mel, patch_map, patches):
    even = jnp.concatenate([log_mel[0, :64], log_mel[1, :64], log_mel[2, :64]], axis=1)
    odd = jnp.concatenate([log_mel[2, :64], log_mel[3, :64], log_mel[0, 32:96]], axis=1)
    patches[416:, :] = mm(jnp.concatenate([even, odd], axis=0), patch_map[...]).astype(BF)


def spread_taps(conv1, taps):
    taps[...] = jnp.zeros_like(taps)
    for j in range(8):
        taps[j, 16 * j : 16 * j + 9, :] = conv1[...]


def conv1_step(block, j, late, patches, taps, first):
    lanes = slice(block * 128, block * 128 + 128)
    target = pl.ds(pl.multiple_of((block * 8 + j + 1) * CH, CH), CH)
    rows, count = (slice(0, 416), 224) if late else (slice(416, 544), 64)
    result = jnp.maximum(mm(patches[rows, lanes], taps[j]), 0.0).astype(BF)
    first[slice(64, 288) if late else slice(0, 64), target] = result[:count]
    first[slice(352, 544) if late else slice(288, 352), target] = result[count:]


def conv2_step(h, first, conv2, features):
    lanes = pl.ds(pl.multiple_of(h * 512, 512), 768)
    total = mm(first[0:256, lanes], conv2[0:768, :])
    total += mm(first[288:544, lanes], conv2[768:1536, :])
    total += mm(first[32:288, lanes], conv2[1536:2304, :])
    features[:, pl.ds(pl.multiple_of(h * CH, CH), CH)] = jnp.maximum(total, 0.0).astype(BF)


def to_rows(projected, slots_wide):
    out_index = lax.broadcasted_iota(jnp.int32, (256, 256), 0)
    in_index = lax.broadcasted_iota(jnp.int32, (256, 256), 1)
    same_row = slots_wide == out_index // 8
    same_frame = in_index // 32 == out_index % 8
    routing = jnp.where(same_row & same_frame, 1.0, 0.0).astype(BF)
    return mm(routing, projected).astype(BF)

MESH_ID = pl.DeviceIdType.MESH
PART = 2 * HEAD_DIM
PAIR = 2 * PART
WIDE = 3 * PAIR + D


class Ring:
    def __init__(self, source, buffer, send, recv, place):
        self.source, self.buffer, self.send, self.recv = source, buffer, send, recv
        self.core, self.a, self.b, self.sa, self.sb, self.sibling = place
        self.count = 0
        self.sent = []
        self.rows = buffer.shape[1]

    def shard(self, da, db):
        return lax.rem(self.a + da + 4, 4) * self.sa + lax.rem(self.b + db + 4, 4) * self.sb + self.core

    def part(self, index, half):
        if half is None:
            return self.buffer.at[index]
        step = self.rows // 2
        return self.buffer.at[index, pl.ds(half * step, step)]

    def origin(self, half):
        step = self.rows // 2
        return self.source if half is None else self.source.at[pl.ds(half * step, step)]

    def put(self, index, half, target, slot, own=False):
        copy = pltpu.make_async_remote_copy(
            src_ref=self.origin(half) if own else self.part(index, half),
            dst_ref=self.part(index, half),
            send_sem=self.send.at[self.count],
            recv_sem=self.recv.at[slot],
            device_id={"dp": target},
            device_id_type=MESH_ID,
        )
        copy.start()
        self.count += 1
        self.sent.append(copy)

    def got(self, index, half, slot):
        pltpu.make_async_remote_copy(
            src_ref=self.part(index, half),
            dst_ref=self.part(index, half),
            send_sem=self.send.at[0],
            recv_sem=self.recv.at[slot],
            device_id={"dp": self.sibling},
            device_id_type=MESH_ID,
        ).wait_recv()

    def to_both(self, index, above, below, base, line, own=False):
        for target, half, slot in ((above, 0, 0), (below, 1, 1)):
            self.put(index, half, target, base + slot, own)
            self.put(index, 1 - half, target, 36 + 2 * line + slot, own)

    def pass_both(self, lower, upper, above, below, base):
        self.got(lower, 0, base)
        self.put(lower, 0, above, base + 2)
        self.got(upper, 1, base + 1)
        self.put(upper, 1, below, base + 3)

    def to_b(self, da, own=False):
        index = self.shard(da, 0)
        self.to_both(index, self.shard(0, 1), self.shard(0, -1), 4 + 4 * (da + 1), da + 2, own)
        self.put(index, None, self.sibling, 20 + 4 * (da + 1) + 1, own)

    def begin(self):
        self.to_both(self.shard(0, 0), self.shard(1, 0), self.shard(-1, 0), 0, 0, True)

    def pass_a(self):
        self.pass_both(self.shard(-1, 0), self.shard(1, 0), self.shard(1, 0), self.shard(-1, 0), 0)
        self.got(self.shard(-1, 0), 1, 36)
        self.to_b(-1)
        self.got(self.shard(1, 0), 0, 37)
        self.to_b(1)

    def end_a(self):
        index = self.shard(2, 0)
        self.got(index, 0, 2)
        self.got(index, 1, 3)
        self.to_b(2)

    def pass_b(self, da):
        lower, upper, slot = self.shard(da, -1), self.shard(da, 1), 36 + 2 * (da + 2)
        self.pass_both(lower, upper, self.shard(0, 1), self.shard(0, -1), 4 + 4 * (da + 1))
        self.got(lower, 1, slot)
        self.put(lower, None, self.sibling, 20 + 4 * (da + 1))
        self.got(upper, 0, slot + 1)
        self.put(upper, None, self.sibling, 20 + 4 * (da + 1) + 2)

    def end_b(self, da):
        base = 4 + 4 * (da + 1)
        index = self.shard(da, 2)
        self.got(index, 0, base + 2)
        self.got(index, 1, base + 3)
        self.put(index, None, self.sibling, 20 + 4 * (da + 1) + 3)

    def from_sibling(self):
        for slot in range(16):
            self.got(self.sibling, None, 20 + slot)

    def drain(self):
        for copy in self.sent:
            copy.wait_send()


def normalised(values):
    mean = jnp.mean(values, axis=-1, keepdims=True)
    centered = values - mean
    variance = jnp.mean(centered * centered, axis=-1, keepdims=True)
    return (centered * lax.rsqrt(variance + EPS_NORM)).astype(BF)


def nt(a, b):
    return lax.dot_general(a, b, (((1,), (1,)), ((), ())), preferred_element_type=F32)


def whole_kernel(
    audio_in, starts_in, lengths_in, slots_in, conv1_in, conv2_in, proj_in, qkv_in, out_in,
    dft_high_in, dft_low_in, mel_high_in, mel_low_in, patch_in,
    regrouped, attended,
    ext, frames_high, frames_low, log_mel, patches, taps, first, features,
    starts, lengths, slots, conv1, conv2, dft_high, dft_low, mel_high, mel_low, patch_map,
    proj, wide, rows_out, rows_own, rows_all, normed, mixed, context_out, context_in,
    local_sem, halo_sem, proj_send, proj_recv, wide_send, wide_recv,
    row_send, row_recv, z_send, z_recv, pass_send, pass_recv, keep_sem, context_send, context_recv,
):
    me, z = lax.axis_index("dp"), lax.axis_index("seq")
    x, y, core = me // 8, me // 2 % 4, me % 2
    sibling = me + 1 - 2 * core
    a, b = x * (1 - core) + y * core, y * (1 - core) + x * core
    sa, sb = 8 * (1 - core) + 2 * core, 2 * (1 - core) + 8 * core
    place = (core, a, b, sa, sb, sibling)
    line = me * 4 + z
    after, before = lax.rem(line + 1, 128), lax.rem(line + 127, 128)
    keeper = core == z // 2
    helper = core != z // 2
    row = me - core + z // 2
    partner, cross = z + 1 - 2 * (z % 2), 3 - z
    beyond = 3 - partner
    pair = z % 2 * 2 + core

    def local(source, target, index):
        copy = pltpu.make_async_copy(source, target, local_sem.at[index])
        copy.start()
        return copy

    loads = [
        local(source, target, index)
        for index, (source, target) in enumerate(
            (
                (audio_in, ext.at[:, pl.ds(RIM, SPAN)]),
                (dft_high_in, dft_high),
                (dft_low_in, dft_low),
                (mel_high_in, mel_high),
                (mel_low_in, mel_low),
                (patch_in, patch_map),
                (conv2_in, conv2),
                (proj_in, proj.at[me]),
            )
        )
    ]
    parts = [local(out_in, wide.at[me, :, pl.ds(3 * PAIR, D)], 12)] + [
        local(
            qkv_in.at[:, pl.ds(pl.multiple_of(third * D + z % 2 * PAIR, 128), PAIR)],
            wide.at[me, :, pl.ds(third * PAIR, PAIR)],
            8 + third,
        )
        for third in range(3)
    ]

    small = [
        local(source, target, 13 + index)
        for index, (source, target) in enumerate(
            ((conv1_in, conv1), (starts_in, starts), (lengths_in, lengths), (slots_in, slots))
        )
    ]
    barrier = pltpu.get_barrier_semaphore()

    @pl.loop(1, 32)
    def _(offset):
        pl.semaphore_signal(
            barrier, inc=1, device_id={"dp": lax.rem(me + offset, 32)}, device_id_type=MESH_ID
        )

    for offset in range(1, 4):
        pl.semaphore_signal(
            barrier, inc=1, device_id={"seq": lax.rem(z + offset, 4)}, device_id_type=MESH_ID
        )
    for offset in range(1, 4):
        pl.semaphore_signal(
            barrier,
            inc=1,
            device_id={"dp": sibling, "seq": lax.rem(z + offset, 4)},
            device_id_type=MESH_ID,
        )
    for other in (after, before):
        pl.semaphore_signal(
            barrier, inc=1, device_id={"dp": other // 4, "seq": other % 4}, device_id_type=MESH_ID
        )
    for load in small:
        load.wait()
    spread_taps(conv1, taps)
    first[:, :CH] = jnp.zeros((544, CH), BF)
    ext[:, RIM + SPAN :] = jnp.zeros((ROWS, EXT - RIM - SPAN), F32)
    pl.semaphore_wait(barrier, 39)
    halo = pltpu.make_async_remote_copy(
        src_ref=audio_in.at[:, pl.ds(SPAN - RIM, RIM)],
        dst_ref=ext.at[:, pl.ds(0, RIM)],
        send_sem=halo_sem.at[0],
        recv_sem=halo_sem.at[1],
        device_id={"dp": after // 4, "seq": after % 4},
        device_id_type=MESH_ID,
    )
    halo.start()
    ring = Ring(proj_in, proj, proj_send, proj_recv, place)
    ring.begin()

    loads[0].wait()

    @pl.loop(2, 9)
    def _(p):
        frame_step(p, ext, frames_high, frames_low)

    for load in loads[1:5]:
        load.wait()
    tables = (dft_high, dft_low, mel_high, mel_low)

    for q in range(4):
        if q == 1:
            ring.to_b(0, True)
        log_mel[q, 64:, :] = mel_of(frames_high[q, 64:, :], frames_low[q, 64:, :], *tables)

    loads[5].wait()
    late_patches(log_mel, patch_map, patches)

    def conv1_run(late):
        @pl.loop(0, 8)
        def _(j):
            for block in range(5):
                conv1_step(block, j, late, patches, taps, first)

    def conv2_run(low, high):
        @pl.loop(low, high)
        def _(group):
            for i in range(4):
                conv2_step(group * 4 + i, first, conv2, features)

    ring.pass_a()
    conv1_run(True)
    ring.pass_b(0)
    halo.wait_recv()

    @pl.when(line == 0)
    def _():
        ext[:, :RIM] = jnp.zeros((ROWS, RIM), F32)

    @pl.loop(0, 2)
    def _(p):
        frame_step(p, ext, frames_high, frames_low)

    early = mel_of(
        frames_high[:, :64, :].reshape(256, N_FFT), frames_low[:, :64, :].reshape(256, N_FFT), *tables
    )
    for q in range(4):
        log_mel[q, :64, :] = early[64 * q : 64 * q + 64]
    early_patches(log_mel, patch_map, patches)
    conv1_run(False)
    ring.end_a()
    loads[6].wait()
    conv2_run(0, 2)
    ring.pass_b(-1)
    ring.pass_b(1)
    ring.end_b(0)
    conv2_run(2, 4)
    ring.pass_b(2)
    conv2_run(4, 5)
    ring.end_b(-1)
    ring.end_b(1)
    ring.end_b(2)
    for part in parts:
        part.wait()
    wide_ring = Ring(wide.at[me], wide, wide_send, wide_recv, place)
    wide_ring.begin()
    wide_ring.to_b(0, True)
    tile_map = jnp.where(
        lax.broadcasted_iota(jnp.int32, (32, 256), 1) % 32 == lax.broadcasted_iota(jnp.int32, (32, 256), 0),
        1.0, 0.0,
    ).astype(BF)
    slot_values = jnp.broadcast_to(slots[...].astype(F32), (8, 32)).astype(BF)
    slots_wide = mm(slot_values, tile_map)[0:1, :].astype(jnp.int32)
    out_index = lax.broadcasted_iota(jnp.int32, (256, 256), 0)
    in_index = lax.broadcasted_iota(jnp.int32, (256, 256), 1)
    routing = jnp.where((slots_wide == out_index // 8) & (in_index // 32 == out_index % 8), 1.0, 0.0).astype(BF)
    ring.from_sibling()
    loads[7].wait()

    def row_copy(offset, half):
        target = lax.rem(x + 4 - offset // 8, 4) * 8 + lax.rem(me + offset, 8)
        lanes = pl.ds(half * 512, 512)
        return pltpu.make_async_remote_copy(
            src_ref=rows_out.at[target, :, lanes],
            dst_ref=rows_own.at[me, :, lanes],
            send_sem=row_send.at[32 * half + offset],
            recv_sem=row_recv.at[me],
            device_id={"dp": target},
            device_id_type=MESH_ID,
        )

    for half in range(2):
        lanes = slice(half * 512, half * 512 + 512)
        projected = mm(features[...], proj[:, :, lanes].reshape(20 * CH, 512)).astype(BF)
        rows_out[:, :, lanes] = mm(routing, projected).reshape(32, 8, 512).astype(BF)

        @pl.loop(1, 32)
        def _(offset):
            row_copy(offset, half).start()

    mine = local(rows_out.at[me], rows_own.at[me], 11)
    wide_ring.pass_a()
    wide_ring.pass_b(0)
    mine.wait()

    chunks = [lax.rem(x + index, 4) for index in range(4)]
    origins = (z, partner, cross, beyond)

    def part_of(buffer, index):
        return buffer.at[pl.ds(pl.multiple_of(chunks[index] * 8, 8), 8)]

    def row_part(origin, index):
        return rows_all.at[origin, pl.ds(pl.multiple_of(chunks[index] * 8, 8), 8)]

    def to_plane(source, origin, index, base, plane):
        return pltpu.make_async_remote_copy(
            src_ref=source,
            dst_ref=row_part(origin, index),
            send_sem=z_send.at[base + index],
            recv_sem=z_recv.at[base + index],
            device_id={"seq": plane},
            device_id_type=MESH_ID,
        )

    def to_sibling(source, place, index):
        return pltpu.make_async_remote_copy(
            src_ref=source,
            dst_ref=row_part(origins[place], index),
            send_sem=pass_send.at[4 * place + index],
            recv_sem=pass_recv.at[4 * place + index],
            device_id={"dp": sibling},
            device_id_type=MESH_ID,
        )

    def arrived(place, index, base):
        block = row_part(origins[place], index)
        to_plane(block, origins[place], index, base, partner).wait_recv()
        return block

    def own_to_partner(index):
        return to_plane(part_of(rows_own, index), z, index, 0, partner)

    def own_across(index):
        return to_plane(part_of(rows_own, index), z, index, 4, cross)

    def cross_to_partner(index):
        return to_plane(row_part(cross, index), cross, index, 8, partner)

    def own_copy(index):
        return pltpu.make_async_copy(part_of(rows_own, index), row_part(z, index), keep_sem.at[index])

    for index in range(4):
        @pl.loop(0, 8)
        def _(step):
            source = chunks[index] * 8 + step

            @pl.when(source != me)
            def _():
                block = rows_own.at[source]
                pltpu.make_async_remote_copy(
                    src_ref=block,
                    dst_ref=block,
                    send_sem=row_send.at[0],
                    recv_sem=row_recv.at[source],
                    device_id={"dp": sibling},
                    device_id_type=MESH_ID,
                ).wait_recv()

        @pl.when(keeper)
        def _():
            own_to_partner(index).start()
            to_sibling(part_of(rows_own, index), 0, index).start()
            own_copy(index).start()

        @pl.when(helper)
        def _():
            own_across(index).start()

    def pass_cross(index):
        @pl.when(keeper)
        def _():
            block = arrived(2, index, 4)
            cross_to_partner(index).start()
            to_sibling(block, 2, index).start()

    def pass_partner(index):
        @pl.when(keeper)
        def _():
            to_sibling(arrived(1, index, 0), 1, index).start()

    def pass_beyond(index):
        @pl.when(keeper)
        def _():
            to_sibling(arrived(3, index, 8), 3, index).start()

    def helped(place):
        @pl.when(helper)
        def _():
            for index in range(4):
                to_sibling(row_part(origins[place], index), place, index).wait_recv()

    def norm(origin):
        rows = pl.ds(pl.multiple_of(origin * 256, 256), 256)
        normed[rows, :] = normalised(rows_all[origin].astype(F32).reshape(256, D))

    def bounds(owner):
        chosen = slots[...] == owner
        begin = jnp.sum(jnp.where(chosen, starts[...].astype(F32), 0.0), axis=1, keepdims=True)
        span = jnp.sum(jnp.where(chosen, lengths[...].astype(F32), 0.0), axis=1, keepdims=True)
        return begin, begin + span

    def valid_of(owner, index, limits):
        frame = (index // 8 * 4 + owner) * 8 + index % 8
        sample = (frame * (4 * HOP)).astype(F32)
        return (sample >= limits[0]) & (sample < limits[1])

    key_index = lax.broadcasted_iota(jnp.int32, (1, 1024), 1)
    bias = jnp.where(valid_of(key_index // 256, key_index % 256, bounds(row)), 0.0, MASKED)
    row_valid = valid_of(z, lax.broadcasted_iota(jnp.int32, (256, 1), 0), bounds(me))

    pass_cross(0)
    wide_ring.end_a()
    pass_cross(1)
    pass_partner(0)
    wide_ring.end_b(0)
    pass_cross(2)
    pass_partner(1)
    wide_ring.pass_b(-1)
    pass_cross(3)
    pass_partner(2)
    wide_ring.pass_b(1)
    pass_partner(3)

    @pl.when(keeper)
    def _():
        for index in range(4):
            own_copy(index).wait()

    helped(0)
    norm(z)
    wide_ring.pass_b(2)
    pass_beyond(0)
    wide_ring.end_b(-1)
    wide_ring.end_b(1)
    pass_beyond(1)
    helped(1)
    norm(partner)
    pass_beyond(2)
    wide_ring.end_b(2)
    helped(2)
    norm(cross)
    pass_beyond(3)
    helped(3)
    norm(beyond)
    wide_ring.from_sibling()
    for third in range(3):
        lanes = pl.ds(pl.multiple_of(third * PAIR + core * PART, 128), PART)
        result = mm(normed[...], wide[:, :, lanes].reshape(D, PART))
        mixed[:, third * PART : third * PART + PART] = result.astype(BF)

    scale = HEAD_DIM ** (-0.5) * math.log2(math.e)

    def context_target(step):
        return lax.rem(z + 2 + step - step // 2 * (2 * step - 1), 4)

    def context_copy(step, head):
        target = context_target(step)
        lanes = pl.ds(head * HEAD_DIM, HEAD_DIM)
        return pltpu.make_async_remote_copy(
            src_ref=context_out.at[target, :, lanes],
            dst_ref=context_in.at[pair, :, lanes],
            send_sem=context_send.at[2 * step + head],
            recv_sem=context_recv.at[pair],
            device_id={"dp": row, "seq": target},
            device_id_type=MESH_ID,
        )

    @pl.loop(0, 4)
    def _(step):
        target = context_target(step)
        rows = pl.ds(pl.multiple_of(target * 256, 256), 256)
        for head in range(2):
            lanes = slice(head * HEAD_DIM, (head + 1) * HEAD_DIM)
            query = mixed[rows, lanes]
            key = mixed[:, PART + head * HEAD_DIM : PART + (head + 1) * HEAD_DIM]
            value = mixed[:, 2 * PART + head * HEAD_DIM : 2 * PART + (head + 1) * HEAD_DIM]
            scores = nt(query, key) * scale + bias
            weights = jnp.exp2(scores - jnp.max(scores, axis=1, keepdims=True))
            total = jnp.sum(weights, axis=1, keepdims=True)
            context_out[target, :, lanes] = (mm(weights.astype(BF), value) / total).astype(BF)

            @pl.when((step < 3) | helper)
            def _():
                context_copy(step, head).start()

    @pl.when(keeper)
    def _():
        context_in[pair] = context_out[z]

    def context_wait(other):
        pltpu.make_async_remote_copy(
            src_ref=context_in.at[other],
            dst_ref=context_in.at[other],
            send_sem=context_send.at[3],
            recv_sem=context_recv.at[other],
            device_id={"dp": row, "seq": cross},
            device_id_type=MESH_ID,
        ).wait_recv()

    for offset in range(1, 4):
        context_wait(lax.rem(pair + offset, 4))

    @pl.when(helper)
    def _():
        context_wait(pair)

    output = jnp.zeros((256, D), F32)
    for part in range(4):
        start = 3 * PAIR + part * PART
        output += nt(context_in[part], wide[:, :, start : start + PART].reshape(D, PART))
    attended[...] = jnp.where(row_valid, output, 0.0).reshape(32, 8, D).astype(BF)
    own = rows_own[...].astype(F32).reshape(256, D)
    regrouped[...] = jnp.where(row_valid, own, 0.0).reshape(32, 8, D).astype(BF)

    halo.wait_send()
    ring.drain()
    wide_ring.drain()

    @pl.loop(1, 32)
    def _(offset):
        for half in range(2):
            row_copy(offset, half).wait_send()

    @pl.when(keeper)
    def _():
        for index in range(4):
            own_to_partner(index).wait_send()
            cross_to_partner(index).wait_send()
            for place in range(4):
                to_sibling(part_of(rows_own, index), place, index).wait_send()

    @pl.when(helper)
    def _():
        for index in range(4):
            own_across(index).wait_send()
        for head in range(2):
            context_copy(3, head).wait_send()

    @pl.loop(0, 3)
    def _(step):
        for head in range(2):
            context_copy(step, head).wait_send()


def on_device(
    audio, starts, lengths, slots, conv1_weight, conv2_weight, proj_weight, qkv_weight, out_weight
):
    args = (
        audio, starts.reshape(1, 32), lengths.reshape(1, 32), slots.reshape(1, 32),
        conv1_weight, conv2_weight, proj_weight, qkv_weight, out_weight.T,
        *spectrum_tables(), *filter_tables(), patch_table(),
    )
    vmem = pl.BlockSpec(memory_space=pltpu.VMEM)
    dma = pltpu.SemaphoreType.DMA
    shape = jax.ShapeDtypeStruct((32, 8, D), BF)
    regrouped, attended = pl.pallas_call(
        whole_kernel,
        out_shape=(shape, shape),
        in_specs=[pl.BlockSpec(memory_space=pltpu.HBM)] * 14,
        out_specs=(vmem, vmem),
        scratch_shapes=[
            pltpu.VMEM((ROWS, EXT), F32),
            pltpu.VMEM((4, 288, N_FFT), BF),
            pltpu.VMEM((4, 288, N_FFT), BF),
            pltpu.VMEM((4, 288, 128), BF),
            pltpu.VMEM((544, 640), BF),
            pltpu.VMEM((8, 128, CH), BF),
            pltpu.VMEM((544, 41 * CH), BF),
            pltpu.VMEM((256, 20 * CH), BF),
            pltpu.VMEM((1, 32), jnp.int32),
            pltpu.VMEM((1, 32), jnp.int32),
            pltpu.VMEM((1, 32), jnp.int32),
            pltpu.VMEM((9, CH), BF),
            pltpu.VMEM((9 * CH, CH), BF),
            pltpu.VMEM((N_FFT, N_FFT), BF),
            pltpu.VMEM((N_FFT, N_FFT), BF),
            pltpu.VMEM((N_FFT // 2, 128), BF),
            pltpu.VMEM((N_FFT // 2, 128), BF),
            pltpu.VMEM((384, 640), BF),
            pltpu.VMEM((32, 160, D), BF),
            pltpu.VMEM((32, 32, WIDE), BF),
            pltpu.VMEM((32, 8, D), BF),
            pltpu.VMEM((32, 8, D), BF),
            pltpu.VMEM((4, 32, 8, D), BF),
            pltpu.VMEM((1024, D), BF),
            pltpu.VMEM((1024, 3 * PART), BF),
            pltpu.VMEM((4, 256, PART), BF),
            pltpu.VMEM((4, 256, PART), BF),
            dma((17,)), dma((2,)),
            dma((46,)), dma((46,)), dma((46,)), dma((46,)),
            dma((64,)), dma((32,)), dma((12,)), dma((12,)), dma((16,)), dma((16,)), dma((4,)), dma((8,)), dma((4,)),
        ],
        compiler_params=pltpu.CompilerParams(
            vmem_limit_bytes=VMEM_LIMIT, collective_id=0, has_side_effects=True
        ),
        name="whole",
    )(*args)
    return regrouped.reshape(1, 32, 1, 8, D), attended.reshape(1, 32, 1, 8, D)


def solution(mesh):
    in_specs = (
        P(None, ("dp", "seq")), P(), P(), P(), P(), P(), P("dp", None), P("dp", None), P(None, "dp"),
    )
    out_specs = (P("dp", None, "seq", None, None), P("dp", None, "seq", None, None))
    return jax.shard_map(
        on_device, mesh=mesh, in_specs=in_specs, out_specs=out_specs, check_vma=False
    )
```
